32 devices in a mesh: groups: 2 (over y), hours: 4 (over z), years: 2 (over x), lines: 2 (over core).
Axes of the slice: x: 2, y: 2, z: 4, core: 2. Of those that a mesh axis runs over, the one named last changes fastest.
Arguments:
- demand: bfloat16 [8, 4, 2048], P(('groups', 'years'), 'hours'), parts along dimension 0, may hold values from 0.19921875 to 0.796875
- avail: bfloat16 [8, 4, 4096], P(('groups', 'years'), 'hours', 'lines'), parts along dimension 0, may hold values from 0.099609375 to 1
- ptdf: bfloat16 [1536, 2048], P('lines'), may hold values from -0.125 to 0.125
- line_limit: float32 [1536], P('lines'), may hold values from 0.3 to 3
- gen_cost: float32 [4096], P('lines'), may hold values from 0.2 to 5
- gen_cap: float32 [4096], P('lines'), may hold values from 0.3 to 1.5
- gen_node: int32 [4096], P('lines'), may hold values from 0 to 2047
- store_node: int32 [8192], P('lines'), may hold values from 0 to 2047
- store_power: float32 [8192], P('lines'), may hold values from 0.2 to 1
- capex: float32 [8192], P('lines'), may hold values from 0.05 to 1
- gen_state: float32 [8, 4, 4096], P(('groups', 'years'), 'hours', 'lines'), parts along dimension 0, may hold values from 0 to 0.6
- store_state: float32 [8, 4, 8192], P(('groups', 'years'), 'hours', 'lines'), parts along dimension 0, may hold values from -0.5 to 0.5
- level_upper: float32 [8, 4, 8192], P(('groups', 'years'), 'hours', 'lines'), parts along dimension 0, may hold values from 0 to 9, as said below
- level_lower: float32 [8, 4, 8192], P(('groups', 'years'), 'hours', 'lines'), parts along dimension 0, may hold values from 0 to 0.5
- flow_dual: float32 [8, 4, 1536], P(('groups', 'years'), 'hours', 'lines'), parts along dimension 0, may hold values from -3 to 3
- balance_dual: float32 [8, 4], P(('groups', 'years'), 'hours'), parts along dimension 0, may hold values from -6 to 6
- capacity: float32 [16384], P(('groups', 'lines')), parts along dimension 0, may hold values from 0.05 to 2
Outputs:
- gen_next: float32 [8, 4, 4096], P(('groups', 'years'), 'hours', 'lines'), parts along dimension 0
- store_next: float32 [8, 4, 8192], P(('groups', 'years'), 'hours', 'lines'), parts along dimension 0
- capacity_next: float32 [16384], P(('groups', 'lines')), parts along dimension 0
- balance_next: float32 [8, 4], P(('groups', 'years'), 'hours'), parts along dimension 0
- flow_next: float32 [8, 4, 1536], P(('groups', 'years'), 'hours', 'lines'), parts along dimension 0
- upper_next: float32 [8, 4, 8192], P(('groups', 'years'), 'hours', 'lines'), parts along dimension 0
- lower_next: float32 [8, 4, 8192], P(('groups', 'years'), 'hours', 'lines'), parts along dimension 0
The draws below stay inside these ranges and needn't reach their ends.
There are 2 independent parts, one for each index of `groups`. The reference program is written for one: setup_inputs(seed, part) draws one part's arguments, and reference() takes and returns one part's arrays. A program takes and returns all parts, laid end to end along the dimension named above; an argument that names none is the same for every part. Nothing has to cross between parts.
Inputs may be any that keep to these rules, and one draw needn't show every extreme that they name: `level_upper`: nonnegative.
All inputs are finite; a program needn't handle non-finite values.
Results may differ from the reference program's by a relative error of at most 0.004.
Values may be sent and summed in bfloat16 or wider, within the bound.
A program may use at most 64 MiB of HBM per device.

```python
import math
import jax
import jax.numpy as jnp
from jax import lax

NODES = 2048
LINES = 1536
STORAGES = 8192
GENS = 4096
ITERS = 1
YEARS = 4
HOURS = 4


def draw_level_upper(key, part):
    first, second, third = jax.random.split(jax.random.fold_in(key, 11), 3)
    uniform_part = jax.random.uniform(first, (YEARS, HOURS, STORAGES), jnp.float32)
    row_scale = jnp.exp(jax.random.uniform(second, (YEARS, HOURS, 1), jnp.float32, jnp.log(0.1), 0.0))
    rising = 1.0 + 2.0 * jnp.arange(HOURS, dtype=jnp.float32)[None, :, None] / (HOURS - 1)
    column_scale = jnp.exp(jax.random.uniform(third, (1, 1, STORAGES), jnp.float32, jnp.log(0.5), jnp.log(2.0)))
    return uniform_part * row_scale * rising * column_scale


def place_ends(result, own_key, low, largest):
    index_at = [jax.random.randint(jax.random.fold_in(own_key, axis), (), 0, length) for axis, length in enumerate(result.shape)]
    longest = result.shape.index(max(result.shape))
    neighbour = index_at[:longest] + [(index_at[longest] + 1) % result.shape[longest]] + index_at[longest + 1:]
    return result.at[tuple(index_at)].set(low).at[tuple(neighbour)].set(largest)


def levels(own_key, extent, cuts, low, largest):
    loudness, own = 1.0, jax.random.fold_in(own_key, 6)
    for position, blocks in cuts:
        heights = jnp.exp(jax.random.uniform(jax.random.fold_in(own, position), (blocks,), jnp.float32, low / len(cuts), largest / len(cuts)))
        loudness = loudness * jnp.repeat(heights, extent[position] // blocks).reshape([-1 if axis == position else 1 for axis in range(len(extent))])
    return loudness


def centred(stream_key, dims, spread, bound, shards=(), held_as=jnp.bfloat16):
    gain = levels(stream_key, dims, shards, -0.22, 0.18) if shards else 1.0
    entries = jax.random.normal(stream_key, dims, jnp.float32) * spread * gain
    return jnp.minimum(jnp.maximum(entries, -bound), bound).astype(held_as)


def setup_inputs(seed: int = 0, part: int = 0) -> dict:
    arg_keys = jax.random.split(jax.random.key(seed), 18)
    part_splits = jax.random.split(jax.random.fold_in(arg_keys[17], part), 18)
    return {
        "demand": jnp.clip(0.19921875 + 0.59765625 * jax.random.uniform(part_splits[0], (YEARS, HOURS, NODES), jnp.float32) ** levels(part_splits[0], (YEARS, HOURS, NODES), ((0, 2), (1, 4)), -0.2, 0.2), 0.19921875, 0.796875).astype(jnp.bfloat16),
        "avail": jnp.clip(0.099609375 + 0.9003906 * jax.random.uniform(part_splits[1], (YEARS, HOURS, GENS), jnp.float32) ** levels(part_splits[1], (YEARS, HOURS, GENS), ((0, 2), (1, 4), (2, 2)), -0.2, 0.2), 0.099609375, 1.0).astype(jnp.bfloat16),
        "ptdf": centred(arg_keys[2], (LINES, NODES), NODES ** -0.5, 0.125, ((0, 2),)),
        "line_limit": jnp.clip(jnp.exp(math.log(3.0) - 2.3025851 * jax.random.uniform(arg_keys[3], (LINES,), jnp.float32) ** levels(arg_keys[3], (LINES,), ((0, 2),), -0.2, 0.2)), 0.3, 3.0),
        "gen_cost": jnp.clip(jnp.exp(math.log(5.0) - 3.218876 * jax.random.uniform(arg_keys[4], (GENS,), jnp.float32) ** levels(arg_keys[4], (GENS,), ((0, 2),), -0.2, 0.2)), 0.2, 5.0),
        "gen_cap": jnp.clip(jnp.exp(math.log(1.5) - 1.60943787 * jax.random.uniform(arg_keys[5], (GENS,), jnp.float32) ** levels(arg_keys[5], (GENS,), ((0, 2),), -0.2, 0.2)), 0.3, 1.5),
        "gen_node": place_ends(jax.random.randint(arg_keys[6], (GENS,), 0, NODES), jax.random.fold_in(arg_keys[6], 1), 0, NODES - 1).astype(jnp.int32),
        "store_node": place_ends(jax.random.randint(arg_keys[7], (STORAGES,), 0, NODES), jax.random.fold_in(arg_keys[7], 1), 0, NODES - 1).astype(jnp.int32),
        "store_power": jnp.clip(jnp.exp(math.log(1.0) - 1.609438 * jax.random.uniform(arg_keys[8], (STORAGES,), jnp.float32) ** levels(arg_keys[8], (STORAGES,), ((0, 2),), -0.2, 0.2)), 0.2, 1.0),
        "capex": jnp.clip(jnp.exp(math.log(1.0) - 2.9957323 * jax.random.uniform(arg_keys[9], (STORAGES,), jnp.float32) ** levels(arg_keys[9], (STORAGES,), ((0, 2),), -0.2, 0.2)), 0.05, 1.0),
        "gen_state": jnp.clip(0.6 * jax.random.uniform(part_splits[10], (YEARS, HOURS, GENS), jnp.float32) ** levels(part_splits[10], (YEARS, HOURS, GENS), ((0, 2), (1, 4), (2, 2)), -0.2, 0.2), 0.0, 0.6),
        "store_state": jnp.clip(jax.random.uniform(part_splits[11], (YEARS, HOURS, STORAGES), jnp.float32, -0.5, 0.5) * levels(part_splits[11], (YEARS, HOURS, STORAGES), ((0, 2), (1, 4), (2, 2)), -0.4, 0.0), -0.5, 0.5),
        "level_upper": draw_level_upper(jax.random.fold_in(jax.random.fold_in(arg_keys[17], part), 71), part),
        "level_lower": jnp.clip(0.5 * jax.random.uniform(part_splits[13], (YEARS, HOURS, STORAGES), jnp.float32) ** levels(part_splits[13], (YEARS, HOURS, STORAGES), ((0, 2), (1, 4), (2, 2)), -0.2, 0.2), 0.0, 0.5),
        "flow_dual": centred(part_splits[14], (YEARS, HOURS, LINES), 0.5, 3.0, ((0, 2), (1, 4), (2, 2)), jnp.float32),
        "balance_dual": centred(part_splits[15], (YEARS, HOURS), 1.0, 6.0, ((0, 2), (1, 4)), jnp.float32),
        "capacity": jnp.clip(jnp.exp(math.log(2.0) - 3.6888794 * jax.random.uniform(part_splits[16], (STORAGES,), jnp.float32) ** levels(part_splits[16], (STORAGES,), ((0, 2),), -0.2, 0.2)), 0.05, 2.0),
    }


TAU = 0.1
SIGMA = 0.5
TAU_CAP = 1.0

def reference(demand, avail, ptdf, line_limit, gen_cost, gen_cap, gen_node, store_node, store_power, capex, gen_state, store_state, level_upper, level_lower, flow_dual, balance_dual, capacity):
    level_scale = 1.0 / math.sqrt(HOURS)
    node_scale = 1.0 / math.sqrt(NODES)
    hour_count = YEARS * HOURS
    demand_full = demand.astype(jnp.float32)
    gen_limit = gen_cap * avail.astype(jnp.float32)
    dispatch, storage, capacity_now = (gen_state, store_state, capacity)
    upper, lower, line_dual, balance = (level_upper, level_lower, flow_dual, balance_dual)
    for iteration in range(ITERS):
        dual_half = line_dual.astype(jnp.bfloat16).reshape(YEARS * HOURS, LINES)
        network = jnp.dot(dual_half, ptdf, preferred_element_type=jnp.float32).reshape(YEARS, HOURS, NODES)
        prices = node_scale * balance[:, :, None] + network
        dispatch_next = jnp.clip(dispatch - TAU * (gen_cost + prices[:, :, gen_node]), 0.0, gen_limit)
        suffix = level_scale * lax.cumsum(upper - lower, axis=1, reverse=True)
        storage_next = jnp.clip(storage - TAU * (suffix - prices[:, :, store_node]), -store_power, store_power)
        upper_total = lax.optimization_barrier(jnp.sum(upper, axis=(0, 1)))
        capacity_next = jnp.maximum(capacity_now - TAU_CAP * (capex - upper_total / hour_count), 0.0)
        dispatch_bar = 2.0 * dispatch_next - dispatch
        storage_bar = 2.0 * storage_next - storage
        capacity_bar = 2.0 * capacity_next - capacity_now
        empty = jnp.zeros((YEARS, HOURS, NODES), jnp.float32)
        inject = empty.at[:, :, gen_node].add(dispatch_bar).at[:, :, store_node].add(-storage_bar) - demand_full
        balance = balance + SIGMA * node_scale * lax.optimization_barrier(jnp.sum(inject, axis=2))
        inject_half = inject.astype(jnp.bfloat16).reshape(YEARS * HOURS, NODES)
        line_flows = jnp.dot(inject_half, ptdf.T, preferred_element_type=jnp.float32).reshape(YEARS, HOURS, LINES)
        shifted = line_dual + SIGMA * line_flows
        line_dual = shifted - SIGMA * jnp.clip(shifted / SIGMA, -line_limit, line_limit)
        level = level_scale * lax.cumsum(storage_bar, axis=1)
        upper = jnp.maximum(upper + SIGMA * (level - capacity_bar), 0.0)
        lower = jnp.maximum(lower - SIGMA * level, 0.0)
        dispatch, storage, capacity_now = (dispatch_next, storage_next, capacity_next)
    return (dispatch, storage, capacity_now, balance, line_dual, upper, lower)
```

```python
import functools
import math

import jax
import jax.numpy as jnp
from jax import lax
from jax.experimental import pallas as pl
from jax.experimental.pallas import tpu as pltpu
from jax.sharding import PartitionSpec as P

TAU = 0.1
SIGMA = 0.5
TAU_CAP = 1.0
LANES = 128
SPLITS = 2
LINK = jnp.bfloat16
MESH = pl.DeviceIdType.MESH


def step_kernel(
    sizes,
    demand_h, avail_h, ptdf_h, limit_h, cost_h, cap_h, gnode_h, snode_h, power_h,
    capex_h, gen_h, store_h, upper_h, lower_h, flow_h, capacity_h, balance_h,
    gen_w, store_w, capacity_w, flow_w, upper_w, lower_w, balance_o,
    demand_v, avail_v, ptdf_v, limit_v, cost_v, cap_v, gnode_v, snode_v, power_v,
    capex_v, gen_v, store_v, upper_v, lower_v, flow_v, capacity_v, balance_v,
    flow8, limit1, net_s, net_r, inj_s, inj_r, inj8, avail_d, demand_d,
    dual_s, dual_r, up_s, up_r, year_s, year_r, bar_s, bar_r, suffix_v, level_v,
    gbar_v, sbar_v, price_v, spread, onehot, highhot, placed_v, sent, loaded,
    in_sem, send_sem, recv_sem,
):
    years_dev, hours_dev, hours, years, level_scale, node_scale, hour_count = sizes
    rows = years_dev * hours_dev
    me_h, me_y, me_l = lax.axis_index("hours"), lax.axis_index("years"), lax.axis_index("lines")
    nodes = ptdf_v.shape[1]
    hi_count = nodes // LANES
    line_local = ptdf_v.shape[0]
    gen_rows, store_rows = gnode_v.shape[0], snode_v.shape[0]
    link = dual_s.dtype

    order = (
        (upper_h, upper_v, 0), (lower_h, lower_v, 0), (flow_h, flow_v, 1), (ptdf_h, ptdf_v, 1),
        (snode_h, snode_v, 2), (gnode_h, gnode_v, 2), (store_h, store_v, 2), (power_h, power_v, 2),
        (gen_h, gen_v, 2), (cost_h, cost_v, 2), (cap_h, cap_v, 2), (avail_h, avail_v, 2),
        (demand_h, demand_v, 2), (limit_h, limit_v, 2), (capex_h, capex_v, 2), (capacity_h, capacity_v, 2),
        (balance_h, balance_v, 2),
    )
    loads = [pltpu.make_async_copy(s, d, in_sem.at[i]) for s, d, i in order]
    for copy in loads:
        copy.start()

    def hour_peer(k):
        return {"hours": lax.rem(me_h + k, hours)}

    def year_peer(k):
        return {"years": lax.rem(me_y + k, years)}

    partner = {"lines": 1 - me_l}
    barrier = pltpu.get_barrier_semaphore()

    def ready(peer):
        pl.semaphore_signal(barrier, inc=1, device_id=peer, device_id_type=MESH)

    dual_r[...] = jnp.zeros_like(dual_r)
    bar_r[...] = jnp.zeros_like(bar_r)
    ready(partner)
    for k in range(1, years):
        ready(year_peer(k))
    for k in range(1, hours):
        @pl.when(me_h + k < hours)
        def _(k=k):
            ready(hour_peer(k))

    loads[0].wait()
    loads[1].wait()
    local_upper = None
    for y in range(years_dev):
        total = None
        for h in range(hours_dev):
            r = y * hours_dev + h
            diff = upper_v[r] - lower_v[r]
            total = diff if total is None else total + diff
            local_upper = upper_v[r] if local_upper is None else local_upper + upper_v[r]
        dual_s[y] = total.astype(link)
    year_s[...] = local_upper

    pl.semaphore_wait(barrier, years + me_h)

    def remote(src, dst, sem, peer):
        return pltpu.make_async_remote_copy(
            src_ref=src, dst_ref=dst, send_sem=send_sem, recv_sem=recv_sem.at[sem],
            device_id=peer, device_id_type=MESH,
        )

    def arrive(ref, sem):
        pltpu.make_async_copy(ref, ref, sem).wait()

    def dual_copy(k):
        return remote(dual_s, dual_r.at[k - 1], 2, hour_peer(hours - k))

    def bar_copy(k):
        return remote(bar_s, bar_r.at[k - 1], 3, hour_peer(k))

    def up_copy(k):
        return remote(up_s, up_r.at[k - 1], 4, hour_peer(k))

    year_copies = [remote(year_s, year_r.at[k - 1], 5, year_peer(k)) for k in range(1, years)]
    net_copy = remote(net_s, net_r, 0, partner)
    inj_copy = remote(inj_s, inj_r, 1, partner)

    for k in range(hours - 1, 0, -1):
        @pl.when(me_h >= k)
        def _(k=k):
            dual_copy(k).start()
    for copy in year_copies:
        copy.start()

    loads[2].wait()
    loads[3].wait()
    flow8[...] = jnp.zeros_like(flow8)
    for r in range(rows):
        flow8[r : r + 1, :] = flow_v[r]
    dual_half = flow8[...].astype(jnp.bfloat16)
    net = jnp.dot(dual_half, ptdf_v[...], preferred_element_type=jnp.float32)
    net_s[...] = net[:rows]
    net_copy.start()

    for copy in loads[4:]:
        copy.wait()
    high_rows = lax.broadcasted_iota(jnp.int32, (hi_count, LANES), 0)
    lane_rows = lax.broadcasted_iota(jnp.int32, (LANES, LANES), 0)

    def node_row(a):
        if a < store_rows:
            return snode_v[a : a + 1, :]
        return gnode_v[a - store_rows : a - store_rows + 1, :]

    for a in range(store_rows + gen_rows):
        low = jnp.broadcast_to(node_row(a) % LANES, (LANES, LANES))
        onehot[:, a * LANES : (a + 1) * LANES] = jnp.where(low == lane_rows, 1.0, 0.0).astype(jnp.bfloat16)
        high = jnp.broadcast_to(node_row(a) // LANES, (hi_count, LANES))
        highhot[:, a * LANES : (a + 1) * LANES] = jnp.where(high == high_rows, 1.0, 0.0).astype(jnp.bfloat16)

    for r in range(rows):
        for j in range(hi_count):
            piece = slice(j * LANES, (j + 1) * LANES)
            demand_d[r, j : j + 1, :] = demand_v[r : r + 1, piece].astype(jnp.float32)
        for j in range(gen_rows):
            piece = slice(j * LANES, (j + 1) * LANES)
            avail_d[r, j : j + 1, :] = avail_v[r : r + 1, piece].astype(jnp.float32)

    arrive(year_r, recv_sem.at[5])
    block_upper = year_s[...]
    for k in range(1, years):
        block_upper = block_upper + year_r[k - 1]
    up_s[...] = block_upper
    for k in range(1, hours):
        @pl.when(me_h + k >= hours)
        def _(k=k):
            up_copy(k).start()

    net_copy.wait_recv()
    prices = net_s[...] + net_r[...]

    def gather(r, node):
        price_row = prices[r : r + 1] + node_scale * balance_v[:, r : r + 1]
        high, low = node // LANES, node % LANES
        result = jnp.zeros(node.shape, jnp.float32)
        for j in range(hi_count):
            table = jnp.broadcast_to(price_row[:, j * LANES : (j + 1) * LANES], node.shape)
            picked = jnp.take_along_axis(table, low, axis=1, mode="promise_in_bounds")
            result = jnp.where(high == j, picked, result)
        return result

    for r in range(rows):
        for b in range(0, store_rows, 8):
            price_v[r, b : b + 8] = gather(r, snode_v[b : b + 8])

    for r in range(rows):
        for b in range(0, gen_rows, 8):
            part = slice(b, b + 8)
            price = gather(r, gnode_v[part])
            new = gen_v[r, part] - TAU * (cost_v[part] + price)
            new = jnp.minimum(jnp.maximum(new, 0.0), cap_v[part] * avail_d[r, part])
            gen_w[r, part] = new
            gbar_v[r, part] = 2.0 * new - gen_v[r, part]

    def place(values, sign, first, count):
        for r in range(rows):
            rest = sign * values[r]
            for p in range(SPLITS):
                piece = rest.astype(jnp.bfloat16).astype(jnp.float32)
                rest = rest - piece
                base = (r * SPLITS + p) * hi_count
                for a in range(count):
                    cols = slice((first + a) * LANES, (first + a + 1) * LANES)
                    wide = jnp.broadcast_to(piece[a : a + 1], (hi_count, LANES)).astype(jnp.bfloat16)
                    spread[base : base + hi_count, cols] = wide * highhot[:, cols]
        cols = slice(first * LANES, (first + count) * LANES)
        return lax.dot_general(
            spread[:, cols], onehot[:, cols], (((1,), (1,)), ((), ())), preferred_element_type=jnp.float32
        )

    placed_v[...] = place(gbar_v, 1.0, store_rows, gen_rows)

    for count in range(1, hours):
        @pl.when(me_h + count == hours - 1)
        def _(count=count):
            arrive(dual_r.at[pl.ds(0, count)], recv_sem.at[2])
    for y in range(years_dev):
        beyond = jnp.zeros_like(suffix_v[y])
        for k in range(1, hours):
            beyond = beyond + dual_r[k - 1, y].astype(jnp.float32)
        bar_total = jnp.zeros_like(beyond)
        for h in reversed(range(hours_dev)):
            r = y * hours_dev + h
            beyond = beyond + (upper_v[r] - lower_v[r])
            suffix = level_scale * beyond
            power = power_v[...]
            new = store_v[r] - TAU * (suffix - price_v[r])
            new = jnp.minimum(jnp.maximum(new, -power), power)
            store_w[r] = new
            sbar = 2.0 * new - store_v[r]
            sbar_v[r] = sbar
            bar_total = bar_total + sbar
        bar_s[y] = bar_total.astype(link)
    for k in range(hours - 1, 0, -1):
        @pl.when(me_h + k < hours)
        def _(k=k):
            bar_copy(k).start()
            up_copy(k).start()
    placed = placed_v[...] + place(sbar_v, -1.0, 0, store_rows)
    for r in range(rows):
        total = None
        for p in range(SPLITS):
            base = (r * SPLITS + p) * hi_count
            piece = placed[base : base + hi_count]
            total = piece if total is None else total + piece
        inj_s[r] = total
    inj_copy.start()

    for c in range(line_local // LANES):
        limit1[:, c * LANES : (c + 1) * LANES] = limit_v[c : c + 1, :]
    inj8[...] = jnp.zeros_like(inj8)

    inj_copy.wait_recv()
    for r in range(rows):
        inject = inj_s[r] + inj_r[r] - demand_d[r]
        balance_o[:, r : r + 1] = balance_v[:, r : r + 1] + SIGMA * node_scale * jnp.sum(inject, keepdims=True)
        for j in range(hi_count):
            inj8[r : r + 1, j * LANES : (j + 1) * LANES] = inject[j : j + 1]
    line_flows = lax.dot_general(
        inj8[...].astype(jnp.bfloat16), ptdf_v[...], (((1,), (1,)), ((), ())),
        preferred_element_type=jnp.float32,
    )
    shifted = flow8[...] + SIGMA * line_flows
    limit = limit1[...]
    line_next = shifted - SIGMA * jnp.minimum(jnp.maximum(shifted / SIGMA, -limit), limit)
    for r in range(rows):
        flow_w[r] = line_next[r : r + 1]

    arrive(up_r, recv_sem.at[4])
    upper_total = up_s[...]
    for k in range(1, hours):
        upper_total = upper_total + up_r[k - 1]
    capacity_next = jnp.maximum(capacity_v[...] - TAU_CAP * (capex_v[...] - upper_total / hour_count), 0.0)
    capacity_w[...] = capacity_next
    capacity_bar = 2.0 * capacity_next - capacity_v[...]

    for count in range(1, hours):
        @pl.when(me_h == count)
        def _(count=count):
            arrive(bar_r.at[pl.ds(0, count)], recv_sem.at[3])
    for y in range(years_dev):
        before = jnp.zeros_like(level_v[y])
        for k in range(1, hours):
            before = before + bar_r[k - 1, y].astype(jnp.float32)
        for h in range(hours_dev):
            r = y * hours_dev + h
            before = before + sbar_v[r]
            level = level_scale * before
            upper_w[r] = jnp.maximum(upper_v[r] + SIGMA * (level - capacity_bar), 0.0)
            lower_w[r] = jnp.maximum(lower_v[r] - SIGMA * level, 0.0)

    arrive(sent, send_sem)


def finish_kernel(count, *refs):
    sources, targets, sem = refs[:count], refs[count : 2 * count], refs[2 * count]
    copies = [pltpu.make_async_copy(s, t, sem) for s, t in zip(sources, targets)]
    for copy in copies:
        copy.start()
    for copy in copies:
        copy.wait()


def local(
    demand, avail, ptdf, line_limit, gen_cost, gen_cap, gen_node, store_node, store_power,
    capex, gen_state, store_state, level_upper, level_lower, flow_dual, balance_dual, capacity,
):
    years_dev, hours_dev, nodes = demand.shape
    rows = years_dev * hours_dev
    hours, years = lax.axis_size("hours"), lax.axis_size("years")
    hours_total = hours_dev * hours
    hour_count = years_dev * years * hours_total
    level_scale = 1.0 / math.sqrt(hours_total)
    node_scale = 1.0 / math.sqrt(nodes)
    sizes = (years_dev, hours_dev, hours, years, level_scale, node_scale, hour_count)

    def fold(x):
        return x.reshape(-1, LANES)

    def fold_rows(x):
        return x.reshape(rows, -1, LANES)

    args = (
        demand.reshape(rows, nodes), avail.reshape(rows, -1), ptdf, fold(line_limit), fold(gen_cost),
        fold(gen_cap), fold(gen_node), fold(store_node), fold(store_power), fold(capex),
        fold_rows(gen_state), fold_rows(store_state), fold_rows(level_upper), fold_rows(level_lower),
        flow_dual.reshape(rows, 1, -1), fold(capacity), balance_dual.reshape(1, rows),
    )
    f32 = jnp.float32
    gen_rows, store_rows = args[6].shape[0], args[7].shape[0]
    line_local, hi_count = ptdf.shape[0], nodes // LANES
    padded = max(8, -(-rows // 8) * 8)
    out_shapes = [
        (rows, gen_rows, LANES), (rows, store_rows, LANES), (store_rows, LANES),
        (rows, 1, line_local), (rows, store_rows, LANES), (rows, store_rows, LANES),
    ]
    any_spec = pl.BlockSpec(memory_space=pl.ANY)
    block, blocks = (store_rows, LANES), (years_dev, store_rows, LANES)
    h1, y1 = max(hours - 1, 1), max(years - 1, 1)
    dma = pltpu.SemaphoreType.DMA
    block_size = store_rows * LANES * 4
    sent_bytes = 8 * rows * nodes + (hours + years - 2) * block_size
    sent_bytes += (hours - 1) * years_dev * store_rows * LANES * jnp.dtype(LINK).itemsize
    sent_rows = sent_bytes // (4 * LANES)
    scratch = [pltpu.VMEM(a.shape, a.dtype) for a in args]
    scratch += [
        pltpu.VMEM((padded, line_local), f32), pltpu.VMEM((1, line_local), f32),
        pltpu.VMEM((rows, nodes), f32), pltpu.VMEM((rows, nodes), f32),
        pltpu.VMEM((rows, hi_count, LANES), f32), pltpu.VMEM((rows, hi_count, LANES), f32),
        pltpu.VMEM((padded, nodes), f32), pltpu.VMEM((rows, gen_rows, LANES), f32),
        pltpu.VMEM((rows, hi_count, LANES), f32),
        pltpu.VMEM(blocks, LINK), pltpu.VMEM((h1,) + blocks, LINK),
        pltpu.VMEM(block, f32), pltpu.VMEM((h1,) + block, f32),
        pltpu.VMEM(block, f32), pltpu.VMEM((y1,) + block, f32),
        pltpu.VMEM(blocks, LINK), pltpu.VMEM((h1,) + blocks, LINK),
        pltpu.VMEM(blocks, f32), pltpu.VMEM(blocks, f32),
        pltpu.VMEM((rows, gen_rows, LANES), f32), pltpu.VMEM((rows, store_rows, LANES), f32),
        pltpu.VMEM((rows, store_rows, LANES), f32),
        pltpu.VMEM((rows * SPLITS * hi_count, (gen_rows + store_rows) * LANES), jnp.bfloat16),
        pltpu.VMEM((LANES, (gen_rows + store_rows) * LANES), jnp.bfloat16),
        pltpu.VMEM((hi_count, (gen_rows + store_rows) * LANES), jnp.bfloat16),
        pltpu.VMEM((rows * SPLITS * hi_count, LANES), f32),
        pltpu.VMEM((sent_rows, LANES), f32), pltpu.VMEM((8, LANES), f32),
        dma((3,)), dma, dma((6,)),
    ]
    results = pl.pallas_call(
        functools.partial(step_kernel, sizes),
        out_shape=[pltpu.VMEM(s, f32) for s in out_shapes] + [pltpu.VMEM((1, rows), f32)],
        in_specs=[any_spec] * 17,
        out_specs=[pl.BlockSpec(memory_space=pltpu.VMEM)] * 7,
        scratch_shapes=scratch,
        compiler_params=pltpu.CompilerParams(
            collective_id=0, has_side_effects=True, vmem_limit_bytes=56 * 1024 * 1024
        ),
    )(*args)
    gen, store, cap, flow, upper, lower, balance = pl.pallas_call(
        functools.partial(finish_kernel, len(results)),
        out_shape=[jax.ShapeDtypeStruct(x.shape, f32) for x in results],
        in_specs=[pl.BlockSpec(memory_space=pltpu.VMEM)] * len(results),
        out_specs=[any_spec] * len(results),
        scratch_shapes=[dma],
    )(*[pltpu.with_memory_space_constraint(x, pltpu.VMEM) for x in results])
    return (
        gen.reshape(gen_state.shape), store.reshape(store_state.shape), cap.reshape(capacity.shape),
        balance.reshape(balance_dual.shape), flow.reshape(flow_dual.shape),
        upper.reshape(level_upper.shape), lower.reshape(level_lower.shape),
    )


def solution(mesh):
    row = P(("groups", "years"), "hours", "lines")
    line = P("lines")
    in_specs = (
        P(("groups", "years"), "hours", None), row, P("lines", None), line, line, line, line, line,
        line, line, row, row, row, row, row, P(("groups", "years"), "hours"), P(("groups", "lines")),
    )
    out_specs = (row, row, P(("groups", "lines")), P(("groups", "years"), "hours"), row, row, row)
    return jax.shard_map(local, mesh=mesh, in_specs=in_specs, out_specs=out_specs, check_vma=False)
```

```python
import functools
import math

import jax
import jax.numpy as jnp
from jax import lax
from jax.experimental import pallas as pl
from jax.experimental.pallas import tpu as pltpu
from jax.sharding import PartitionSpec as P

TAU = 0.1
SIGMA = 0.5
TAU_CAP = 1.0
LANES = 128
SPLITS = 2
LINK = jnp.bfloat16
MESH = pl.DeviceIdType.MESH


def step_kernel(
    sizes,
    demand_h, avail_h, ptdf_h, limit_h, cost_h, cap_h, gnode_h, snode_h, power_h,
    capex_h, gen_h, store_h, upper_h, lower_h, flow_h, capacity_h, balance_h,
    gen_w, store_w, capacity_w, flow_w, upper_w, lower_w, balance_o,
    demand_v, avail_v, ptdf_v, limit_v, cost_v, cap_v, gnode_v, snode_v, power_v,
    capex_v, gen_v, store_v, upper_v, lower_v, flow_v, capacity_v, balance_v,
    flow8, limit1, net_s, net_r, inj_s, inj_r, inj8, avail_d, demand_d,
    dual_s, dual_r, total_v, cross_r, above_s, above_r, bar_s, bar_r,
    gbar_v, sbar_v, price_v, spread, onehot, highhot, placed_v, sent,
    in_sem, send_sem, recv_sem, year_ready,
):
    years_dev, hours_dev, hours, years, level_scale, node_scale, hour_count = sizes
    rows = years_dev * hours_dev
    me_h, me_y, me_l = lax.axis_index("hours"), lax.axis_index("years"), lax.axis_index("lines")
    nodes = ptdf_v.shape[1]
    hi_count = nodes // LANES
    line_local = ptdf_v.shape[0]
    gen_rows, store_rows = gnode_v.shape[0], snode_v.shape[0]
    link = dual_s.dtype
    block_rows = store_rows * link.itemsize // 4
    base_rows = 2 * rows * hi_count + ((hours - 1) * (years_dev + 1) + years - 1) * block_rows

    order = (
        (upper_h, upper_v, 0), (lower_h, lower_v, 0), (flow_h, flow_v, 1), (ptdf_h, ptdf_v, 1),
        (snode_h, snode_v, 2), (gnode_h, gnode_v, 2), (store_h, store_v, 2), (power_h, power_v, 2),
        (gen_h, gen_v, 2), (cost_h, cost_v, 2), (cap_h, cap_v, 2), (avail_h, avail_v, 2),
        (demand_h, demand_v, 2), (limit_h, limit_v, 2), (capex_h, capex_v, 2), (capacity_h, capacity_v, 2),
        (balance_h, balance_v, 2),
    )
    loads = [pltpu.make_async_copy(s, d, in_sem.at[i]) for s, d, i in order]
    for copy in loads:
        copy.start()

    def peer(k, j):
        return {"hours": lax.rem(me_h + k, hours), "years": lax.rem(me_y + j, years)}

    partner = {"lines": 1 - me_l}
    barrier = pltpu.get_barrier_semaphore()

    def ready(device):
        pl.semaphore_signal(barrier, inc=1, device_id=device, device_id_type=MESH)

    dual_r[...] = jnp.zeros_like(dual_r)
    bar_r[...] = jnp.zeros_like(bar_r)
    cross_r[...] = jnp.zeros_like(cross_r)
    above_r[...] = jnp.zeros_like(above_r)
    ready(partner)
    for k in range(1, hours):
        @pl.when(me_h + k < hours)
        def _(k=k):
            ready(peer(k, 0))
    for j in range(1, years):
        @pl.when(me_y + j < years)
        def _(j=j):
            ready(peer(0, j))
            for k in range(1, hours):
                @pl.when(me_h + k < hours)
                def _(k=k):
                    ready(peer(k, j))

    pl.semaphore_wait(barrier, 1 + me_y + me_h * (1 + me_y))
    for j in range(1, years):
        @pl.when(me_y + j >= years)
        def _(j=j):
            pl.semaphore_signal(year_ready, inc=1, device_id=peer(0, j), device_id_type=MESH)

    loads[0].wait()
    loads[1].wait()
    local_upper = None
    for y in range(years_dev):
        total = None
        for h in range(hours_dev):
            r = y * hours_dev + h
            diff = upper_v[r] - lower_v[r]
            total = diff if total is None else total + diff
            local_upper = upper_v[r] if local_upper is None else local_upper + upper_v[r]
        dual_s[y] = total.astype(link)
    dual_s[years_dev] = local_upper.astype(link)
    total_v[...] = local_upper

    def remote(src, dst, sem, device):
        return pltpu.make_async_remote_copy(
            src_ref=src, dst_ref=dst, send_sem=send_sem, recv_sem=recv_sem.at[sem],
            device_id=device, device_id_type=MESH,
        )

    def arrive(ref, sem):
        pltpu.make_async_copy(ref, ref, sem).wait()

    def dual_copy(k):
        return remote(dual_s, dual_r.at[k - 1], 2, peer(hours - k, 0))

    def bar_copy(k):
        return remote(bar_s, bar_r.at[k - 1], 3, peer(k, 0))

    def cross_copy(k, j):
        slot = cross_r.at[k, j - 1]
        return remote(dual_s.at[years_dev], slot, 4 if k else 5, peer(hours - k, years - j))

    def above_copy(j):
        return remote(above_s, above_r.at[j - 1], 6, peer(0, j))

    net_copy = remote(net_s, net_r, 0, partner)
    inj_copy = remote(inj_s, inj_r, 1, partner)

    for k in range(hours - 1, 0, -1):
        @pl.when(me_h >= k)
        def _(k=k):
            dual_copy(k).start()
    for j in range(1, years):
        @pl.when(me_y >= j)
        def _(j=j):
            cross_copy(0, j).start()
    for j in range(1, years):
        for k in range(hours - 1, 0, -1):
            @pl.when(jnp.logical_and(me_h >= k, me_y >= j))
            def _(k=k, j=j):
                cross_copy(k, j).start()

    loads[2].wait()
    loads[3].wait()
    flow8[...] = jnp.zeros_like(flow8)
    for r in range(rows):
        flow8[r : r + 1, :] = flow_v[r]
    dual_half = flow8[...].astype(jnp.bfloat16)
    net = jnp.dot(dual_half, ptdf_v[...], preferred_element_type=jnp.float32)
    net_s[...] = net[:rows]
    net_copy.start()

    @pl.when(me_y < years - 1)
    def _():
        pl.semaphore_wait(year_ready, years - 1 - me_y)

    for j in range(1, years):
        @pl.when(me_y + j < years)
        def _(j=j):
            cross_copy(0, years - j).start()

    for copy in loads[4:]:
        copy.wait()
    high_rows = lax.broadcasted_iota(jnp.int32, (hi_count, LANES), 0)
    lane_rows = lax.broadcasted_iota(jnp.int32, (LANES, LANES), 0)

    def node_row(a):
        if a < store_rows:
            return snode_v[a : a + 1, :]
        return gnode_v[a - store_rows : a - store_rows + 1, :]

    for a in range(store_rows + gen_rows):
        low = jnp.broadcast_to(node_row(a) % LANES, (LANES, LANES))
        onehot[:, a * LANES : (a + 1) * LANES] = jnp.where(low == lane_rows, 1.0, 0.0).astype(jnp.bfloat16)
        high = jnp.broadcast_to(node_row(a) // LANES, (hi_count, LANES))
        highhot[:, a * LANES : (a + 1) * LANES] = jnp.where(high == high_rows, 1.0, 0.0).astype(jnp.bfloat16)

    for r in range(rows):
        for j in range(hi_count):
            piece = slice(j * LANES, (j + 1) * LANES)
            demand_d[r, j : j + 1, :] = demand_v[r : r + 1, piece].astype(jnp.float32)
        for j in range(gen_rows):
            piece = slice(j * LANES, (j + 1) * LANES)
            avail_d[r, j : j + 1, :] = avail_v[r : r + 1, piece].astype(jnp.float32)

    net_copy.wait_recv()
    prices = net_s[...] + net_r[...]

    def gather(r, node):
        price_row = prices[r : r + 1] + node_scale * balance_v[:, r : r + 1]
        high, low = node // LANES, node % LANES
        result = jnp.zeros(node.shape, jnp.float32)
        for j in range(hi_count):
            table = jnp.broadcast_to(price_row[:, j * LANES : (j + 1) * LANES], node.shape)
            picked = jnp.take_along_axis(table, low, axis=1, mode="promise_in_bounds")
            result = jnp.where(high == j, picked, result)
        return result

    for r in range(rows):
        for b in range(0, store_rows, 8):
            price_v[r, b : b + 8] = gather(r, snode_v[b : b + 8])

    for r in range(rows):
        for b in range(0, gen_rows, 8):
            part = slice(b, b + 8)
            price = gather(r, gnode_v[part])
            new = gen_v[r, part] - TAU * (cost_v[part] + price)
            new = jnp.minimum(jnp.maximum(new, 0.0), cap_v[part] * avail_d[r, part])
            gen_w[r, part] = new
            gbar_v[r, part] = 2.0 * new - gen_v[r, part]

    def place(values, sign, first, count):
        for r in range(rows):
            rest = sign * values[r]
            for p in range(SPLITS):
                piece = rest.astype(jnp.bfloat16).astype(jnp.float32)
                rest = rest - piece
                base = (r * SPLITS + p) * hi_count
                for a in range(count):
                    cols = slice((first + a) * LANES, (first + a + 1) * LANES)
                    wide = jnp.broadcast_to(piece[a : a + 1], (hi_count, LANES)).astype(jnp.bfloat16)
                    spread[base : base + hi_count, cols] = wide * highhot[:, cols]
        cols = slice(first * LANES, (first + count) * LANES)
        return lax.dot_general(
            spread[:, cols], onehot[:, cols], (((1,), (1,)), ((), ())), preferred_element_type=jnp.float32
        )

    placed_v[...] = place(gbar_v, 1.0, store_rows, gen_rows)

    arrive(cross_r.at[0], recv_sem.at[5])
    hour_upper = total_v[...]
    for j in range(1, years):
        hour_upper = hour_upper + cross_r[0, j - 1].astype(jnp.float32)
    total_v[...] = hour_upper
    bar_s[years_dev] = hour_upper.astype(link)

    for count in range(1, hours):
        @pl.when(me_h + count == hours - 1)
        def _(count=count):
            arrive(dual_r.at[pl.ds(0, count)], recv_sem.at[2])
    above = dual_r[0, years_dev].astype(jnp.float32)
    for k in range(2, hours):
        above = above + dual_r[k - 1, years_dev].astype(jnp.float32)
    above_s[...] = above.astype(link)
    for y in range(years_dev):
        beyond = dual_r[0, y].astype(jnp.float32)
        for k in range(2, hours):
            beyond = beyond + dual_r[k - 1, y].astype(jnp.float32)
        bar_total = None
        for h in reversed(range(hours_dev)):
            r = y * hours_dev + h
            beyond = beyond + (upper_v[r] - lower_v[r])
            suffix = level_scale * beyond
            power = power_v[...]
            new = store_v[r] - TAU * (suffix - price_v[r])
            new = jnp.minimum(jnp.maximum(new, -power), power)
            store_w[r] = new
            sbar = 2.0 * new - store_v[r]
            sbar_v[r] = sbar
            bar_total = sbar if bar_total is None else bar_total + sbar
        bar_s[y] = bar_total.astype(link)
    for k in range(hours - 1, 0, -1):
        @pl.when(me_h + k < hours)
        def _(k=k):
            bar_copy(k).start()
    for j in range(1, years):
        @pl.when(jnp.logical_and(me_h < hours - 1, me_y + j < years))
        def _(j=j):
            above_copy(j).start()
    total_v[...] = total_v[...] + above
    placed = placed_v[...] + place(sbar_v, -1.0, 0, store_rows)
    for r in range(rows):
        total = None
        for p in range(SPLITS):
            base = (r * SPLITS + p) * hi_count
            piece = placed[base : base + hi_count]
            total = piece if total is None else total + piece
        inj_s[r] = total
    inj_copy.start()

    for c in range(line_local // LANES):
        limit1[:, c * LANES : (c + 1) * LANES] = limit_v[c : c + 1, :]
    inj8[...] = jnp.zeros_like(inj8)

    inj_copy.wait_recv()
    for r in range(rows):
        inject = inj_s[r] + inj_r[r] - demand_d[r]
        balance_o[:, r : r + 1] = balance_v[:, r : r + 1] + SIGMA * node_scale * jnp.sum(inject, keepdims=True)
        for j in range(hi_count):
            inj8[r : r + 1, j * LANES : (j + 1) * LANES] = inject[j : j + 1]
    line_flows = lax.dot_general(
        inj8[...].astype(jnp.bfloat16), ptdf_v[...], (((1,), (1,)), ((), ())),
        preferred_element_type=jnp.float32,
    )
    shifted = flow8[...] + SIGMA * line_flows
    limit = limit1[...]
    line_next = shifted - SIGMA * jnp.minimum(jnp.maximum(shifted * (1.0 / SIGMA), -limit), limit)
    for r in range(rows):
        flow_w[r] = line_next[r : r + 1]

    for j in range(1, years):
        for k in range(1, hours):
            @pl.when(jnp.logical_and(me_h + k == hours - 1, me_y + j == years - 1))
            def _(k=k, j=j):
                arrive(cross_r.at[pl.ds(1, k), pl.ds(0, j)], recv_sem.at[4])

        @pl.when(jnp.logical_and(me_h < hours - 1, me_y == j))
        def _(j=j):
            arrive(above_r.at[pl.ds(0, j)], recv_sem.at[6])
    for count in range(1, hours):
        @pl.when(me_h == count)
        def _(count=count):
            arrive(bar_r.at[pl.ds(0, count)], recv_sem.at[3])
    upper_total = total_v[...]
    for k in range(1, hours):
        upper_total = upper_total + bar_r[k - 1, years_dev].astype(jnp.float32)
        for j in range(1, years):
            upper_total = upper_total + cross_r[k, j - 1].astype(jnp.float32)
    for j in range(1, years):
        upper_total = upper_total + above_r[j - 1].astype(jnp.float32)
    capacity_next = jnp.maximum(capacity_v[...] - TAU_CAP * (capex_v[...] - upper_total / hour_count), 0.0)
    capacity_w[...] = capacity_next
    capacity_bar = 2.0 * capacity_next - capacity_v[...]

    for y in range(years_dev):
        before = bar_r[0, y].astype(jnp.float32)
        for k in range(2, hours):
            before = before + bar_r[k - 1, y].astype(jnp.float32)
        for h in range(hours_dev):
            r = y * hours_dev + h
            before = before + sbar_v[r]
            level = level_scale * before
            upper_w[r] = jnp.maximum(upper_v[r] + SIGMA * (level - capacity_bar), 0.0)
            lower_w[r] = jnp.maximum(lower_v[r] - SIGMA * level, 0.0)

    for y in range(years):
        for h in range(hours):
            blocks = h * y + (years - 1 - y if h < hours - 1 else 0)

            @pl.when(jnp.logical_and(me_h == h, me_y == y))
            def _(blocks=blocks):
                arrive(sent.at[pl.ds(0, base_rows + blocks * block_rows)], send_sem)


def finish_kernel(count, *refs):
    sources, targets, sem = refs[:count], refs[count : 2 * count], refs[2 * count]
    copies = [pltpu.make_async_copy(s, t, sem) for s, t in zip(sources, targets)]
    for copy in copies:
        copy.start()
    for copy in copies:
        copy.wait()


def local(
    demand, avail, ptdf, line_limit, gen_cost, gen_cap, gen_node, store_node, store_power,
    capex, gen_state, store_state, level_upper, level_lower, flow_dual, balance_dual, capacity,
):
    years_dev, hours_dev, nodes = demand.shape
    rows = years_dev * hours_dev
    hours, years = lax.axis_size("hours"), lax.axis_size("years")
    hours_total = hours_dev * hours
    hour_count = years_dev * years * hours_total
    level_scale = 1.0 / math.sqrt(hours_total)
    node_scale = 1.0 / math.sqrt(nodes)
    sizes = (years_dev, hours_dev, hours, years, level_scale, node_scale, hour_count)

    def fold(x):
        return x.reshape(-1, LANES)

    def fold_rows(x):
        return x.reshape(rows, -1, LANES)

    args = (
        demand.reshape(rows, nodes), avail.reshape(rows, -1), ptdf, fold(line_limit), fold(gen_cost),
        fold(gen_cap), fold(gen_node), fold(store_node), fold(store_power), fold(capex),
        fold_rows(gen_state), fold_rows(store_state), fold_rows(level_upper), fold_rows(level_lower),
        flow_dual.reshape(rows, 1, -1), fold(capacity), balance_dual.reshape(1, rows),
    )
    f32 = jnp.float32
    gen_rows, store_rows = args[6].shape[0], args[7].shape[0]
    line_local, hi_count = ptdf.shape[0], nodes // LANES
    padded = max(8, -(-rows // 8) * 8)
    out_shapes = [
        (rows, gen_rows, LANES), (rows, store_rows, LANES), (store_rows, LANES),
        (rows, 1, line_local), (rows, store_rows, LANES), (rows, store_rows, LANES),
    ]
    any_spec = pl.BlockSpec(memory_space=pl.ANY)
    block, blocks = (store_rows, LANES), (years_dev + 1, store_rows, LANES)
    h1, y1 = max(hours - 1, 1), max(years - 1, 1)
    dma = pltpu.SemaphoreType.DMA
    block_rows = store_rows * jnp.dtype(LINK).itemsize // 4
    sent_rows = 2 * rows * hi_count + (hours - 1) * (years_dev + 1) * block_rows + (hours + 1) * years * block_rows
    scratch = [pltpu.VMEM(a.shape, a.dtype) for a in args]
    scratch += [
        pltpu.VMEM((padded, line_local), f32), pltpu.VMEM((1, line_local), f32),
        pltpu.VMEM((rows, nodes), f32), pltpu.VMEM((rows, nodes), f32),
        pltpu.VMEM((rows, hi_count, LANES), f32), pltpu.VMEM((rows, hi_count, LANES), f32),
        pltpu.VMEM((padded, nodes), f32), pltpu.VMEM((rows, gen_rows, LANES), f32),
        pltpu.VMEM((rows, hi_count, LANES), f32),
        pltpu.VMEM(blocks, LINK), pltpu.VMEM((h1,) + blocks, LINK),
        pltpu.VMEM(block, f32), pltpu.VMEM((hours, y1) + block, LINK),
        pltpu.VMEM(block, LINK), pltpu.VMEM((y1,) + block, LINK),
        pltpu.VMEM(blocks, LINK), pltpu.VMEM((h1,) + blocks, LINK),
        pltpu.VMEM((rows, gen_rows, LANES), f32), pltpu.VMEM((rows, store_rows, LANES), f32),
        pltpu.VMEM((rows, store_rows, LANES), f32),
        pltpu.VMEM((rows * SPLITS * hi_count, (gen_rows + store_rows) * LANES), jnp.bfloat16),
        pltpu.VMEM((LANES, (gen_rows + store_rows) * LANES), jnp.bfloat16),
        pltpu.VMEM((hi_count, (gen_rows + store_rows) * LANES), jnp.bfloat16),
        pltpu.VMEM((rows * SPLITS * hi_count, LANES), f32),
        pltpu.VMEM((sent_rows, LANES), f32),
        dma((3,)), dma, dma((7,)), pltpu.SemaphoreType.REGULAR,
    ]
    results = pl.pallas_call(
        functools.partial(step_kernel, sizes),
        out_shape=[pltpu.VMEM(s, f32) for s in out_shapes] + [pltpu.VMEM((1, rows), f32)],
        in_specs=[any_spec] * 17,
        out_specs=[pl.BlockSpec(memory_space=pltpu.VMEM)] * 7,
        scratch_shapes=scratch,
        compiler_params=pltpu.CompilerParams(
            collective_id=0, has_side_effects=True, vmem_limit_bytes=56 * 1024 * 1024
        ),
    )(*args)
    gen, store, cap, flow, upper, lower, balance = pl.pallas_call(
        functools.partial(finish_kernel, len(results)),
        out_shape=[jax.ShapeDtypeStruct(x.shape, f32) for x in results],
        in_specs=[pl.BlockSpec(memory_space=pltpu.VMEM)] * len(results),
        out_specs=[any_spec] * len(results),
        scratch_shapes=[dma],
    )(*[pltpu.with_memory_space_constraint(x, pltpu.VMEM) for x in results])
    return (
        gen.reshape(gen_state.shape), store.reshape(store_state.shape), cap.reshape(capacity.shape),
        balance.reshape(balance_dual.shape), flow.reshape(flow_dual.shape),
        upper.reshape(level_upper.shape), lower.reshape(level_lower.shape),
    )


def solution(mesh):
    row = P(("groups", "years"), "hours", "lines")
    line = P("lines")
    in_specs = (
        P(("groups", "years"), "hours", None), row, P("lines", None), line, line, line, line, line,
        line, line, row, row, row, row, row, P(("groups", "years"), "hours"), P(("groups", "lines")),
    )
    out_specs = (row, row, P(("groups", "lines")), P(("groups", "years"), "hours"), row, row, row)
    return jax.shard_map(local, mesh=mesh, in_specs=in_specs, out_specs=out_specs, check_vma=False)
```

```python
import functools
import math

import jax
import jax.numpy as jnp
from jax import lax
from jax.experimental import pallas as pl
from jax.experimental.pallas import tpu as pltpu
from jax.sharding import PartitionSpec as P

TAU = 0.1
SIGMA = 0.5
TAU_CAP = 1.0
LANES = 128
SPLITS = 2
TILE = 256
THIN = 4
LINK = jnp.bfloat16
MESH = pl.DeviceIdType.MESH


def step_kernel(
    sizes,
    demand_h, avail_h, ptdf_h, limit_h, cost_h, cap_h, gnode_h, snode_h, power_h,
    capex_h, gen_h, store_h, upper_h, lower_h, flow_h, capacity_h, balance_h,
    gen_w, store_w, capacity_w, flow_w, upper_w, lower_w, balance_o,
    demand_v, avail_v, ptdf_v, limit_v, cost_v, cap_v, gnode_v, snode_v, power_v,
    capex_v, gen_v, store_v, upper_v, lower_v, flow_v, capacity_v, balance_v,
    flow8, limit1, net_s, net_r, inj_s, inj_r, inj8, line8, avail_d, demand_d,
    dual_s, dual_r, total_v, cross_r, above_s, above_r, bar_s, bar_r,
    gbar_v, sbar_v, price_v, spread, onehot, highhot, placed_v, sent,
    in_sem, send_sem, recv_sem, year_ready,
):
    years_dev, hours_dev, hours, years, level_scale, node_scale, hour_count = sizes
    rows = years_dev * hours_dev
    me_h, me_y, me_l = lax.axis_index("hours"), lax.axis_index("years"), lax.axis_index("lines")
    hi_count, line_local = ptdf_v.shape[0], ptdf_v.shape[1]
    padded = flow8.shape[0]
    gen_rows, store_rows = gnode_v.shape[0], snode_v.shape[0]
    link = dual_s.dtype
    block_rows = store_rows * link.itemsize // 4
    base_rows = 2 * rows * hi_count + ((hours - 1) * (years_dev + 1) + years - 1) * block_rows

    order = (
        (upper_h, upper_v, 0), (lower_h, lower_v, 0), (flow_h, flow_v, 1),
    ) + tuple((ptdf_h.at[:, pl.ds(j * LANES, LANES)], ptdf_v.at[j], 1) for j in range(hi_count)) + (
        (snode_h, snode_v, 2), (gnode_h, gnode_v, 2), (store_h, store_v, 2), (power_h, power_v, 2),
        (gen_h, gen_v, 2), (cost_h, cost_v, 2), (cap_h, cap_v, 2), (avail_h, avail_v, 2),
        (demand_h, demand_v, 2), (limit_h, limit_v, 2), (capex_h, capex_v, 2), (capacity_h, capacity_v, 2),
        (balance_h, balance_v, 2),
    )
    loads = [pltpu.make_async_copy(s, d, in_sem.at[i]) for s, d, i in order]
    for copy in loads:
        copy.start()

    def wide(ref, first, count):
        return jnp.concatenate([ref[first + i] for i in range(count)], axis=1)

    def multiply(jobs, transpose):
        stage = [0, 0]
        for unit, acc, left, right in jobs:
            pltpu.matmul_push_rhs(right, stage[unit], unit, transpose=transpose)
            pltpu.matmul_acc_lhs(acc, left, load_staged_rhs=stage[unit])
            stage[unit] = 1 - stage[unit]

    def tile(i, rows_from):
        rows_here = pl.ds(rows_from * TILE, TILE)
        return jnp.concatenate([ptdf_v[2 * i, rows_here], ptdf_v[2 * i + 1, rows_here]], axis=1)

    def scoped(height, count, body):
        specs = [pltpu.ACC(mxu_id=i)((height, TILE), jnp.float32) for i in range(2) for _ in range(count)]
        pl.run_scoped(lambda *accs: body((accs[:count], accs[count:])), *specs)

    def cols(i):
        return slice(i * TILE, (i + 1) * TILE)

    node_tiles, line_tiles = hi_count * LANES // TILE, line_local // TILE

    def peer(k, j):
        return {"hours": lax.rem(me_h + k, hours), "years": lax.rem(me_y + j, years)}

    partner = {"lines": 1 - me_l}
    barrier = pltpu.get_barrier_semaphore()

    def ready(device):
        pl.semaphore_signal(barrier, inc=1, device_id=device, device_id_type=MESH)

    dual_r[...] = jnp.zeros_like(dual_r)
    bar_r[...] = jnp.zeros_like(bar_r)
    cross_r[...] = jnp.zeros_like(cross_r)
    above_r[...] = jnp.zeros_like(above_r)
    ready(partner)
    for k in range(1, hours):
        @pl.when(me_h + k < hours)
        def _(k=k):
            ready(peer(k, 0))
    for j in range(1, years):
        @pl.when(me_y + j < years)
        def _(j=j):
            ready(peer(0, j))
            for k in range(1, hours):
                @pl.when(me_h + k < hours)
                def _(k=k):
                    ready(peer(k, j))

    pl.semaphore_wait(barrier, 1 + me_y + me_h * (1 + me_y))
    for j in range(1, years):
        @pl.when(me_y + j >= years)
        def _(j=j):
            pl.semaphore_signal(year_ready, inc=1, device_id=peer(0, j), device_id_type=MESH)

    loads[0].wait()
    loads[1].wait()
    local_upper = None
    for y in range(years_dev):
        total = None
        for h in range(hours_dev):
            r = y * hours_dev + h
            diff = upper_v[r] - lower_v[r]
            total = diff if total is None else total + diff
            local_upper = upper_v[r] if local_upper is None else local_upper + upper_v[r]
        dual_s[y] = total.astype(link)
    dual_s[years_dev] = local_upper.astype(link)
    total_v[...] = local_upper

    def remote(src, dst, sem, device):
        return pltpu.make_async_remote_copy(
            src_ref=src, dst_ref=dst, send_sem=send_sem, recv_sem=recv_sem.at[sem],
            device_id=device, device_id_type=MESH,
        )

    def arrive(ref, sem):
        pltpu.make_async_copy(ref, ref, sem).wait()

    def dual_copy(k):
        return remote(dual_s, dual_r.at[k - 1], 2, peer(hours - k, 0))

    def bar_copy(k):
        return remote(bar_s, bar_r.at[k - 1], 3, peer(k, 0))

    def cross_copy(k, j):
        slot = cross_r.at[k, j - 1]
        return remote(dual_s.at[years_dev], slot, 4 if k else 5, peer(hours - k, years - j))

    def above_copy(j):
        return remote(above_s, above_r.at[j - 1], 6, peer(0, j))

    net_copy = remote(net_s, net_r, 0, partner)
    inj_copy = remote(inj_s, inj_r, 1, partner)

    for k in range(hours - 1, 0, -1):
        @pl.when(me_h >= k)
        def _(k=k):
            dual_copy(k).start()
    for j in range(1, years):
        @pl.when(me_y >= j)
        def _(j=j):
            cross_copy(0, j).start()
    for j in range(1, years):
        for k in range(hours - 1, 0, -1):
            @pl.when(jnp.logical_and(me_h >= k, me_y >= j))
            def _(k=k, j=j):
                cross_copy(k, j).start()

    for copy in loads[2 : 3 + hi_count]:
        copy.wait()
    flow8[...] = jnp.zeros_like(flow8)
    for r in range(rows):
        flow8[r : r + 1, :] = flow_v[r]
    dual_half = flow8[...].astype(jnp.bfloat16)
    for first in range(0, node_tiles, 2 * THIN):
        def nodes_group(accs, first=first):
            group = range(first, min(first + 2 * THIN, node_tiles))
            jobs = [
                (n % 2, accs[n % 2][(n - first) // 2], dual_half[:, cols(k)], tile(n, k))
                for base in group[::2] for k in range(line_tiles) for n in (base, base + 1) if n in group
            ]
            multiply(jobs, False)
            for n in group:
                net_s[:, cols(n)] = pltpu.matmul_pop(accs[n % 2][(n - first) // 2])[:rows]

        scoped(padded, THIN, nodes_group)
    net_copy.start()

    @pl.when(me_y < years - 1)
    def _():
        pl.semaphore_wait(year_ready, years - 1 - me_y)

    for j in range(1, years):
        @pl.when(me_y + j < years)
        def _(j=j):
            cross_copy(0, years - j).start()

    for copy in loads[3 + hi_count :]:
        copy.wait()
    high_rows = lax.broadcasted_iota(jnp.int32, (hi_count, LANES), 0)
    lane_rows = lax.broadcasted_iota(jnp.int32, (LANES, LANES), 0)

    def node_row(a):
        if a < store_rows:
            return snode_v[a : a + 1, :]
        return gnode_v[a - store_rows : a - store_rows + 1, :]

    for a in range(store_rows + gen_rows):
        low = jnp.broadcast_to(node_row(a) % LANES, (LANES, LANES))
        onehot[a] = jnp.where(low == lane_rows, 1.0, 0.0).astype(jnp.bfloat16)
        high = jnp.broadcast_to(node_row(a) // LANES, (hi_count, LANES))
        highhot[a] = jnp.where(high == high_rows, 1.0, 0.0).astype(jnp.bfloat16)

    for r in range(rows):
        for j in range(hi_count):
            piece = slice(j * LANES, (j + 1) * LANES)
            demand_d[r, j : j + 1, :] = demand_v[r : r + 1, piece].astype(jnp.float32)
        for j in range(gen_rows):
            piece = slice(j * LANES, (j + 1) * LANES)
            avail_d[r, j : j + 1, :] = avail_v[r : r + 1, piece].astype(jnp.float32)

    net_copy.wait_recv()
    prices = net_s[...] + net_r[...]

    def gather(r, node):
        price_row = prices[r : r + 1] + node_scale * balance_v[:, r : r + 1]
        high, low = node // LANES, node % LANES
        result = jnp.zeros(node.shape, jnp.float32)
        for j in range(hi_count):
            table = jnp.broadcast_to(price_row[:, j * LANES : (j + 1) * LANES], node.shape)
            picked = jnp.take_along_axis(table, low, axis=1, mode="promise_in_bounds")
            result = jnp.where(high == j, picked, result)
        return result

    for r in range(rows):
        for b in range(0, store_rows, 8):
            price_v[r, b : b + 8] = gather(r, snode_v[b : b + 8])

    for r in range(rows):
        for b in range(0, gen_rows, 8):
            part = slice(b, b + 8)
            price = gather(r, gnode_v[part])
            new = gen_v[r, part] - TAU * (cost_v[part] + price)
            new = jnp.minimum(jnp.maximum(new, 0.0), cap_v[part] * avail_d[r, part])
            gen_w[r, part] = new
            gbar_v[r, part] = 2.0 * new - gen_v[r, part]

    def place(values, sign, first, count, start, target):
        for r in range(rows):
            rest = sign * values[r]
            for p in range(SPLITS):
                piece = rest.astype(jnp.bfloat16).astype(jnp.float32)
                rest = rest - piece
                base = (r * SPLITS + p) * hi_count
                for a in range(count):
                    row = jnp.broadcast_to(piece[a : a + 1], (hi_count, LANES)).astype(jnp.bfloat16)
                    spread[first + a, base : base + hi_count] = row * highhot[first + a]
        jobs = []
        for t in range(count // 4):
            a = first + 4 * t
            left = jnp.concatenate([wide(spread, a, 2), wide(spread, a + 2, 2)], axis=0)
            right = jnp.concatenate([wide(onehot, a, 2), wide(onehot, a + 2, 2)], axis=0)
            jobs.append((t % 2, left, right))
        height = rows * SPLITS * hi_count

        def finish(accs):
            multiply([(i, accs[i][0], left, right) for i, left, right in jobs], True)
            for i in range(2):
                both = pltpu.matmul_pop(accs[i][0])
                part = both[:height, :LANES] + both[height:, LANES:]
                target[...] = part + (start if i == 0 else target[...])

        scoped(2 * height, 1, finish)

    place(gbar_v, 1.0, store_rows, gen_rows, 0.0, placed_v)

    arrive(cross_r.at[0], recv_sem.at[5])
    hour_upper = total_v[...]
    for j in range(1, years):
        hour_upper = hour_upper + cross_r[0, j - 1].astype(jnp.float32)
    total_v[...] = hour_upper
    bar_s[years_dev] = hour_upper.astype(link)

    for count in range(1, hours):
        @pl.when(me_h + count == hours - 1)
        def _(count=count):
            arrive(dual_r.at[pl.ds(0, count)], recv_sem.at[2])
    above = dual_r[0, years_dev].astype(jnp.float32)
    for k in range(2, hours):
        above = above + dual_r[k - 1, years_dev].astype(jnp.float32)
    above_s[...] = above.astype(link)
    for y in range(years_dev):
        beyond = dual_r[0, y].astype(jnp.float32)
        for k in range(2, hours):
            beyond = beyond + dual_r[k - 1, y].astype(jnp.float32)
        bar_total = None
        for h in reversed(range(hours_dev)):
            r = y * hours_dev + h
            beyond = beyond + (upper_v[r] - lower_v[r])
            suffix = level_scale * beyond
            power = power_v[...]
            new = store_v[r] - TAU * (suffix - price_v[r])
            new = jnp.minimum(jnp.maximum(new, -power), power)
            store_w[r] = new
            sbar = 2.0 * new - store_v[r]
            sbar_v[r] = sbar
            bar_total = sbar if bar_total is None else bar_total + sbar
        bar_s[y] = bar_total.astype(link)
    for k in range(hours - 1, 0, -1):
        @pl.when(me_h + k < hours)
        def _(k=k):
            bar_copy(k).start()
    for j in range(1, years):
        @pl.when(jnp.logical_and(me_h < hours - 1, me_y + j < years))
        def _(j=j):
            above_copy(j).start()
    total_v[...] = total_v[...] + above
    place(sbar_v, -1.0, 0, store_rows, placed_v[...], placed_v)
    placed = placed_v[...]
    for r in range(rows):
        total = None
        for p in range(SPLITS):
            base = (r * SPLITS + p) * hi_count
            piece = placed[base : base + hi_count]
            total = piece if total is None else total + piece
        inj_s[r] = total
    inj_copy.start()

    for c in range(line_local // LANES):
        limit1[:, c * LANES : (c + 1) * LANES] = limit_v[c : c + 1, :]
    inj8[...] = jnp.zeros_like(inj8)

    inj_copy.wait_recv()
    for r in range(rows):
        inject = inj_s[r] + inj_r[r] - demand_d[r]
        balance_o[:, r : r + 1] = balance_v[:, r : r + 1] + SIGMA * node_scale * jnp.sum(inject, keepdims=True)
        for j in range(hi_count):
            inj8[r : r + 1, j * LANES : (j + 1) * LANES] = inject[j : j + 1]
    inject_half = inj8[...].astype(jnp.bfloat16)
    for first in range(0, line_tiles, THIN):
        def lines_group(accs, first=first):
            group = range(first, min(first + THIN, line_tiles))
            multiply([
                (k % 2, accs[k % 2][n - first], inject_half[:, cols(k)], tile(k, n))
                for n in group for k in range(node_tiles)
            ], True)
            for i, n in enumerate(group):
                line8[:, cols(n)] = pltpu.matmul_pop(accs[0][i]) + pltpu.matmul_pop(accs[1][i])

        scoped(padded, THIN, lines_group)
    line_flows = line8[...]
    shifted = flow8[...] + SIGMA * line_flows
    limit = limit1[...]
    line_next = shifted - SIGMA * jnp.minimum(jnp.maximum(shifted * (1.0 / SIGMA), -limit), limit)
    for r in range(rows):
        flow_w[r] = line_next[r : r + 1]

    for j in range(1, years):
        for k in range(1, hours):
            @pl.when(jnp.logical_and(me_h + k == hours - 1, me_y + j == years - 1))
            def _(k=k, j=j):
                arrive(cross_r.at[pl.ds(1, k), pl.ds(0, j)], recv_sem.at[4])

        @pl.when(jnp.logical_and(me_h < hours - 1, me_y == j))
        def _(j=j):
            arrive(above_r.at[pl.ds(0, j)], recv_sem.at[6])
    for count in range(1, hours):
        @pl.when(me_h == count)
        def _(count=count):
            arrive(bar_r.at[pl.ds(0, count)], recv_sem.at[3])
    upper_total = total_v[...]
    for k in range(1, hours):
        upper_total = upper_total + bar_r[k - 1, years_dev].astype(jnp.float32)
        for j in range(1, years):
            upper_total = upper_total + cross_r[k, j - 1].astype(jnp.float32)
    for j in range(1, years):
        upper_total = upper_total + above_r[j - 1].astype(jnp.float32)
    capacity_next = jnp.maximum(capacity_v[...] - TAU_CAP * (capex_v[...] - upper_total / hour_count), 0.0)
    capacity_w[...] = capacity_next
    capacity_bar = 2.0 * capacity_next - capacity_v[...]

    for y in range(years_dev):
        before = bar_r[0, y].astype(jnp.float32)
        for k in range(2, hours):
            before = before + bar_r[k - 1, y].astype(jnp.float32)
        for h in range(hours_dev):
            r = y * hours_dev + h
            before = before + sbar_v[r]
            level = level_scale * before
            upper_w[r] = jnp.maximum(upper_v[r] + SIGMA * (level - capacity_bar), 0.0)
            lower_w[r] = jnp.maximum(lower_v[r] - SIGMA * level, 0.0)

    for y in range(years):
        for h in range(hours):
            blocks = h * y + (years - 1 - y if h < hours - 1 else 0)

            @pl.when(jnp.logical_and(me_h == h, me_y == y))
            def _(blocks=blocks):
                arrive(sent.at[pl.ds(0, base_rows + blocks * block_rows)], send_sem)


def finish_kernel(count, *refs):
    sources, targets, sem = refs[:count], refs[count : 2 * count], refs[2 * count]
    copies = [pltpu.make_async_copy(s, t, sem) for s, t in zip(sources, targets)]
    for copy in copies:
        copy.start()
    for copy in copies:
        copy.wait()


def local(
    mesh,
    demand, avail, ptdf, line_limit, gen_cost, gen_cap, gen_node, store_node, store_power,
    capex, gen_state, store_state, level_upper, level_lower, flow_dual, balance_dual, capacity,
):
    years_dev, hours_dev, nodes = demand.shape
    rows = years_dev * hours_dev
    hours, years = lax.axis_size("hours"), lax.axis_size("years")
    hours_total = hours_dev * hours
    hour_count = years_dev * years * hours_total
    level_scale = 1.0 / math.sqrt(hours_total)
    node_scale = 1.0 / math.sqrt(nodes)
    sizes = (years_dev, hours_dev, hours, years, level_scale, node_scale, hour_count)

    def fold(x):
        return x.reshape(-1, LANES)

    def fold_rows(x):
        return x.reshape(rows, -1, LANES)

    args = (
        demand.reshape(rows, nodes), avail.reshape(rows, -1), ptdf, fold(line_limit), fold(gen_cost),
        fold(gen_cap), fold(gen_node), fold(store_node), fold(store_power), fold(capex),
        fold_rows(gen_state), fold_rows(store_state), fold_rows(level_upper), fold_rows(level_lower),
        flow_dual.reshape(rows, 1, -1), fold(capacity), balance_dual.reshape(1, rows),
    )
    f32 = jnp.float32
    gen_rows, store_rows = args[6].shape[0], args[7].shape[0]
    line_local, hi_count = ptdf.shape[0], nodes // LANES
    padded = max(16, -(-rows // 16) * 16)
    out_shapes = [
        (rows, gen_rows, LANES), (rows, store_rows, LANES), (store_rows, LANES),
        (rows, 1, line_local), (rows, store_rows, LANES), (rows, store_rows, LANES),
    ]
    any_spec = pl.BlockSpec(memory_space=pl.ANY)
    block, blocks = (store_rows, LANES), (years_dev + 1, store_rows, LANES)
    h1, y1 = max(hours - 1, 1), max(years - 1, 1)
    dma = pltpu.SemaphoreType.DMA
    block_rows = store_rows * jnp.dtype(LINK).itemsize // 4
    sent_rows = 2 * rows * hi_count + (hours - 1) * (years_dev + 1) * block_rows + (hours + 1) * years * block_rows
    scratch = [pltpu.VMEM(a.shape, a.dtype) for a in args]
    scratch[2] = pltpu.VMEM((hi_count, line_local, LANES), ptdf.dtype)
    scratch += [
        pltpu.VMEM((padded, line_local), f32), pltpu.VMEM((1, line_local), f32),
        pltpu.VMEM((rows, nodes), f32), pltpu.VMEM((rows, nodes), f32),
        pltpu.VMEM((rows, hi_count, LANES), f32), pltpu.VMEM((rows, hi_count, LANES), f32),
        pltpu.VMEM((padded, nodes), f32), pltpu.VMEM((padded, line_local), f32),
        pltpu.VMEM((rows, gen_rows, LANES), f32),
        pltpu.VMEM((rows, hi_count, LANES), f32),
        pltpu.VMEM(blocks, LINK), pltpu.VMEM((h1,) + blocks, LINK),
        pltpu.VMEM(block, f32), pltpu.VMEM((hours, y1) + block, LINK),
        pltpu.VMEM(block, LINK), pltpu.VMEM((y1,) + block, LINK),
        pltpu.VMEM(blocks, LINK), pltpu.VMEM((h1,) + blocks, LINK),
        pltpu.VMEM((rows, gen_rows, LANES), f32), pltpu.VMEM((rows, store_rows, LANES), f32),
        pltpu.VMEM((rows, store_rows, LANES), f32),
        pltpu.VMEM((gen_rows + store_rows, rows * SPLITS * hi_count, LANES), jnp.bfloat16),
        pltpu.VMEM((gen_rows + store_rows, LANES, LANES), jnp.bfloat16),
        pltpu.VMEM((gen_rows + store_rows, hi_count, LANES), jnp.bfloat16),
        pltpu.VMEM((rows * SPLITS * hi_count, LANES), f32),
        pltpu.VMEM((sent_rows, LANES), f32),
        dma((3,)), dma, dma((7,)), pltpu.SemaphoreType.REGULAR,
    ]
    results = pl.pallas_call(
        functools.partial(step_kernel, sizes),
        out_shape=[pltpu.VMEM(s, f32) for s in out_shapes] + [pltpu.VMEM((1, rows), f32)],
        in_specs=[any_spec] * 17,
        out_specs=[pl.BlockSpec(memory_space=pltpu.VMEM)] * 7,
        scratch_shapes=scratch,
        compiler_params=pltpu.CompilerParams(
            collective_id=0, has_side_effects=True, vmem_limit_bytes=56 * 1024 * 1024
        ),
    )(*args)
    gen, store, cap, flow, upper, lower, balance = pl.pallas_call(
        functools.partial(finish_kernel, len(results)),
        out_shape=[jax.ShapeDtypeStruct(x.shape, f32) for x in results],
        in_specs=[pl.BlockSpec(memory_space=pltpu.VMEM)] * len(results),
        out_specs=[any_spec] * len(results),
        scratch_shapes=[dma],
    )(*[pltpu.with_memory_space_constraint(x, pltpu.VMEM) for x in results])
    return (
        gen.reshape(gen_state.shape), store.reshape(store_state.shape), cap.reshape(capacity.shape),
        balance.reshape(balance_dual.shape), flow.reshape(flow_dual.shape),
        upper.reshape(level_upper.shape), lower.reshape(level_lower.shape),
    )


def solution(mesh):
    row = P(("groups", "years"), "hours", "lines")
    line = P("lines")
    in_specs = (
        P(("groups", "years"), "hours", None), row, P("lines", None), line, line, line, line, line,
        line, line, row, row, row, row, row, P(("groups", "years"), "hours"), P(("groups", "lines")),
    )
    out_specs = (row, row, P(("groups", "lines")), P(("groups", "years"), "hours"), row, row, row)
    step = jax.shard_map(functools.partial(local, mesh), mesh=mesh, in_specs=in_specs, out_specs=out_specs, check_vma=False)

    def run(*args):
        with jax.sharding.use_abstract_mesh(mesh.abstract_mesh):
            return step(*args)

    return run
```

```python
import functools
import math

import jax
import jax.numpy as jnp
from jax import lax
from jax.experimental import pallas as pl
from jax.experimental.pallas import tpu as pltpu
from jax.sharding import PartitionSpec as P

TAU = 0.1
SIGMA = 0.5
TAU_CAP = 1.0
LANES = 128
SPLITS = 2
TILE = 256
THIN = 4
LINK = jnp.bfloat16
MESH = pl.DeviceIdType.MESH


def step_kernel(
    sizes,
    demand_h, avail_h, ptdf_h, limit_h, cost_h, cap_h, gnode_h, snode_h, power_h,
    capex_h, gen_h, store_h, upper_h, lower_h, flow_h, capacity_h, balance_h,
    gen_w, store_w, capacity_w, flow_w, upper_w, lower_w, balance_o,
    demand_v, avail_v, ptdf_v, limit_v, cost_v, cap_v, gnode_v, snode_v, power_v,
    capex_v, gen_v, store_v, upper_v, lower_v, flow_v, capacity_v, balance_v,
    flow8, limit1, net_s, net_r, inj_s, inj_r, inj8, line8, avail_d, demand_d,
    dual_s, dual_r, total_v, cross_r, above_s, above_r, up_s, up_r, bar_s, bar_r,
    gbar_v, sbar_v, price_v, onehot, highhot, placed_v, sent,
    mate_s, mate_v, mate_node, mate_bar, mate_r, bal_s, bal_r,
    in_sem, send_sem, recv_sem, year_ready, hour_ready,
):
    years_dev, hours_dev, hours, years, level_scale, node_scale, hour_count = sizes
    rows = years_dev * hours_dev
    me_h, me_y, me_l = lax.axis_index("hours"), lax.axis_index("years"), lax.axis_index("lines")
    hi_count, line_local = ptdf_v.shape[0], ptdf_v.shape[1]
    padded = flow8.shape[0]
    gen_rows, store_rows = gnode_v.shape[0], snode_v.shape[0]
    link = dual_s.dtype
    block_rows = store_rows * link.itemsize // 4
    base_rows = 2 * rows * hi_count + 8 * rows + ((hours - 1) * (years_dev + 1) + years - 1) * block_rows

    order = (
        (upper_h, upper_v, 0), (lower_h, lower_v, 0), (flow_h, flow_v, 1),
    ) + tuple((ptdf_h.at[:, pl.ds(j * LANES, LANES)], ptdf_v.at[j], 1) for j in range(hi_count)) + (
        (snode_h, snode_v, 2), (gnode_h, gnode_v, 2), (store_h, store_v, 2), (power_h, power_v, 2),
        (gen_h, gen_v, 2), (cost_h, cost_v, 2), (cap_h, cap_v, 2), (avail_h, avail_v, 2),
        (demand_h, demand_v, 2), (limit_h, limit_v, 2), (capex_h, capex_v, 2), (capacity_h, capacity_v, 2),
        (balance_h, balance_v, 2),
    )
    loads = [pltpu.make_async_copy(s, d, in_sem.at[i]) for s, d, i in order]
    for copy in loads:
        copy.start()

    def wide(ref, first, count):
        return jnp.concatenate([ref[first + i] for i in range(count)], axis=1)

    def multiply(jobs, transpose):
        stage = [0, 0]
        for unit, acc, left, right in jobs:
            pltpu.matmul_push_rhs(right, stage[unit], unit, transpose=transpose)
            pltpu.matmul_acc_lhs(acc, left, load_staged_rhs=stage[unit])
            stage[unit] = 1 - stage[unit]

    def tile(i, rows_from):
        rows_here = pl.ds(rows_from * TILE, TILE)
        return jnp.concatenate([ptdf_v[2 * i, rows_here], ptdf_v[2 * i + 1, rows_here]], axis=1)

    def scoped(height, count, body):
        specs = [pltpu.ACC(mxu_id=i)((height, TILE), jnp.float32) for i in range(2) for _ in range(count)]
        pl.run_scoped(lambda *accs: body((accs[:count], accs[count:])), *specs)

    def cols(i):
        return slice(i * TILE, (i + 1) * TILE)

    node_tiles, line_tiles = hi_count * LANES // TILE, line_local // TILE

    def peer(k, j):
        return {"hours": lax.rem(me_h + k, hours), "years": lax.rem(me_y + j, years)}

    partner = {"lines": 1 - me_l}
    barrier = pltpu.get_barrier_semaphore()

    def ready(device):
        pl.semaphore_signal(barrier, inc=1, device_id=device, device_id_type=MESH)

    dual_r[...] = jnp.zeros_like(dual_r)
    bar_r[...] = jnp.zeros_like(bar_r)
    up_r[...] = jnp.zeros_like(up_r)
    cross_r[...] = jnp.zeros_like(cross_r)
    mate_r[...] = jnp.zeros_like(mate_r)
    above_r[...] = jnp.zeros_like(above_r)
    ready(partner)
    for k in range(1, hours):
        @pl.when(me_h + k < hours)
        def _(k=k):
            ready(peer(k, 0))
        @pl.when(jnp.logical_and(me_h + k < hours, me_l == 1))
        def _(k=k):
            ready({**peer(k, 0), **partner})
    for j in range(1, years):
        @pl.when(me_y + j < years)
        def _(j=j):
            ready(peer(0, j))
            for k in range(1, hours):
                @pl.when(me_h + k < hours)
                def _(k=k):
                    ready(peer(k, j))

    pl.semaphore_wait(barrier, 1 + me_y + me_h * (2 + me_y - me_l))
    for j in range(1, years):
        @pl.when(me_y + j >= years)
        def _(j=j):
            pl.semaphore_signal(year_ready, inc=1, device_id=peer(0, j), device_id_type=MESH)
    for k in range(hours - 1, 0, -1):
        @pl.when(me_h >= k)
        def _(k=k):
            pl.semaphore_signal(hour_ready, inc=1, device_id=peer(hours - k, 0), device_id_type=MESH)

    loads[0].wait()
    loads[1].wait()
    local_upper = None
    for y in range(years_dev):
        total = None
        for h in range(hours_dev):
            r = y * hours_dev + h
            diff = upper_v[r] - lower_v[r]
            total = diff if total is None else total + diff
            local_upper = upper_v[r] if local_upper is None else local_upper + upper_v[r]
        dual_s[y] = total.astype(link)
    dual_s[years_dev] = local_upper.astype(link)
    total_v[...] = local_upper

    def remote(src, dst, sem, device):
        return pltpu.make_async_remote_copy(
            src_ref=src, dst_ref=dst, send_sem=send_sem, recv_sem=recv_sem.at[sem],
            device_id=device, device_id_type=MESH,
        )

    def arrive(ref, sem):
        pltpu.make_async_copy(ref, ref, sem).wait()

    def dual_copy(k):
        return remote(dual_s, dual_r.at[k - 1], 2, peer(hours - k, 0))

    def bar_copy(k):
        return remote(bar_s, bar_r.at[k - 1], 3, peer(k, 0))

    def mate_dual_copy(k):
        return remote(dual_s.at[pl.ds(0, years_dev)], mate_r.at[k - 1], 8, {**peer(hours - k, 0), **partner})

    node_copy = remote(snode_v, mate_node, 9, partner)
    mate_copy = remote(mate_s, mate_v, 10, partner)
    bal_copy = remote(bal_s, bal_r, 11, partner)

    def up_copy(k):
        return remote(up_s, up_r.at[k - 1], 7, peer(k, 0))

    def cross_copy(k, j):
        slot = cross_r.at[k, j - 1]
        return remote(dual_s.at[years_dev], slot, 4 if k else 5, peer(hours - k, years - j))

    def above_copy(j):
        return remote(above_s, above_r.at[j - 1], 6, peer(0, j))

    net_copy = remote(net_s, net_r, 0, partner)
    inj_copy = remote(inj_s, inj_r, 1, partner)

    for j in range(1, years):
        for k in range(hours - 1, 0, -1):
            @pl.when(jnp.logical_and(me_h >= k, me_y >= j))
            def _(k=k, j=j):
                cross_copy(k, j).start()
    for k in range(hours - 1, 0, -1):
        @pl.when(me_h >= k)
        def _(k=k):
            dual_copy(k).start()

        @pl.when(jnp.logical_and(me_h >= k, me_l == 0))
        def _(k=k):
            mate_dual_copy(k).start()
    for j in range(1, years):
        @pl.when(me_y >= j)
        def _(j=j):
            cross_copy(0, j).start()

    for copy in loads[2 : 3 + hi_count]:
        copy.wait()
    flow8[...] = jnp.zeros_like(flow8)
    for r in range(rows):
        flow8[r : r + 1, :] = flow_v[r]
    dual_half = flow8[...].astype(jnp.bfloat16)
    for first in range(0, node_tiles, 2 * THIN):
        def nodes_group(accs, first=first):
            group = range(first, min(first + 2 * THIN, node_tiles))
            jobs = [
                (n % 2, accs[n % 2][(n - first) // 2], dual_half[:, cols(k)], tile(n, k))
                for base in group[::2] for k in range(line_tiles) for n in (base, base + 1) if n in group
            ]
            multiply(jobs, False)
            for n in group:
                net_s[:, cols(n)] = pltpu.matmul_pop(accs[n % 2][(n - first) // 2])[:rows]

        scoped(padded, THIN, nodes_group)
    net_copy.start()

    @pl.when(me_y < years - 1)
    def _():
        pl.semaphore_wait(year_ready, years - 1 - me_y)

    for j in range(1, years):
        @pl.when(me_y + j < years)
        def _(j=j):
            cross_copy(0, years - j).start()

    for copy in loads[3 + hi_count :]:
        copy.wait()

    @pl.when(me_l == 0)
    def _():
        node_copy.start()
    high_rows = lax.broadcasted_iota(jnp.int32, (hi_count, LANES), 0)
    lane_rows = lax.broadcasted_iota(jnp.int32, (LANES, LANES), 0)

    def encode(ref, first, count):
        for a in range(count):
            row = ref[a : a + 1, :]
            low = jnp.broadcast_to(row % LANES, (LANES, LANES))
            onehot[first + a] = jnp.where(low == lane_rows, 1.0, 0.0).astype(jnp.bfloat16)
            high = jnp.broadcast_to(row // LANES, (hi_count, LANES))
            highhot[first + a] = jnp.where(high == high_rows, 1.0, 0.0).astype(jnp.bfloat16)

    encode(snode_v, 0, store_rows)
    encode(gnode_v, store_rows, gen_rows)
    for r in range(rows):
        for j in range(hi_count):
            piece = slice(j * LANES, (j + 1) * LANES)
            demand_d[r, j : j + 1, :] = demand_v[r : r + 1, piece].astype(jnp.float32)
        for j in range(gen_rows):
            piece = slice(j * LANES, (j + 1) * LANES)
            avail_d[r, j : j + 1, :] = avail_v[r : r + 1, piece].astype(jnp.float32)

    net_copy.wait_recv()
    prices = net_s[...] + net_r[...]

    def gather(r, node):
        price_row = prices[r : r + 1] + node_scale * balance_v[:, r : r + 1]
        high, low = node // LANES, node % LANES
        result = jnp.zeros(node.shape, jnp.float32)
        for j in range(hi_count):
            table = jnp.broadcast_to(price_row[:, j * LANES : (j + 1) * LANES], node.shape)
            picked = jnp.take_along_axis(table, low, axis=1, mode="promise_in_bounds")
            result = jnp.where(high == j, picked, result)
        return result

    for r in range(rows):
        for b in range(0, store_rows, 8):
            price_v[r, b : b + 8] = gather(r, snode_v[b : b + 8])

    @pl.when(me_l == 0)
    def _():
        mate_s[2 * rows] = power_v[...]
        for y in range(years_dev):
            own = None
            for h in reversed(range(hours_dev)):
                r = y * hours_dev + h
                diff = upper_v[r] - lower_v[r]
                own = diff if own is None else own + diff
                mate_s[r] = store_v[r] - TAU * (level_scale * own - price_v[r])
                mate_s[rows + r] = store_v[r]
        mate_copy.start()

    for r in range(rows):
        for b in range(0, gen_rows, 8):
            part = slice(b, b + 8)
            price = gather(r, gnode_v[part])
            new = gen_v[r, part] - TAU * (cost_v[part] + price)
            new = jnp.minimum(jnp.maximum(new, 0.0), cap_v[part] * avail_d[r, part])
            gen_w[r, part] = new
            gbar_v[r, part] = 2.0 * new - gen_v[r, part]

    def place(values, sign, first, count, start, target):
        pieces = []
        for r in range(rows):
            rest = sign * values[r]
            for _ in range(SPLITS):
                piece = rest.astype(jnp.bfloat16).astype(jnp.float32)
                rest = rest - piece
                pieces.append(piece)

        def spread(a):
            return jnp.concatenate([
                jnp.broadcast_to(piece[a : a + 1], (hi_count, LANES)).astype(jnp.bfloat16) * highhot[first + a]
                for piece in pieces
            ], axis=0)

        def pair(make, a):
            return jnp.concatenate([make(a), make(a + 1)], axis=1)

        jobs = []
        for t in range(count // 4):
            left = jnp.concatenate([pair(spread, 4 * t), pair(spread, 4 * t + 2)], axis=0)
            right = jnp.concatenate([wide(onehot, first + 4 * t, 2), wide(onehot, first + 4 * t + 2, 2)], axis=0)
            jobs.append((t % 2, left, right))
        height = rows * SPLITS * hi_count

        def finish(accs):
            multiply([(i, accs[i][0], left, right) for i, left, right in jobs], True)
            for i in range(2):
                both = pltpu.matmul_pop(accs[i][0])
                part = both[:height, :LANES] + both[height:, LANES:]
                target[...] = part + (start if i == 0 else target[...])

        scoped(2 * height, 1, finish)

    place(gbar_v, 1.0, store_rows, gen_rows, 0.0, placed_v)

    def inject_part(r):
        total = None
        for p in range(SPLITS):
            base = (r * SPLITS + p) * hi_count
            piece = placed_v[base : base + hi_count]
            total = piece if total is None else total + piece
        return total

    @pl.when(me_l == 0)
    def _():
        for r in range(rows):
            inj_s[r] = inject_part(r)
        inj_copy.start()

    @pl.when(me_l == 1)
    def _():
        arrive(mate_node, recv_sem.at[9])
        encode(mate_node, store_rows + gen_rows, store_rows)
        arrive(mate_v, recv_sem.at[10])

    arrive(cross_r.at[0], recv_sem.at[5])
    hour_upper = total_v[...]
    for j in range(1, years):
        hour_upper = hour_upper + cross_r[0, j - 1].astype(jnp.float32)
    total_v[...] = hour_upper
    up_s[...] = hour_upper.astype(link)

    @pl.when(me_h < hours - 1)
    def _():
        pl.semaphore_wait(hour_ready, hours - 1 - me_h)
        for k in range(hours - 1, 0, -1):
            @pl.when(me_h + k < hours)
            def _(k=k):
                up_copy(k).start()

    for count in range(1, hours):
        @pl.when(me_h + count == hours - 1)
        def _(count=count):
            arrive(dual_r.at[pl.ds(0, count)], recv_sem.at[2])
    above = dual_r[0, years_dev].astype(jnp.float32)
    for k in range(2, hours):
        above = above + dual_r[k - 1, years_dev].astype(jnp.float32)
    above_s[...] = above.astype(link)
    for y in range(years_dev):
        beyond = dual_r[0, y].astype(jnp.float32)
        for k in range(2, hours):
            beyond = beyond + dual_r[k - 1, y].astype(jnp.float32)
        bar_total = None
        for h in reversed(range(hours_dev)):
            r = y * hours_dev + h
            beyond = beyond + (upper_v[r] - lower_v[r])
            suffix = level_scale * beyond
            power = power_v[...]
            new = store_v[r] - TAU * (suffix - price_v[r])
            new = jnp.minimum(jnp.maximum(new, -power), power)
            store_w[r] = new
            sbar = 2.0 * new - store_v[r]
            sbar_v[r] = sbar
            bar_total = sbar if bar_total is None else bar_total + sbar
        bar_s[y] = bar_total.astype(link)
    for k in range(hours - 1, 0, -1):
        @pl.when(me_h + k < hours)
        def _(k=k):
            bar_copy(k).start()
    for j in range(1, years):
        @pl.when(jnp.logical_and(me_h < hours - 1, me_y + j < years))
        def _(j=j):
            above_copy(j).start()
    total_v[...] = total_v[...] + above
    place(sbar_v, -1.0, 0, store_rows, placed_v[...], placed_v)

    @pl.when(me_l == 1)
    def _():
        for r in range(rows):
            inj_s[r] = inject_part(r)
        inj_copy.start()

    for r in range(rows):
        part = None
        for b in range(0, gen_rows, 8):
            part = gbar_v[r, b : b + 8] if part is None else part + gbar_v[r, b : b + 8]
        for b in range(0, store_rows, 8):
            part = part - sbar_v[r, b : b + 8]
        bal_s[r] = part
    bal_copy.start()

    for c in range(line_local // LANES):
        limit1[:, c * LANES : (c + 1) * LANES] = limit_v[c : c + 1, :]
    inj8[...] = jnp.zeros_like(inj8)

    @pl.when(me_l == 1)
    def _():
        for count in range(1, hours):
            @pl.when(me_h + count == hours - 1)
            def _(count=count):
                arrive(mate_r.at[pl.ds(0, count)], recv_sem.at[8])
        power = mate_v[2 * rows]
        for y in range(years_dev):
            beyond = mate_r[0, y].astype(jnp.float32)
            for k in range(2, hours):
                beyond = beyond + mate_r[k - 1, y].astype(jnp.float32)
            for h in range(hours_dev):
                r = y * hours_dev + h
                new = mate_v[r] - TAU * level_scale * beyond
                new = jnp.minimum(jnp.maximum(new, -power), power)
                mate_bar[r] = 2.0 * new - mate_v[rows + r]
        place(mate_bar, -1.0, store_rows + gen_rows, store_rows, placed_v[...], placed_v)

    inj_copy.wait_recv()
    for r in range(rows):
        inject = inject_part(r) + inj_r[r] - demand_d[r]
        for j in range(hi_count):
            inj8[r : r + 1, j * LANES : (j + 1) * LANES] = inject[j : j + 1]
    inject_half = inj8[...].astype(jnp.bfloat16)
    for first in range(0, line_tiles, THIN):
        def lines_group(accs, first=first):
            group = range(first, min(first + THIN, line_tiles))
            multiply([
                (k % 2, accs[k % 2][n - first], inject_half[:, cols(k)], tile(k, n))
                for n in group for k in range(node_tiles)
            ], True)
            for i, n in enumerate(group):
                line8[:, cols(n)] = pltpu.matmul_pop(accs[0][i]) + pltpu.matmul_pop(accs[1][i])

        scoped(padded, THIN, lines_group)
    line_flows = line8[...]
    shifted = flow8[...] + SIGMA * line_flows
    limit = limit1[...]
    line_next = shifted - SIGMA * jnp.minimum(jnp.maximum(shifted * (1.0 / SIGMA), -limit), limit)
    for r in range(rows):
        flow_w[r] = line_next[r : r + 1]

    for j in range(1, years):
        for k in range(1, hours):
            @pl.when(jnp.logical_and(me_h + k == hours - 1, me_y + j == years - 1))
            def _(k=k, j=j):
                arrive(cross_r.at[pl.ds(1, k), pl.ds(0, j)], recv_sem.at[4])

        @pl.when(jnp.logical_and(me_h < hours - 1, me_y == j))
        def _(j=j):
            arrive(above_r.at[pl.ds(0, j)], recv_sem.at[6])
    for count in range(1, hours):
        @pl.when(me_h == count)
        def _(count=count):
            arrive(bar_r.at[pl.ds(0, count)], recv_sem.at[3])
            arrive(up_r.at[pl.ds(0, count)], recv_sem.at[7])
    upper_total = total_v[...]
    for k in range(1, hours):
        upper_total = upper_total + up_r[k - 1].astype(jnp.float32)
        for j in range(1, years):
            upper_total = upper_total + cross_r[k, j - 1].astype(jnp.float32)
    for j in range(1, years):
        upper_total = upper_total + above_r[j - 1].astype(jnp.float32)
    capacity_next = jnp.maximum(capacity_v[...] - TAU_CAP * (capex_v[...] - upper_total / hour_count), 0.0)
    capacity_w[...] = capacity_next
    capacity_bar = 2.0 * capacity_next - capacity_v[...]

    for y in range(years_dev):
        before = bar_r[0, y].astype(jnp.float32)
        for k in range(2, hours):
            before = before + bar_r[k - 1, y].astype(jnp.float32)
        for h in range(hours_dev):
            r = y * hours_dev + h
            before = before + sbar_v[r]
            level = level_scale * before
            upper_w[r] = jnp.maximum(upper_v[r] + SIGMA * (level - capacity_bar), 0.0)
            lower_w[r] = jnp.maximum(lower_v[r] - SIGMA * level, 0.0)

    bal_copy.wait_recv()
    for r in range(rows):
        part = bal_s[r] + bal_r[r]
        for b in range(0, hi_count, 8):
            part = part - demand_d[r, b : b + 8]
        balance_o[:, r : r + 1] = balance_v[:, r : r + 1] + SIGMA * node_scale * jnp.sum(part, keepdims=True)

    for y in range(years):
        for h in range(hours):
            blocks = h * y + (years - 1 - y if h < hours - 1 else 0)
            extra = (2 * rows + 2) * store_rows + h * years_dev * block_rows

            @pl.when(jnp.logical_and(jnp.logical_and(me_h == h, me_y == y), me_l == 0))
            def _(size=base_rows + blocks * block_rows + extra):
                arrive(sent.at[pl.ds(0, size)], send_sem)

            @pl.when(jnp.logical_and(jnp.logical_and(me_h == h, me_y == y), me_l == 1))
            def _(size=base_rows + blocks * block_rows):
                arrive(sent.at[pl.ds(0, size)], send_sem)


def finish_kernel(count, *refs):
    sources, targets, sem = refs[:count], refs[count : 2 * count], refs[2 * count]
    copies = [pltpu.make_async_copy(s, t, sem) for s, t in zip(sources, targets)]
    for copy in copies:
        copy.start()
    for copy in copies:
        copy.wait()


def local(
    mesh,
    demand, avail, ptdf, line_limit, gen_cost, gen_cap, gen_node, store_node, store_power,
    capex, gen_state, store_state, level_upper, level_lower, flow_dual, balance_dual, capacity,
):
    years_dev, hours_dev, nodes = demand.shape
    rows = years_dev * hours_dev
    hours, years = lax.axis_size("hours"), lax.axis_size("years")
    hours_total = hours_dev * hours
    hour_count = years_dev * years * hours_total
    level_scale = 1.0 / math.sqrt(hours_total)
    node_scale = 1.0 / math.sqrt(nodes)
    sizes = (years_dev, hours_dev, hours, years, level_scale, node_scale, hour_count)

    def fold(x):
        return x.reshape(-1, LANES)

    def fold_rows(x):
        return x.reshape(rows, -1, LANES)

    args = (
        demand.reshape(rows, nodes), avail.reshape(rows, -1), ptdf, fold(line_limit), fold(gen_cost),
        fold(gen_cap), fold(gen_node), fold(store_node), fold(store_power), fold(capex),
        fold_rows(gen_state), fold_rows(store_state), fold_rows(level_upper), fold_rows(level_lower),
        flow_dual.reshape(rows, 1, -1), fold(capacity), balance_dual.reshape(1, rows),
    )
    f32 = jnp.float32
    gen_rows, store_rows = args[6].shape[0], args[7].shape[0]
    line_local, hi_count = ptdf.shape[0], nodes // LANES
    padded = max(16, -(-rows // 16) * 16)
    out_shapes = [
        (rows, gen_rows, LANES), (rows, store_rows, LANES), (store_rows, LANES),
        (rows, 1, line_local), (rows, store_rows, LANES), (rows, store_rows, LANES),
    ]
    any_spec = pl.BlockSpec(memory_space=pl.ANY)
    block, blocks = (store_rows, LANES), (years_dev + 1, store_rows, LANES)
    h1, y1 = max(hours - 1, 1), max(years - 1, 1)
    dma = pltpu.SemaphoreType.DMA
    block_rows = store_rows * jnp.dtype(LINK).itemsize // 4
    sent_rows = 2 * rows * hi_count + 8 * rows + (2 * rows + 2) * store_rows + hours * years_dev * block_rows + (hours - 1) * (years_dev + 1) * block_rows + (hours + 1) * years * block_rows
    scratch = [pltpu.VMEM(a.shape, a.dtype) for a in args]
    scratch[2] = pltpu.VMEM((hi_count, line_local, LANES), ptdf.dtype)
    scratch += [
        pltpu.VMEM((padded, line_local), f32), pltpu.VMEM((1, line_local), f32),
        pltpu.VMEM((rows, nodes), f32), pltpu.VMEM((rows, nodes), f32),
        pltpu.VMEM((rows, hi_count, LANES), f32), pltpu.VMEM((rows, hi_count, LANES), f32),
        pltpu.VMEM((padded, nodes), f32), pltpu.VMEM((padded, line_local), f32),
        pltpu.VMEM((rows, gen_rows, LANES), f32),
        pltpu.VMEM((rows, hi_count, LANES), f32),
        pltpu.VMEM(blocks, LINK), pltpu.VMEM((h1,) + blocks, LINK),
        pltpu.VMEM(block, f32), pltpu.VMEM((hours, y1) + block, LINK),
        pltpu.VMEM(block, LINK), pltpu.VMEM((y1,) + block, LINK),
        pltpu.VMEM(block, LINK), pltpu.VMEM((h1,) + block, LINK),
        pltpu.VMEM((years_dev,) + block, LINK), pltpu.VMEM((h1, years_dev) + block, LINK),
        pltpu.VMEM((rows, gen_rows, LANES), f32), pltpu.VMEM((rows, store_rows, LANES), f32),
        pltpu.VMEM((rows, store_rows, LANES), f32),
        pltpu.VMEM((gen_rows + 2 * store_rows, LANES, LANES), jnp.bfloat16),
        pltpu.VMEM((gen_rows + 2 * store_rows, hi_count, LANES), jnp.bfloat16),
        pltpu.VMEM((rows * SPLITS * hi_count, LANES), f32),
        pltpu.VMEM((sent_rows, LANES), f32),
        pltpu.VMEM((2 * rows + 1,) + block, f32), pltpu.VMEM((2 * rows + 1,) + block, f32),
        pltpu.VMEM(block, jnp.int32), pltpu.VMEM((rows,) + block, f32), pltpu.VMEM((h1, years_dev) + block, LINK),
        pltpu.VMEM((rows, 8, LANES), f32), pltpu.VMEM((rows, 8, LANES), f32),
        dma((3,)), dma, dma((12,)), pltpu.SemaphoreType.REGULAR, pltpu.SemaphoreType.REGULAR,
    ]
    results = pl.pallas_call(
        functools.partial(step_kernel, sizes),
        out_shape=[pltpu.VMEM(s, f32) for s in out_shapes] + [pltpu.VMEM((1, rows), f32)],
        in_specs=[any_spec] * 17,
        out_specs=[pl.BlockSpec(memory_space=pltpu.VMEM)] * 7,
        scratch_shapes=scratch,
        compiler_params=pltpu.CompilerParams(
            collective_id=0, has_side_effects=True, vmem_limit_bytes=56 * 1024 * 1024
        ),
    )(*args)
    gen, store, cap, flow, upper, lower, balance = pl.pallas_call(
        functools.partial(finish_kernel, len(results)),
        out_shape=[jax.ShapeDtypeStruct(x.shape, f32) for x in results],
        in_specs=[pl.BlockSpec(memory_space=pltpu.VMEM)] * len(results),
        out_specs=[any_spec] * len(results),
        scratch_shapes=[dma],
    )(*[pltpu.with_memory_space_constraint(x, pltpu.VMEM) for x in results])
    return (
        gen.reshape(gen_state.shape), store.reshape(store_state.shape), cap.reshape(capacity.shape),
        balance.reshape(balance_dual.shape), flow.reshape(flow_dual.shape),
        upper.reshape(level_upper.shape), lower.reshape(level_lower.shape),
    )


def solution(mesh):
    row = P(("groups", "years"), "hours", "lines")
    line = P("lines")
    in_specs = (
        P(("groups", "years"), "hours", None), row, P("lines", None), line, line, line, line, line,
        line, line, row, row, row, row, row, P(("groups", "years"), "hours"), P(("groups", "lines")),
    )
    out_specs = (row, row, P(("groups", "lines")), P(("groups", "years"), "hours"), row, row, row)
    step = jax.shard_map(functools.partial(local, mesh), mesh=mesh, in_specs=in_specs, out_specs=out_specs, check_vma=False)

    def run(*args):
        with jax.sharding.use_abstract_mesh(mesh.abstract_mesh):
            return step(*args)

    return run
```

```python
import functools
import math

import jax
import jax.numpy as jnp
from jax import lax
from jax.experimental import pallas as pl
from jax.experimental.pallas import tpu as pltpu
from jax.sharding import PartitionSpec as P

TAU = 0.1
SIGMA = 0.5
TAU_CAP = 1.0
LANES = 128
SPLITS = 2
TILE = 256
THIN = 4
LINK = jnp.bfloat16
MESH = pl.DeviceIdType.MESH


def step_kernel(
    sizes,
    demand_h, avail_h, ptdf_h, limit_h, cost_h, cap_h, gnode_h, snode_h, power_h,
    capex_h, gen_h, store_h, upper_h, lower_h, flow_h, capacity_h, balance_h,
    gen_w, store_w, capacity_w, flow_w, upper_w, lower_w, balance_o,
    demand_v, avail_v, ptdf_v, limit_v, cost_v, cap_v, gnode_v, snode_v, power_v,
    capex_v, gen_v, store_v, upper_v, lower_v, flow_v, capacity_v, balance_v,
    flow8, limit1, net_s, net_r, inj_s, inj_r, inj8, line8, avail_d, demand_d,
    dual_s, dual_r, total_v, cross_r, above_s, above_r, up_s, up_r, bar_s, bar_r,
    gbar_v, sbar_v, price_v, onehot, highhot, placed_v, sent,
    mate_s, mate_v, mate_node, mate_bar, mate_sum, mate_r, bal_s, bal_r,
    in_sem, send_sem, recv_sem, year_ready, hour_ready,
):
    years_dev, hours_dev, hours, years, level_scale, node_scale, hour_count = sizes
    rows = years_dev * hours_dev
    me_h, me_y, me_l = lax.axis_index("hours"), lax.axis_index("years"), lax.axis_index("lines")
    hi_count, line_local = ptdf_v.shape[0], ptdf_v.shape[1]
    padded = flow8.shape[0]
    gen_rows, store_rows = gnode_v.shape[0], snode_v.shape[0]
    link = dual_s.dtype
    block_rows = store_rows * link.itemsize // 4
    base_rows = 2 * rows * hi_count + 8 * rows + (hours - 1 + years - 1) * block_rows

    order = (
        (upper_h, upper_v, 0), (lower_h, lower_v, 0), (flow_h, flow_v, 1),
    ) + tuple((ptdf_h.at[:, pl.ds(j * LANES, LANES)], ptdf_v.at[j], 1) for j in range(hi_count)) + (
        (snode_h, snode_v, 1), (gnode_h, gnode_v, 1), (store_h, store_v, 1), (power_h, power_v, 1),
        (gen_h, gen_v, 1), (cost_h, cost_v, 1), (cap_h, cap_v, 1), (avail_h, avail_v, 1),
        (demand_h, demand_v, 1), (limit_h, limit_v, 1), (capex_h, capex_v, 1), (capacity_h, capacity_v, 1),
        (balance_h, balance_v, 1),
    )
    loads = [pltpu.make_async_copy(s, d, in_sem.at[i]) for s, d, i in order]
    for copy in loads:
        copy.start()

    def wide(ref, first, count):
        return jnp.concatenate([ref[first + i] for i in range(count)], axis=1)

    def multiply(jobs, transpose):
        stage = [0, 0]
        for unit, acc, left, right in jobs:
            pltpu.matmul_push_rhs(right, stage[unit], unit, transpose=transpose)
            pltpu.matmul_acc_lhs(acc, left, load_staged_rhs=stage[unit])
            stage[unit] = 1 - stage[unit]

    def tile(i, rows_from):
        rows_here = pl.ds(rows_from * TILE, TILE)
        return jnp.concatenate([ptdf_v[2 * i, rows_here], ptdf_v[2 * i + 1, rows_here]], axis=1)

    def scoped(height, count, body):
        specs = [pltpu.ACC(mxu_id=i)((height, TILE), jnp.float32) for i in range(2) for _ in range(count)]
        pl.run_scoped(lambda *accs: body((accs[:count], accs[count:])), *specs)

    def cols(i):
        return slice(i * TILE, (i + 1) * TILE)

    node_tiles, line_tiles = hi_count * LANES // TILE, line_local // TILE

    def peer(k, j):
        return {"hours": lax.rem(me_h + k, hours), "years": lax.rem(me_y + j, years)}

    partner = {"lines": 1 - me_l}
    barrier = pltpu.get_barrier_semaphore()

    def ready(device):
        pl.semaphore_signal(barrier, inc=1, device_id=device, device_id_type=MESH)

    dual_r[...] = jnp.zeros_like(dual_r)
    bar_r[...] = jnp.zeros_like(bar_r)
    up_r[...] = jnp.zeros_like(up_r)
    cross_r[...] = jnp.zeros_like(cross_r)
    mate_r[...] = jnp.zeros_like(mate_r)
    above_r[...] = jnp.zeros_like(above_r)
    ready(partner)
    for k in range(1, hours):
        @pl.when(me_h + k < hours)
        def _(k=k):
            ready(peer(k, 0))
        @pl.when(jnp.logical_and(me_h + k < hours, me_l == 1))
        def _(k=k):
            ready({**peer(k, 0), **partner})
    for j in range(1, years):
        @pl.when(me_y + j < years)
        def _(j=j):
            ready(peer(0, j))
            for k in range(1, hours):
                @pl.when(me_h + k < hours)
                def _(k=k):
                    ready(peer(k, j))

    pl.semaphore_wait(barrier, 1 + me_y + me_h * (2 + me_y - me_l))
    for j in range(1, years):
        @pl.when(me_y + j >= years)
        def _(j=j):
            pl.semaphore_signal(year_ready, inc=1, device_id=peer(0, j), device_id_type=MESH)
    for k in range(hours - 1, 0, -1):
        @pl.when(me_h >= k)
        def _(k=k):
            pl.semaphore_signal(hour_ready, inc=1, device_id=peer(hours - k, 0), device_id_type=MESH)

    loads[0].wait()
    loads[1].wait()
    local_upper = None
    for y in range(years_dev):
        total = None
        for h in range(hours_dev):
            r = y * hours_dev + h
            diff = upper_v[r] - lower_v[r]
            total = diff if total is None else total + diff
            local_upper = upper_v[r] if local_upper is None else local_upper + upper_v[r]
        dual_s[y] = total.astype(link)
    dual_s[years_dev] = local_upper.astype(link)
    total_v[...] = local_upper

    def remote(src, dst, sem, device):
        return pltpu.make_async_remote_copy(
            src_ref=src, dst_ref=dst, send_sem=send_sem, recv_sem=recv_sem.at[sem],
            device_id=device, device_id_type=MESH,
        )

    def arrive(ref, sem):
        pltpu.make_async_copy(ref, ref, sem).wait()

    def dual_copy(k):
        return remote(dual_s, dual_r.at[k - 1], 2, peer(hours - k, 0))

    def bar_copy(k):
        return remote(bar_s, bar_r.at[k - 1], 3, peer(k, 0))

    def mate_bar_copy(k):
        return remote(mate_sum, bar_r.at[k - 1], 3, {**peer(k, 0), **partner})

    def mate_dual_copy(k):
        return remote(dual_s.at[pl.ds(0, years_dev)], mate_r.at[k - 1], 6, {**peer(hours - k, 0), **partner})

    node_copy = remote(snode_v, mate_node, 4, partner)
    mate_copy = remote(mate_s, mate_v, 4, partner)
    bal_copy = remote(bal_s, bal_r, 7, partner)

    def up_copy(k):
        return remote(up_s, up_r.at[k - 1], 3, peer(k, 0))

    def cross_copy(k, j):
        slot = cross_r.at[k, j - 1]
        return remote(dual_s.at[years_dev], slot, 3 if k else 5, peer(hours - k, years - j))

    def above_copy(j):
        return remote(above_s, above_r.at[j - 1], 3, peer(0, j))

    net_copy = remote(net_s, net_r, 0, partner)
    inj_copy = remote(inj_s, inj_r, 1, partner)

    for j in range(1, years):
        for k in range(hours - 1, 0, -1):
            @pl.when(jnp.logical_and(me_h >= k, me_y >= j))
            def _(k=k, j=j):
                cross_copy(k, j).start()
    for k in range(hours - 1, 0, -1):
        @pl.when(me_h >= k)
        def _(k=k):
            dual_copy(k).start()

        @pl.when(jnp.logical_and(me_h >= k, me_l == 0))
        def _(k=k):
            mate_dual_copy(k).start()
    for j in range(1, years):
        @pl.when(me_y >= j)
        def _(j=j):
            cross_copy(0, j).start()

    for copy in loads[2:]:
        copy.wait()
    flow8[...] = jnp.zeros_like(flow8)
    for r in range(rows):
        flow8[r : r + 1, :] = flow_v[r]
    dual_half = flow8[...].astype(jnp.bfloat16)
    for first in range(0, node_tiles, 2 * THIN):
        def nodes_group(accs, first=first):
            group = range(first, min(first + 2 * THIN, node_tiles))
            jobs = [
                (n % 2, accs[n % 2][(n - first) // 2], dual_half[:, cols(k)], tile(n, k))
                for base in group[::2] for k in range(line_tiles) for n in (base, base + 1) if n in group
            ]
            multiply(jobs, False)
            for n in group:
                net_s[:, cols(n)] = pltpu.matmul_pop(accs[n % 2][(n - first) // 2])[:rows]

        scoped(padded, THIN, nodes_group)
    net_copy.start()

    @pl.when(me_y < years - 1)
    def _():
        pl.semaphore_wait(year_ready, years - 1 - me_y)

    for j in range(1, years):
        @pl.when(me_y + j < years)
        def _(j=j):
            cross_copy(0, years - j).start()

    @pl.when(me_l == 0)
    def _():
        node_copy.start()
    high_rows = lax.broadcasted_iota(jnp.int32, (hi_count, LANES), 0)
    lane_rows = lax.broadcasted_iota(jnp.int32, (LANES, LANES), 0)

    def encode(ref, first, count):
        for a in range(count):
            row = ref[a : a + 1, :]
            low = jnp.broadcast_to(row % LANES, (LANES, LANES))
            onehot[first + a] = jnp.where(low == lane_rows, 1.0, 0.0).astype(jnp.bfloat16)
            high = jnp.broadcast_to(row // LANES, (hi_count, LANES))
            highhot[first + a] = jnp.where(high == high_rows, 1.0, 0.0).astype(jnp.bfloat16)

    encode(snode_v, 0, store_rows)
    encode(gnode_v, store_rows, gen_rows)
    for r in range(rows):
        for j in range(hi_count):
            piece = slice(j * LANES, (j + 1) * LANES)
            demand_d[r, j : j + 1, :] = demand_v[r : r + 1, piece].astype(jnp.float32)
        for j in range(gen_rows):
            piece = slice(j * LANES, (j + 1) * LANES)
            avail_d[r, j : j + 1, :] = avail_v[r : r + 1, piece].astype(jnp.float32)

    net_copy.wait_recv()
    prices = net_s[...] + net_r[...]

    def gather(r, node):
        price_row = prices[r : r + 1] + node_scale * balance_v[:, r : r + 1]
        high, low = node // LANES, node % LANES
        result = jnp.zeros(node.shape, jnp.float32)
        for j in range(hi_count):
            table = jnp.broadcast_to(price_row[:, j * LANES : (j + 1) * LANES], node.shape)
            picked = jnp.take_along_axis(table, low, axis=1, mode="promise_in_bounds")
            result = jnp.where(high == j, picked, result)
        return result

    for r in range(rows):
        for b in range(0, store_rows, 8):
            price_v[r, b : b + 8] = gather(r, snode_v[b : b + 8])

    @pl.when(me_l == 0)
    def _():
        mate_s[2 * rows] = power_v[...]
        for y in range(years_dev):
            own = None
            for h in reversed(range(hours_dev)):
                r = y * hours_dev + h
                diff = upper_v[r] - lower_v[r]
                own = diff if own is None else own + diff
                mate_s[r] = store_v[r] - TAU * (level_scale * own - price_v[r])
                mate_s[rows + r] = store_v[r]
        mate_copy.start()

    for r in range(rows):
        for b in range(0, gen_rows, 8):
            part = slice(b, b + 8)
            price = gather(r, gnode_v[part])
            new = gen_v[r, part] - TAU * (cost_v[part] + price)
            new = jnp.minimum(jnp.maximum(new, 0.0), cap_v[part] * avail_d[r, part])
            gen_w[r, part] = new
            gbar_v[r, part] = 2.0 * new - gen_v[r, part]

    def place(values, sign, first, count, start, target):
        pieces = []
        for r in range(rows):
            rest = sign * values[r]
            for _ in range(SPLITS):
                piece = rest.astype(jnp.bfloat16).astype(jnp.float32)
                rest = rest - piece
                pieces.append(piece)

        def spread(a):
            return jnp.concatenate([
                jnp.broadcast_to(piece[a : a + 1], (hi_count, LANES)).astype(jnp.bfloat16) * highhot[first + a]
                for piece in pieces
            ], axis=0)

        def pair(make, a):
            return jnp.concatenate([make(a), make(a + 1)], axis=1)

        jobs = []
        for t in range(count // 4):
            left = jnp.concatenate([pair(spread, 4 * t), pair(spread, 4 * t + 2)], axis=0)
            right = jnp.concatenate([wide(onehot, first + 4 * t, 2), wide(onehot, first + 4 * t + 2, 2)], axis=0)
            jobs.append((t % 2, left, right))
        height = rows * SPLITS * hi_count

        def finish(accs):
            multiply([(i, accs[i][0], left, right) for i, left, right in jobs], True)
            for i in range(2):
                both = pltpu.matmul_pop(accs[i][0])
                part = both[:height, :LANES] + both[height:, LANES:]
                target[...] = part + (start if i == 0 else target[...])

        scoped(2 * height, 1, finish)

    place(gbar_v, 1.0, store_rows, gen_rows, 0.0, placed_v)

    def inject_part(r):
        total = None
        for p in range(SPLITS):
            base = (r * SPLITS + p) * hi_count
            piece = placed_v[base : base + hi_count]
            total = piece if total is None else total + piece
        return total

    @pl.when(me_l == 0)
    def _():
        for r in range(rows):
            inj_s[r] = inject_part(r)
        inj_copy.start()

    @pl.when(me_l == 1)
    def _():
        arrive(sent.at[pl.ds(0, (2 * rows + 2) * store_rows)], recv_sem.at[4])
        encode(mate_node, store_rows + gen_rows, store_rows)

    arrive(cross_r.at[0], recv_sem.at[5])
    hour_upper = total_v[...]
    for j in range(1, years):
        hour_upper = hour_upper + cross_r[0, j - 1].astype(jnp.float32)
    total_v[...] = hour_upper
    up_s[...] = hour_upper.astype(link)

    @pl.when(me_h < hours - 1)
    def _():
        pl.semaphore_wait(hour_ready, hours - 1 - me_h)
        for k in range(hours - 1, 0, -1):
            @pl.when(me_h + k < hours)
            def _(k=k):
                up_copy(k).start()

    for count in range(1, hours):
        @pl.when(me_h + count == hours - 1)
        def _(count=count):
            arrive(dual_r.at[pl.ds(0, count)], recv_sem.at[2])
    above = dual_r[0, years_dev].astype(jnp.float32)
    for k in range(2, hours):
        above = above + dual_r[k - 1, years_dev].astype(jnp.float32)
    above_s[...] = above.astype(link)
    for y in range(years_dev):
        beyond = dual_r[0, y].astype(jnp.float32)
        for k in range(2, hours):
            beyond = beyond + dual_r[k - 1, y].astype(jnp.float32)
        bar_total = None
        for h in reversed(range(hours_dev)):
            r = y * hours_dev + h
            beyond = beyond + (upper_v[r] - lower_v[r])
            suffix = level_scale * beyond
            power = power_v[...]
            new = store_v[r] - TAU * (suffix - price_v[r])
            new = jnp.minimum(jnp.maximum(new, -power), power)
            store_w[r] = new
            sbar = 2.0 * new - store_v[r]
            sbar_v[r] = sbar
            bar_total = sbar if bar_total is None else bar_total + sbar
        bar_s[y] = bar_total.astype(link)
    for k in range(hours - 1, 0, -1):
        @pl.when(jnp.logical_or(me_h + k == hours - 1, jnp.logical_and(me_h + k < hours, me_l == 1)))
        def _(k=k):
            bar_copy(k).start()
    for j in range(1, years):
        @pl.when(jnp.logical_and(me_h < hours - 1, me_y + j < years))
        def _(j=j):
            above_copy(j).start()
    total_v[...] = total_v[...] + above
    place(sbar_v, -1.0, 0, store_rows, placed_v[...], placed_v)

    @pl.when(me_l == 1)
    def _():
        for r in range(rows):
            inj_s[r] = inject_part(r)
        inj_copy.start()

    for r in range(rows):
        part = None
        for b in range(0, gen_rows, 8):
            part = gbar_v[r, b : b + 8] if part is None else part + gbar_v[r, b : b + 8]
        for b in range(0, store_rows, 8):
            part = part - sbar_v[r, b : b + 8]
        bal_s[r] = part
    bal_copy.start()

    for c in range(line_local // LANES):
        limit1[:, c * LANES : (c + 1) * LANES] = limit_v[c : c + 1, :]
    inj8[...] = jnp.zeros_like(inj8)

    @pl.when(me_l == 1)
    def _():
        for count in range(1, hours):
            @pl.when(me_h + count == hours - 1)
            def _(count=count):
                arrive(mate_r.at[pl.ds(0, count)], recv_sem.at[6])
        power = mate_v[2 * rows]
        for y in range(years_dev):
            beyond = mate_r[0, y].astype(jnp.float32)
            for k in range(2, hours):
                beyond = beyond + mate_r[k - 1, y].astype(jnp.float32)
            bar_total = None
            for h in range(hours_dev):
                r = y * hours_dev + h
                new = mate_v[r] - TAU * level_scale * beyond
                new = jnp.minimum(jnp.maximum(new, -power), power)
                sbar = 2.0 * new - mate_v[rows + r]
                mate_bar[r] = sbar
                bar_total = sbar if bar_total is None else bar_total + sbar
            mate_sum[y] = bar_total.astype(link)
        for k in range(hours - 2, 0, -1):
            @pl.when(me_h + k < hours - 1)
            def _(k=k):
                mate_bar_copy(k).start()
        place(mate_bar, -1.0, store_rows + gen_rows, store_rows, placed_v[...], placed_v)

    inj_copy.wait_recv()
    for r in range(rows):
        inject = inject_part(r) + inj_r[r] - demand_d[r]
        for j in range(hi_count):
            inj8[r : r + 1, j * LANES : (j + 1) * LANES] = inject[j : j + 1]
    inject_half = inj8[...].astype(jnp.bfloat16)
    for first in range(0, line_tiles, THIN):
        def lines_group(accs, first=first):
            group = range(first, min(first + THIN, line_tiles))
            multiply([
                (k % 2, accs[k % 2][n - first], inject_half[:, cols(k)], tile(k, n))
                for n in group for k in range(node_tiles)
            ], True)
            for i, n in enumerate(group):
                line8[:, cols(n)] = pltpu.matmul_pop(accs[0][i]) + pltpu.matmul_pop(accs[1][i])

        scoped(padded, THIN, lines_group)
    line_flows = line8[...]
    shifted = flow8[...] + SIGMA * line_flows
    limit = limit1[...]
    line_next = shifted - SIGMA * jnp.minimum(jnp.maximum(shifted * (1.0 / SIGMA), -limit), limit)
    for r in range(rows):
        flow_w[r] = line_next[r : r + 1]

    for y in range(years):
        for h in range(hours):
            late = h * (years_dev + 1) + (hours - 1 - h) * (years - 1 - y) + (y if h < hours - 1 else 0)
            if late:
                @pl.when(jnp.logical_and(me_h == h, me_y == y))
                def _(size=late * block_rows):
                    arrive(sent.at[pl.ds(0, size)], recv_sem.at[3])
    bal_copy.wait_recv()
    for r in range(rows):
        part = bal_s[r] + bal_r[r]
        for b in range(0, hi_count, 8):
            part = part - demand_d[r, b : b + 8]
        balance_o[:, r : r + 1] = balance_v[:, r : r + 1] + SIGMA * node_scale * jnp.sum(part, keepdims=True)

    upper_total = total_v[...]
    for k in range(1, hours):
        upper_total = upper_total + up_r[k - 1].astype(jnp.float32)
        for j in range(1, years):
            upper_total = upper_total + cross_r[k, j - 1].astype(jnp.float32)
    for j in range(1, years):
        upper_total = upper_total + above_r[j - 1].astype(jnp.float32)
    capacity_next = jnp.maximum(capacity_v[...] - TAU_CAP * (capex_v[...] - upper_total / hour_count), 0.0)
    capacity_w[...] = capacity_next
    capacity_bar = 2.0 * capacity_next - capacity_v[...]

    for y in range(years_dev):
        before = bar_r[0, y].astype(jnp.float32)
        for k in range(2, hours):
            before = before + bar_r[k - 1, y].astype(jnp.float32)
        for h in range(hours_dev):
            r = y * hours_dev + h
            before = before + sbar_v[r]
            level = level_scale * before
            upper_w[r] = jnp.maximum(upper_v[r] + SIGMA * (level - capacity_bar), 0.0)
            lower_w[r] = jnp.maximum(lower_v[r] - SIGMA * level, 0.0)

    for y in range(years):
        for h in range(hours):
            blocks = h * years_dev + h * y + (years - 1 - y if h < hours - 1 else 0)
            near = years_dev * (h + (1 if h < hours - 1 else 0))
            far = years_dev * (hours - 1 - h + max(hours - 2 - h, 0))
            extra = (2 * rows + 2) * store_rows

            @pl.when(jnp.logical_and(jnp.logical_and(me_h == h, me_y == y), me_l == 0))
            def _(size=base_rows + (blocks + near) * block_rows + extra):
                arrive(sent.at[pl.ds(0, size)], send_sem)

            @pl.when(jnp.logical_and(jnp.logical_and(me_h == h, me_y == y), me_l == 1))
            def _(size=base_rows + (blocks + far) * block_rows):
                arrive(sent.at[pl.ds(0, size)], send_sem)


def finish_kernel(count, *refs):
    sources, targets, sem = refs[:count], refs[count : 2 * count], refs[2 * count]
    copies = [pltpu.make_async_copy(s, t, sem) for s, t in zip(sources, targets)]
    for copy in copies:
        copy.start()
    for copy in copies:
        copy.wait()


def local(
    mesh,
    demand, avail, ptdf, line_limit, gen_cost, gen_cap, gen_node, store_node, store_power,
    capex, gen_state, store_state, level_upper, level_lower, flow_dual, balance_dual, capacity,
):
    years_dev, hours_dev, nodes = demand.shape
    rows = years_dev * hours_dev
    hours, years = lax.axis_size("hours"), lax.axis_size("years")
    hours_total = hours_dev * hours
    hour_count = years_dev * years * hours_total
    level_scale = 1.0 / math.sqrt(hours_total)
    node_scale = 1.0 / math.sqrt(nodes)
    sizes = (years_dev, hours_dev, hours, years, level_scale, node_scale, hour_count)

    def fold(x):
        return x.reshape(-1, LANES)

    def fold_rows(x):
        return x.reshape(rows, -1, LANES)

    args = (
        demand.reshape(rows, nodes), avail.reshape(rows, -1), ptdf, fold(line_limit), fold(gen_cost),
        fold(gen_cap), fold(gen_node), fold(store_node), fold(store_power), fold(capex),
        fold_rows(gen_state), fold_rows(store_state), fold_rows(level_upper), fold_rows(level_lower),
        flow_dual.reshape(rows, 1, -1), fold(capacity), balance_dual.reshape(1, rows),
    )
    f32 = jnp.float32
    gen_rows, store_rows = args[6].shape[0], args[7].shape[0]
    line_local, hi_count = ptdf.shape[0], nodes // LANES
    padded = max(16, -(-rows // 16) * 16)
    out_shapes = [
        (rows, gen_rows, LANES), (rows, store_rows, LANES), (store_rows, LANES),
        (rows, 1, line_local), (rows, store_rows, LANES), (rows, store_rows, LANES),
    ]
    any_spec = pl.BlockSpec(memory_space=pl.ANY)
    block, blocks = (store_rows, LANES), (years_dev + 1, store_rows, LANES)
    h1, y1 = max(hours - 1, 1), max(years - 1, 1)
    dma = pltpu.SemaphoreType.DMA
    block_rows = store_rows * jnp.dtype(LINK).itemsize // 4
    sent_rows = 2 * rows * hi_count + 8 * rows + (2 * rows + 2) * store_rows + 2 * hours * years_dev * block_rows + (hours - 1) * (years_dev + 1) * block_rows + (hours + 1) * years * block_rows
    scratch = [pltpu.VMEM(a.shape, a.dtype) for a in args]
    scratch[2] = pltpu.VMEM((hi_count, line_local, LANES), ptdf.dtype)
    scratch += [
        pltpu.VMEM((padded, line_local), f32), pltpu.VMEM((1, line_local), f32),
        pltpu.VMEM((rows, nodes), f32), pltpu.VMEM((rows, nodes), f32),
        pltpu.VMEM((rows, hi_count, LANES), f32), pltpu.VMEM((rows, hi_count, LANES), f32),
        pltpu.VMEM((padded, nodes), f32), pltpu.VMEM((padded, line_local), f32),
        pltpu.VMEM((rows, gen_rows, LANES), f32),
        pltpu.VMEM((rows, hi_count, LANES), f32),
        pltpu.VMEM(blocks, LINK), pltpu.VMEM((h1,) + blocks, LINK),
        pltpu.VMEM(block, f32), pltpu.VMEM((hours, y1) + block, LINK),
        pltpu.VMEM(block, LINK), pltpu.VMEM((y1,) + block, LINK),
        pltpu.VMEM(block, LINK), pltpu.VMEM((h1,) + block, LINK),
        pltpu.VMEM((years_dev,) + block, LINK), pltpu.VMEM((h1, years_dev) + block, LINK),
        pltpu.VMEM((rows, gen_rows, LANES), f32), pltpu.VMEM((rows, store_rows, LANES), f32),
        pltpu.VMEM((rows, store_rows, LANES), f32),
        pltpu.VMEM((gen_rows + 2 * store_rows, LANES, LANES), jnp.bfloat16),
        pltpu.VMEM((gen_rows + 2 * store_rows, hi_count, LANES), jnp.bfloat16),
        pltpu.VMEM((rows * SPLITS * hi_count, LANES), f32),
        pltpu.VMEM((sent_rows, LANES), f32),
        pltpu.VMEM((2 * rows + 1,) + block, f32), pltpu.VMEM((2 * rows + 1,) + block, f32),
        pltpu.VMEM(block, jnp.int32), pltpu.VMEM((rows,) + block, f32), pltpu.VMEM((years_dev,) + block, LINK),
        pltpu.VMEM((h1, years_dev) + block, LINK),
        pltpu.VMEM((rows, 8, LANES), f32), pltpu.VMEM((rows, 8, LANES), f32),
        dma((2,)), dma, dma((8,)), pltpu.SemaphoreType.REGULAR, pltpu.SemaphoreType.REGULAR,
    ]
    results = pl.pallas_call(
        functools.partial(step_kernel, sizes),
        out_shape=[pltpu.VMEM(s, f32) for s in out_shapes] + [pltpu.VMEM((1, rows), f32)],
        in_specs=[any_spec] * 17,
        out_specs=[pl.BlockSpec(memory_space=pltpu.VMEM)] * 7,
        scratch_shapes=scratch,
        compiler_params=pltpu.CompilerParams(
            collective_id=0, has_side_effects=True, vmem_limit_bytes=56 * 1024 * 1024
        ),
    )(*args)
    gen, store, cap, flow, upper, lower, balance = pl.pallas_call(
        functools.partial(finish_kernel, len(results)),
        out_shape=[jax.ShapeDtypeStruct(x.shape, f32) for x in results],
        in_specs=[pl.BlockSpec(memory_space=pltpu.VMEM)] * len(results),
        out_specs=[any_spec] * len(results),
        scratch_shapes=[dma],
    )(*[pltpu.with_memory_space_constraint(x, pltpu.VMEM) for x in results])
    return (
        gen.reshape(gen_state.shape), store.reshape(store_state.shape), cap.reshape(capacity.shape),
        balance.reshape(balance_dual.shape), flow.reshape(flow_dual.shape),
        upper.reshape(level_upper.shape), lower.reshape(level_lower.shape),
    )


def solution(mesh):
    row = P(("groups", "years"), "hours", "lines")
    line = P("lines")
    in_specs = (
        P(("groups", "years"), "hours", None), row, P("lines", None), line, line, line, line, line,
        line, line, row, row, row, row, row, P(("groups", "years"), "hours"), P(("groups", "lines")),
    )
    out_specs = (row, row, P(("groups", "lines")), P(("groups", "years"), "hours"), row, row, row)
    step = jax.shard_map(functools.partial(local, mesh), mesh=mesh, in_specs=in_specs, out_specs=out_specs, check_vma=False)

    def run(*args):
        with jax.sharding.use_abstract_mesh(mesh.abstract_mesh):
            return step(*args)

    return run
```

```python
import functools
import math

import jax
import jax.numpy as jnp
from jax import lax
from jax.experimental import pallas as pl
from jax.experimental.pallas import tpu as pltpu
from jax.sharding import PartitionSpec as P

TAU = 0.1
SIGMA = 0.5
TAU_CAP = 1.0
LANES = 128
SPLITS = 2
TILE = 256
THIN = 4
DEPTH = 1
LINK = jnp.bfloat16
MESH = pl.DeviceIdType.MESH


def step_kernel(
    sizes,
    demand_h, avail_h, ptdf_h, limit_h, cost_h, cap_h, gnode_h, snode_h, power_h,
    capex_h, gen_h, store_h, upper_h, lower_h, flow_h, capacity_h, balance_h,
    gen_w, store_w, capacity_w, flow_w, upper_w, lower_w, balance_o,
    demand_v, avail_v, ptdf_v, limit_v, cost_v, cap_v, gnode_v, snode_v, power_v,
    capex_v, gen_v, store_v, upper_v, lower_v, flow_v, capacity_v, balance_v,
    flow8, limit1, net_s, net_r, inj_s, inj_r, inj8, line8, avail_d, demand_d,
    dual_s, dual_r, total_v, cross_r, above_s, above_r, up_s, up_r, bar_s, bar_r,
    gbar_v, sbar_v, price_v, onehot, highhot, placed_v, sent,
    mate_s, mate_v, mate_node, mate_bar, mate_sum, mate_r, bal_s, bal_r, ptdf_t,
    in_sem, send_sem, recv_sem, year_ready, hour_ready,
):
    years_dev, hours_dev, hours, years, level_scale, node_scale, hour_count = sizes
    rows = years_dev * hours_dev
    me_h, me_y, me_l = lax.axis_index("hours"), lax.axis_index("years"), lax.axis_index("lines")
    hi_count, line_local = ptdf_v.shape[0], ptdf_v.shape[1]
    padded = flow8.shape[0]
    gen_rows, store_rows = gnode_v.shape[0], snode_v.shape[0]
    link = dual_s.dtype
    block_rows = store_rows * link.itemsize // 4
    base_rows = 2 * rows * hi_count + 8 * rows + (hours - 1 + years - 1) * block_rows

    order = (
        (upper_h, upper_v, 0), (lower_h, lower_v, 0), (flow_h, flow_v, 1),
    ) + tuple((ptdf_h.at[:, pl.ds(j * LANES, LANES)], ptdf_v.at[j], 1) for j in range(hi_count)) + (
        (snode_h, snode_v, 1), (gnode_h, gnode_v, 1), (store_h, store_v, 1), (power_h, power_v, 1),
        (gen_h, gen_v, 1), (cost_h, cost_v, 1), (cap_h, cap_v, 1), (avail_h, avail_v, 1),
        (demand_h, demand_v, 1), (limit_h, limit_v, 1), (capex_h, capex_v, 1), (capacity_h, capacity_v, 1),
        (balance_h, balance_v, 1),
    )
    loads = [pltpu.make_async_copy(s, d, in_sem.at[i]) for s, d, i in order]
    for copy in loads:
        copy.start()

    def wide(ref, first, count):
        return jnp.concatenate([ref[first + i] for i in range(count)], axis=1)

    def multiply(jobs, transpose):
        stage = [0, 0]
        for unit, acc, left, right in jobs:
            pltpu.matmul_push_rhs(right, stage[unit], unit, transpose=transpose)
            pltpu.matmul_acc_lhs(acc, left, load_staged_rhs=stage[unit])
            stage[unit] = 1 - stage[unit]

    def tile(i, rows_from):
        rows_here = pl.ds(rows_from * TILE, TILE)
        return jnp.concatenate([ptdf_v[2 * i, rows_here], ptdf_v[2 * i + 1, rows_here]], axis=1)

    def scoped(height, count, body):
        specs = [pltpu.ACC(mxu_id=i)((height, TILE), jnp.float32) for i in range(2) for _ in range(count)]
        pl.run_scoped(lambda *accs: body((accs[:count], accs[count:])), *specs)

    def cols(i):
        return slice(i * TILE, (i + 1) * TILE)

    node_tiles, line_tiles = hi_count * LANES // TILE, line_local // TILE

    def peer(k, j):
        return {"hours": lax.rem(me_h + k, hours), "years": lax.rem(me_y + j, years)}

    partner = {"lines": 1 - me_l}
    barrier = pltpu.get_barrier_semaphore()

    def ready(device):
        pl.semaphore_signal(barrier, inc=1, device_id=device, device_id_type=MESH)

    dual_r[...] = jnp.zeros_like(dual_r)
    bar_r[...] = jnp.zeros_like(bar_r)
    up_r[...] = jnp.zeros_like(up_r)
    cross_r[...] = jnp.zeros_like(cross_r)
    mate_r[...] = jnp.zeros_like(mate_r)
    above_r[...] = jnp.zeros_like(above_r)
    ready(partner)
    for k in range(1, hours):
        @pl.when(me_h + k < hours)
        def _(k=k):
            ready(peer(k, 0))
        @pl.when(jnp.logical_and(me_h + k < hours, me_l == 1))
        def _(k=k):
            ready({**peer(k, 0), **partner})
    for j in range(1, years):
        @pl.when(me_y + j < years)
        def _(j=j):
            ready(peer(0, j))
            for k in range(1, hours):
                @pl.when(me_h + k < hours)
                def _(k=k):
                    ready(peer(k, j))

    pl.semaphore_wait(barrier, 1 + me_y + me_h * (2 + me_y - me_l))
    for j in range(1, years):
        @pl.when(me_y + j >= years)
        def _(j=j):
            pl.semaphore_signal(year_ready, inc=1, device_id=peer(0, j), device_id_type=MESH)
    for k in range(hours - 1, 0, -1):
        @pl.when(me_h >= k)
        def _(k=k):
            pl.semaphore_signal(hour_ready, inc=1, device_id=peer(hours - k, 0), device_id_type=MESH)

    loads[0].wait()
    loads[1].wait()
    local_upper = None
    for y in range(years_dev):
        total = None
        for h in range(hours_dev):
            r = y * hours_dev + h
            diff = upper_v[r] - lower_v[r]
            total = diff if total is None else total + diff
            local_upper = upper_v[r] if local_upper is None else local_upper + upper_v[r]
        dual_s[y] = total.astype(link)
    dual_s[years_dev] = local_upper.astype(link)
    total_v[...] = local_upper

    def remote(src, dst, sem, device):
        return pltpu.make_async_remote_copy(
            src_ref=src, dst_ref=dst, send_sem=send_sem, recv_sem=recv_sem.at[sem],
            device_id=device, device_id_type=MESH,
        )

    def arrive(ref, sem):
        pltpu.make_async_copy(ref, ref, sem).wait()

    def dual_copy(k):
        return remote(dual_s, dual_r.at[k - 1], 2, peer(hours - k, 0))

    def bar_copy(k):
        return remote(bar_s, bar_r.at[k - 1], 3, peer(k, 0))

    def mate_bar_copy(k):
        return remote(mate_sum, bar_r.at[k - 1], 3, {**peer(k, 0), **partner})

    def mate_dual_copy(k):
        return remote(dual_s.at[pl.ds(0, years_dev)], mate_r.at[k - 1], 6, {**peer(hours - k, 0), **partner})

    node_copy = remote(snode_v, mate_node, 4, partner)
    mate_copy = remote(mate_s, mate_v, 4, partner)
    bal_copy = remote(bal_s, bal_r, 7, partner)

    def up_copy(k):
        return remote(up_s, up_r.at[k - 1], 3, peer(k, 0))

    def cross_copy(k, j):
        slot = cross_r.at[k, j - 1]
        return remote(dual_s.at[years_dev], slot, 3 if k else 5, peer(hours - k, years - j))

    def above_copy(j):
        return remote(above_s, above_r.at[j - 1], 3, peer(0, j))

    net_copy = remote(net_s, net_r, 0, partner)
    inj_copy = remote(inj_s, inj_r, 1, partner)

    for j in range(1, years):
        for k in range(hours - 1, 0, -1):
            @pl.when(jnp.logical_and(me_h >= k, me_y >= j))
            def _(k=k, j=j):
                cross_copy(k, j).start()
    for k in range(hours - 1, 0, -1):
        @pl.when(me_h >= k)
        def _(k=k):
            dual_copy(k).start()

        @pl.when(jnp.logical_and(me_h >= k, me_l == 0))
        def _(k=k):
            mate_dual_copy(k).start()
    for j in range(1, years):
        @pl.when(me_y >= j)
        def _(j=j):
            cross_copy(0, j).start()

    for copy in loads[2:]:
        copy.wait()
    flow8[...] = jnp.zeros_like(flow8)
    for r in range(rows):
        flow8[r : r + 1, :] = flow_v[r]
    dual_half = flow8[...].astype(jnp.bfloat16)
    for first in range(0, node_tiles, 2 * THIN):
        def nodes_group(accs, first=first):
            group = range(first, min(first + 2 * THIN, node_tiles))
            jobs = [
                (n % 2, accs[n % 2][(n - first) // 2], dual_half[:, cols(k)], tile(n, k))
                for base in group[::2] for k in range(line_tiles) for n in (base, base + 1) if n in group
            ]
            multiply(jobs, False)
            for n in group:
                net_s[:, cols(n)] = pltpu.matmul_pop(accs[n % 2][(n - first) // 2])[:rows]

        scoped(padded, THIN, nodes_group)
    net_copy.start()

    @pl.when(me_y < years - 1)
    def _():
        pl.semaphore_wait(year_ready, years - 1 - me_y)

    for j in range(1, years):
        @pl.when(me_y + j < years)
        def _(j=j):
            cross_copy(0, years - j).start()

    @pl.when(me_l == 0)
    def _():
        node_copy.start()
    high_rows = lax.broadcasted_iota(jnp.int32, (hi_count, LANES), 0)
    lane_rows = lax.broadcasted_iota(jnp.int32, (LANES, LANES), 0)

    def encode(ref, first, count):
        for a in range(count):
            row = ref[a : a + 1, :]
            low = jnp.broadcast_to(row % LANES, (LANES, LANES))
            onehot[first + a] = jnp.where(low == lane_rows, 1.0, 0.0).astype(jnp.bfloat16)
            high = jnp.broadcast_to(row // LANES, (hi_count, LANES))
            highhot[first + a] = jnp.where(high == high_rows, 1.0, 0.0).astype(jnp.bfloat16)

    encode(snode_v, 0, store_rows)
    encode(gnode_v, store_rows, gen_rows)
    for r in range(rows):
        for j in range(hi_count):
            piece = slice(j * LANES, (j + 1) * LANES)
            demand_d[r, j : j + 1, :] = demand_v[r : r + 1, piece].astype(jnp.float32)
        for j in range(gen_rows):
            piece = slice(j * LANES, (j + 1) * LANES)
            avail_d[r, j : j + 1, :] = avail_v[r : r + 1, piece].astype(jnp.float32)

    diagonal = lax.broadcasted_iota(jnp.int32, (TILE, TILE), 0) == lax.broadcasted_iota(jnp.int32, (TILE, TILE), 1)
    identity = jnp.where(diagonal, 1.0, 0.0).astype(jnp.bfloat16)

    def turn(accs):
        work = [(k, n) for k in range(node_tiles) for n in range(line_tiles)]
        held = 2 * DEPTH
        for i in range(len(work) + held):
            if i >= held:
                k, n = work[i - held]
                turned = pltpu.matmul_pop(accs[i % 2][(i // 2) % DEPTH]).astype(ptdf_t.dtype)
                for c in range(2):
                    ptdf_t[k, n, c] = turned[:, c * LANES : (c + 1) * LANES]
            if i < len(work):
                k, n = work[i]
                pltpu.matmul_push_rhs(tile(k, n), (i // 2) % 2, i % 2, transpose=True)
                pltpu.matmul_acc_lhs(accs[i % 2][(i // 2) % DEPTH], identity, load_staged_rhs=(i // 2) % 2)

    scoped(TILE, DEPTH, turn)

    net_copy.wait_recv()
    prices = net_s[...] + net_r[...]

    def gather(r, node):
        price_row = prices[r : r + 1] + node_scale * balance_v[:, r : r + 1]
        high, low = node // LANES, node % LANES
        result = jnp.zeros(node.shape, jnp.float32)
        for j in range(hi_count):
            table = jnp.broadcast_to(price_row[:, j * LANES : (j + 1) * LANES], node.shape)
            picked = jnp.take_along_axis(table, low, axis=1, mode="promise_in_bounds")
            result = jnp.where(high == j, picked, result)
        return result

    for r in range(rows):
        for b in range(0, store_rows, 8):
            price_v[r, b : b + 8] = gather(r, snode_v[b : b + 8])

    @pl.when(me_l == 0)
    def _():
        mate_s[2 * rows] = power_v[...]
        for y in range(years_dev):
            own = None
            for h in reversed(range(hours_dev)):
                r = y * hours_dev + h
                diff = upper_v[r] - lower_v[r]
                own = diff if own is None else own + diff
                mate_s[r] = store_v[r] - TAU * (level_scale * own - price_v[r])
                mate_s[rows + r] = store_v[r]
        mate_copy.start()

    for r in range(rows):
        for b in range(0, gen_rows, 8):
            part = slice(b, b + 8)
            price = gather(r, gnode_v[part])
            new = gen_v[r, part] - TAU * (cost_v[part] + price)
            new = jnp.minimum(jnp.maximum(new, 0.0), cap_v[part] * avail_d[r, part])
            gen_w[r, part] = new
            gbar_v[r, part] = 2.0 * new - gen_v[r, part]

    def place(values, sign, first, count, start, target):
        pieces = []
        for r in range(rows):
            rest = sign * values[r]
            for _ in range(SPLITS):
                piece = rest.astype(jnp.bfloat16).astype(jnp.float32)
                rest = rest - piece
                pieces.append(piece)

        def spread(a):
            return jnp.concatenate([
                jnp.broadcast_to(piece[a : a + 1], (hi_count, LANES)).astype(jnp.bfloat16) * highhot[first + a]
                for piece in pieces
            ], axis=0)

        def pair(make, a):
            return jnp.concatenate([make(a), make(a + 1)], axis=1)

        jobs = []
        for t in range(count // 4):
            left = jnp.concatenate([pair(spread, 4 * t), pair(spread, 4 * t + 2)], axis=0)
            right = jnp.concatenate([wide(onehot, first + 4 * t, 2), wide(onehot, first + 4 * t + 2, 2)], axis=0)
            jobs.append((t % 2, left, right))
        height = rows * SPLITS * hi_count

        def finish(accs):
            multiply([(i, accs[i][0], left, right) for i, left, right in jobs], True)
            for i in range(2):
                both = pltpu.matmul_pop(accs[i][0])
                part = both[:height, :LANES] + both[height:, LANES:]
                target[...] = part + (start if i == 0 else target[...])

        scoped(2 * height, 1, finish)

    place(gbar_v, 1.0, store_rows, gen_rows, 0.0, placed_v)

    for r in range(rows):
        part = gbar_v[r, 0:8]
        for b in range(8, gen_rows, 8):
            part = part + gbar_v[r, b : b + 8]
        bal_s[r] = part

    def inject_part(r):
        total = None
        for p in range(SPLITS):
            base = (r * SPLITS + p) * hi_count
            piece = placed_v[base : base + hi_count]
            total = piece if total is None else total + piece
        return total

    @pl.when(me_l == 0)
    def _():
        for r in range(rows):
            inj_s[r] = inject_part(r)
        inj_copy.start()


    arrive(cross_r.at[0], recv_sem.at[5])
    hour_upper = total_v[...]
    for j in range(1, years):
        hour_upper = hour_upper + cross_r[0, j - 1].astype(jnp.float32)
    total_v[...] = hour_upper
    up_s[...] = hour_upper.astype(link)

    @pl.when(me_h < hours - 1)
    def _():
        pl.semaphore_wait(hour_ready, hours - 1 - me_h)
        for k in range(hours - 1, 0, -1):
            @pl.when(me_h + k < hours)
            def _(k=k):
                up_copy(k).start()

    for count in range(1, hours):
        @pl.when(me_h + count == hours - 1)
        def _(count=count):
            arrive(dual_r.at[pl.ds(0, count)], recv_sem.at[2])
    above = dual_r[0, years_dev].astype(jnp.float32)
    for k in range(2, hours):
        above = above + dual_r[k - 1, years_dev].astype(jnp.float32)
    above_s[...] = above.astype(link)
    for j in range(1, years):
        @pl.when(jnp.logical_and(me_h < hours - 1, me_y + j < years))
        def _(j=j):
            above_copy(j).start()
    for y in range(years_dev):
        beyond = dual_r[0, y].astype(jnp.float32)
        for k in range(2, hours):
            beyond = beyond + dual_r[k - 1, y].astype(jnp.float32)
        bar_total = None
        for h in reversed(range(hours_dev)):
            r = y * hours_dev + h
            beyond = beyond + (upper_v[r] - lower_v[r])
            suffix = level_scale * beyond
            power = power_v[...]
            new = store_v[r] - TAU * (suffix - price_v[r])
            new = jnp.minimum(jnp.maximum(new, -power), power)
            store_w[r] = new
            sbar = 2.0 * new - store_v[r]
            sbar_v[r] = sbar
            bar_total = sbar if bar_total is None else bar_total + sbar
        bar_s[y] = bar_total.astype(link)
    for k in range(hours - 1, 0, -1):
        @pl.when(jnp.logical_or(me_h + k == hours - 1, jnp.logical_and(me_h + k < hours, me_l == 1)))
        def _(k=k):
            bar_copy(k).start()
    for r in range(rows):
        part = bal_s[r]
        for b in range(0, store_rows, 8):
            part = part - sbar_v[r, b : b + 8]
        bal_s[r] = part
    bal_copy.start()
    total_v[...] = total_v[...] + above
    place(sbar_v, -1.0, 0, store_rows, placed_v[...], placed_v)

    @pl.when(me_l == 1)
    def _():
        for r in range(rows):
            inj_s[r] = inject_part(r)
        inj_copy.start()


    for c in range(line_local // LANES):
        limit1[:, c * LANES : (c + 1) * LANES] = limit_v[c : c + 1, :]
    inj8[...] = jnp.zeros_like(inj8)

    @pl.when(me_l == 1)
    def _():
        arrive(sent.at[pl.ds(0, (2 * rows + 2) * store_rows)], recv_sem.at[4])
        encode(mate_node, store_rows + gen_rows, store_rows)
        for count in range(1, hours):
            @pl.when(me_h + count == hours - 1)
            def _(count=count):
                arrive(mate_r.at[pl.ds(0, count)], recv_sem.at[6])
        power = mate_v[2 * rows]
        for y in range(years_dev):
            beyond = mate_r[0, y].astype(jnp.float32)
            for k in range(2, hours):
                beyond = beyond + mate_r[k - 1, y].astype(jnp.float32)
            bar_total = None
            for h in range(hours_dev):
                r = y * hours_dev + h
                new = mate_v[r] - TAU * level_scale * beyond
                new = jnp.minimum(jnp.maximum(new, -power), power)
                sbar = 2.0 * new - mate_v[rows + r]
                mate_bar[r] = sbar
                bar_total = sbar if bar_total is None else bar_total + sbar
            mate_sum[y] = bar_total.astype(link)
        for k in range(hours - 2, 0, -1):
            @pl.when(me_h + k < hours - 1)
            def _(k=k):
                mate_bar_copy(k).start()
        place(mate_bar, -1.0, store_rows + gen_rows, store_rows, placed_v[...], placed_v)

    inj_copy.wait_recv()
    for r in range(rows):
        inject = inject_part(r) + inj_r[r] - demand_d[r]
        for j in range(hi_count):
            inj8[r : r + 1, j * LANES : (j + 1) * LANES] = inject[j : j + 1]
    inject_half = inj8[...].astype(jnp.bfloat16)
    for first in range(0, line_tiles, THIN):
        def lines_group(accs, first=first):
            group = range(first, min(first + THIN, line_tiles))
            multiply([
                (k % 2, accs[k % 2][n - first], inject_half[:, cols(k)], wide(ptdf_t.at[k, n], 0, 2))
                for n in group for k in range(node_tiles)
            ], False)
            for i, n in enumerate(group):
                line8[:, cols(n)] = pltpu.matmul_pop(accs[0][i]) + pltpu.matmul_pop(accs[1][i])

        scoped(padded, THIN, lines_group)
    line_flows = line8[...]
    shifted = flow8[...] + SIGMA * line_flows
    limit = limit1[...]
    line_next = shifted - SIGMA * jnp.minimum(jnp.maximum(shifted * (1.0 / SIGMA), -limit), limit)
    for r in range(rows):
        flow_w[r] = line_next[r : r + 1]

    for y in range(years):
        for h in range(hours):
            late = h * (years_dev + 1) + (hours - 1 - h) * (years - 1 - y) + (y if h < hours - 1 else 0)
            if late:
                @pl.when(jnp.logical_and(me_h == h, me_y == y))
                def _(size=late * block_rows):
                    arrive(sent.at[pl.ds(0, size)], recv_sem.at[3])
    bal_copy.wait_recv()
    for r in range(rows):
        part = bal_s[r] + bal_r[r]
        for b in range(0, hi_count, 8):
            part = part - demand_d[r, b : b + 8]
        balance_o[:, r : r + 1] = balance_v[:, r : r + 1] + SIGMA * node_scale * jnp.sum(part, keepdims=True)

    upper_total = total_v[...]
    for k in range(1, hours):
        upper_total = upper_total + up_r[k - 1].astype(jnp.float32)
        for j in range(1, years):
            upper_total = upper_total + cross_r[k, j - 1].astype(jnp.float32)
    for j in range(1, years):
        upper_total = upper_total + above_r[j - 1].astype(jnp.float32)
    capacity_next = jnp.maximum(capacity_v[...] - TAU_CAP * (capex_v[...] - upper_total / hour_count), 0.0)
    capacity_w[...] = capacity_next
    capacity_bar = 2.0 * capacity_next - capacity_v[...]

    for y in range(years_dev):
        before = bar_r[0, y].astype(jnp.float32)
        for k in range(2, hours):
            before = before + bar_r[k - 1, y].astype(jnp.float32)
        for h in range(hours_dev):
            r = y * hours_dev + h
            before = before + sbar_v[r]
            level = level_scale * before
            upper_w[r] = jnp.maximum(upper_v[r] + SIGMA * (level - capacity_bar), 0.0)
            lower_w[r] = jnp.maximum(lower_v[r] - SIGMA * level, 0.0)

    for y in range(years):
        for h in range(hours):
            blocks = h * years_dev + h * y + (years - 1 - y if h < hours - 1 else 0)
            near = years_dev * (h + (1 if h < hours - 1 else 0))
            far = years_dev * (hours - 1 - h + max(hours - 2 - h, 0))
            extra = (2 * rows + 2) * store_rows

            @pl.when(jnp.logical_and(jnp.logical_and(me_h == h, me_y == y), me_l == 0))
            def _(size=base_rows + (blocks + near) * block_rows + extra):
                arrive(sent.at[pl.ds(0, size)], send_sem)

            @pl.when(jnp.logical_and(jnp.logical_and(me_h == h, me_y == y), me_l == 1))
            def _(size=base_rows + (blocks + far) * block_rows):
                arrive(sent.at[pl.ds(0, size)], send_sem)


def finish_kernel(count, *refs):
    sources, targets, sem = refs[:count], refs[count : 2 * count], refs[2 * count]
    copies = [pltpu.make_async_copy(s, t, sem) for s, t in zip(sources, targets)]
    for copy in copies:
        copy.start()
    for copy in copies:
        copy.wait()


def local(
    mesh,
    demand, avail, ptdf, line_limit, gen_cost, gen_cap, gen_node, store_node, store_power,
    capex, gen_state, store_state, level_upper, level_lower, flow_dual, balance_dual, capacity,
):
    years_dev, hours_dev, nodes = demand.shape
    rows = years_dev * hours_dev
    hours, years = lax.axis_size("hours"), lax.axis_size("years")
    hours_total = hours_dev * hours
    hour_count = years_dev * years * hours_total
    level_scale = 1.0 / math.sqrt(hours_total)
    node_scale = 1.0 / math.sqrt(nodes)
    sizes = (years_dev, hours_dev, hours, years, level_scale, node_scale, hour_count)

    def fold(x):
        return x.reshape(-1, LANES)

    def fold_rows(x):
        return x.reshape(rows, -1, LANES)

    args = (
        demand.reshape(rows, nodes), avail.reshape(rows, -1), ptdf, fold(line_limit), fold(gen_cost),
        fold(gen_cap), fold(gen_node), fold(store_node), fold(store_power), fold(capex),
        fold_rows(gen_state), fold_rows(store_state), fold_rows(level_upper), fold_rows(level_lower),
        flow_dual.reshape(rows, 1, -1), fold(capacity), balance_dual.reshape(1, rows),
    )
    f32 = jnp.float32
    gen_rows, store_rows = args[6].shape[0], args[7].shape[0]
    line_local, hi_count = ptdf.shape[0], nodes // LANES
    padded = max(16, -(-rows // 16) * 16)
    out_shapes = [
        (rows, gen_rows, LANES), (rows, store_rows, LANES), (store_rows, LANES),
        (rows, 1, line_local), (rows, store_rows, LANES), (rows, store_rows, LANES),
    ]
    any_spec = pl.BlockSpec(memory_space=pl.ANY)
    block, blocks = (store_rows, LANES), (years_dev + 1, store_rows, LANES)
    h1, y1 = max(hours - 1, 1), max(years - 1, 1)
    dma = pltpu.SemaphoreType.DMA
    block_rows = store_rows * jnp.dtype(LINK).itemsize // 4
    sent_rows = 2 * rows * hi_count + 8 * rows + (2 * rows + 2) * store_rows + 2 * hours * years_dev * block_rows + (hours - 1) * (years_dev + 1) * block_rows + (hours + 1) * years * block_rows
    scratch = [pltpu.VMEM(a.shape, a.dtype) for a in args]
    scratch[2] = pltpu.VMEM((hi_count, line_local, LANES), ptdf.dtype)
    scratch += [
        pltpu.VMEM((padded, line_local), f32), pltpu.VMEM((1, line_local), f32),
        pltpu.VMEM((rows, nodes), f32), pltpu.VMEM((rows, nodes), f32),
        pltpu.VMEM((rows, hi_count, LANES), f32), pltpu.VMEM((rows, hi_count, LANES), f32),
        pltpu.VMEM((padded, nodes), f32), pltpu.VMEM((padded, line_local), f32),
        pltpu.VMEM((rows, gen_rows, LANES), f32),
        pltpu.VMEM((rows, hi_count, LANES), f32),
        pltpu.VMEM(blocks, LINK), pltpu.VMEM((h1,) + blocks, LINK),
        pltpu.VMEM(block, f32), pltpu.VMEM((hours, y1) + block, LINK),
        pltpu.VMEM(block, LINK), pltpu.VMEM((y1,) + block, LINK),
        pltpu.VMEM(block, LINK), pltpu.VMEM((h1,) + block, LINK),
        pltpu.VMEM((years_dev,) + block, LINK), pltpu.VMEM((h1, years_dev) + block, LINK),
        pltpu.VMEM((rows, gen_rows, LANES), f32), pltpu.VMEM((rows, store_rows, LANES), f32),
        pltpu.VMEM((rows, store_rows, LANES), f32),
        pltpu.VMEM((gen_rows + 2 * store_rows, LANES, LANES), jnp.bfloat16),
        pltpu.VMEM((gen_rows + 2 * store_rows, hi_count, LANES), jnp.bfloat16),
        pltpu.VMEM((rows * SPLITS * hi_count, LANES), f32),
        pltpu.VMEM((sent_rows, LANES), f32),
        pltpu.VMEM((2 * rows + 1,) + block, f32), pltpu.VMEM((2 * rows + 1,) + block, f32),
        pltpu.VMEM(block, jnp.int32), pltpu.VMEM((rows,) + block, f32), pltpu.VMEM((years_dev,) + block, LINK),
        pltpu.VMEM((h1, years_dev) + block, LINK),
        pltpu.VMEM((rows, 8, LANES), f32), pltpu.VMEM((rows, 8, LANES), f32),
        pltpu.VMEM((nodes // TILE, line_local // TILE, 2, TILE, LANES), ptdf.dtype),
        dma((2,)), dma, dma((8,)), pltpu.SemaphoreType.REGULAR, pltpu.SemaphoreType.REGULAR,
    ]
    results = pl.pallas_call(
        functools.partial(step_kernel, sizes),
        out_shape=[pltpu.VMEM(s, f32) for s in out_shapes] + [pltpu.VMEM((1, rows), f32)],
        in_specs=[any_spec] * 17,
        out_specs=[pl.BlockSpec(memory_space=pltpu.VMEM)] * 7,
        scratch_shapes=scratch,
        compiler_params=pltpu.CompilerParams(
            collective_id=0, has_side_effects=True, vmem_limit_bytes=56 * 1024 * 1024
        ),
    )(*args)
    gen, store, cap, flow, upper, lower, balance = pl.pallas_call(
        functools.partial(finish_kernel, len(results)),
        out_shape=[jax.ShapeDtypeStruct(x.shape, f32) for x in results],
        in_specs=[pl.BlockSpec(memory_space=pltpu.VMEM)] * len(results),
        out_specs=[any_spec] * len(results),
        scratch_shapes=[dma],
    )(*[pltpu.with_memory_space_constraint(x, pltpu.VMEM) for x in results])
    return (
        gen.reshape(gen_state.shape), store.reshape(store_state.shape), cap.reshape(capacity.shape),
        balance.reshape(balance_dual.shape), flow.reshape(flow_dual.shape),
        upper.reshape(level_upper.shape), lower.reshape(level_lower.shape),
    )


def solution(mesh):
    row = P(("groups", "years"), "hours", "lines")
    line = P("lines")
    in_specs = (
        P(("groups", "years"), "hours", None), row, P("lines", None), line, line, line, line, line,
        line, line, row, row, row, row, row, P(("groups", "years"), "hours"), P(("groups", "lines")),
    )
    out_specs = (row, row, P(("groups", "lines")), P(("groups", "years"), "hours"), row, row, row)
    step = jax.shard_map(functools.partial(local, mesh), mesh=mesh, in_specs=in_specs, out_specs=out_specs, check_vma=False)

    def run(*args):
        with jax.sharding.use_abstract_mesh(mesh.abstract_mesh):
            return step(*args)

    return run
```

```python
import functools
import math

import jax
import jax.numpy as jnp
from jax import lax
from jax.experimental import pallas as pl
from jax.experimental.pallas import tpu as pltpu
from jax.sharding import PartitionSpec as P

TAU = 0.1
SIGMA = 0.5
TAU_CAP = 1.0
LANES = 128
SPLITS = 2
TILE = 256
THIN = 4
DEPTH = 1
LINK = jnp.bfloat16
MESH = pl.DeviceIdType.MESH


def step_kernel(
    sizes,
    demand_h, avail_h, ptdf_h, limit_h, cost_h, cap_h, gnode_h, snode_h, power_h,
    capex_h, gen_h, store_h, upper_h, lower_h, flow_h, capacity_h, balance_h,
    gen_w, store_w, capacity_w, flow_w, upper_w, lower_w, balance_o,
    demand_v, avail_v, ptdf_v, limit_v, cost_v, cap_v, gnode_v, snode_v, power_v,
    capex_v, gen_v, store_v, upper_v, lower_v, flow_v, capacity_v, balance_v,
    flow8, limit1, net_s, net_r, inj_s, inj_r, inj8, line8, avail_d, demand_d,
    dual_s, dual_r, total_v, cross_r, above_s, above_r, up_s, up_r, bar_s, bar_r,
    gbar_v, sbar_v, price_v, onehot, highhot, placed_v, sent,
    mate_s, mate_v, mate_node, mate_bar, mate_sum, mate_r, bal_s, bal_r, ptdf_t,
    in_sem, send_sem, recv_sem, year_ready, hour_ready,
):
    years_dev, hours_dev, hours, years, level_scale, node_scale, hour_count = sizes
    rows = years_dev * hours_dev
    me_h, me_y, me_l = lax.axis_index("hours"), lax.axis_index("years"), lax.axis_index("lines")
    hi_count, line_local = ptdf_v.shape[0], ptdf_v.shape[1]
    padded = flow8.shape[0]
    gen_rows, store_rows = gnode_v.shape[0], snode_v.shape[0]
    link = dual_s.dtype
    block_rows = store_rows * link.itemsize // 4
    base_rows = 2 * rows * hi_count + 8 * rows + (hours - 1 + years - 1) * block_rows

    order = (
        (upper_h, upper_v, 0), (lower_h, lower_v, 0), (flow_h, flow_v, 1),
    ) + tuple((ptdf_h.at[:, pl.ds(j * LANES, LANES)], ptdf_v.at[j], 1) for j in range(hi_count)) + (
        (snode_h, snode_v, 1), (gnode_h, gnode_v, 1), (store_h, store_v, 1), (power_h, power_v, 1),
        (gen_h, gen_v, 1), (cost_h, cost_v, 1), (cap_h, cap_v, 1), (avail_h, avail_v, 1),
        (demand_h, demand_v, 1), (limit_h, limit_v, 1), (capex_h, capex_v, 1), (capacity_h, capacity_v, 1),
        (balance_h, balance_v, 1),
    )
    loads = [pltpu.make_async_copy(s, d, in_sem.at[i]) for s, d, i in order]
    for copy in loads:
        copy.start()

    def wide(ref, first, count):
        return jnp.concatenate([ref[first + i] for i in range(count)], axis=1)

    def stage_first(rights, transpose):
        for unit in range(2):
            for i, right in enumerate(rights[unit][:2]):
                pltpu.matmul_push_rhs(right, i, unit, transpose=transpose)

    def multiply(jobs, transpose, staged=False):
        split = [[job for job in jobs if job[0] == unit] for unit in range(2)]
        if not staged:
            stage_first([[job[3] for job in part] for part in split], transpose)
        for i in range(max(len(part) for part in split)):
            for unit, part in enumerate(split):
                if i < len(part):
                    pltpu.matmul_acc_lhs(part[i][1], part[i][2], load_staged_rhs=i % 2)
                if i + 2 < len(part):
                    pltpu.matmul_push_rhs(part[i + 2][3], i % 2, unit, transpose=transpose)

    def tile(i, rows_from):
        rows_here = pl.ds(rows_from * TILE, TILE)
        return jnp.concatenate([ptdf_v[2 * i, rows_here], ptdf_v[2 * i + 1, rows_here]], axis=1)

    def scoped(height, count, body):
        specs = [pltpu.ACC(mxu_id=i)((height, TILE), jnp.float32) for i in range(2) for _ in range(count)]
        pl.run_scoped(lambda *accs: body((accs[:count], accs[count:])), *specs)

    def cols(i):
        return slice(i * TILE, (i + 1) * TILE)

    node_tiles, line_tiles = hi_count * LANES // TILE, line_local // TILE

    def peer(k, j):
        return {"hours": lax.rem(me_h + k, hours), "years": lax.rem(me_y + j, years)}

    partner = {"lines": 1 - me_l}
    barrier = pltpu.get_barrier_semaphore()

    def ready(device):
        pl.semaphore_signal(barrier, inc=1, device_id=device, device_id_type=MESH)

    dual_r[...] = jnp.zeros_like(dual_r)
    bar_r[...] = jnp.zeros_like(bar_r)
    up_r[...] = jnp.zeros_like(up_r)
    cross_r[...] = jnp.zeros_like(cross_r)
    mate_r[...] = jnp.zeros_like(mate_r)
    above_r[...] = jnp.zeros_like(above_r)
    ready(partner)
    for k in range(1, hours):
        @pl.when(me_h + k < hours)
        def _(k=k):
            ready(peer(k, 0))
        @pl.when(jnp.logical_and(me_h + k < hours, me_l == 1))
        def _(k=k):
            ready({**peer(k, 0), **partner})
    for j in range(1, years):
        @pl.when(me_y + j < years)
        def _(j=j):
            ready(peer(0, j))
            for k in range(1, hours):
                @pl.when(me_h + k < hours)
                def _(k=k):
                    ready(peer(k, j))

    pl.semaphore_wait(barrier, 1 + me_y + me_h * (2 + me_y - me_l))
    for j in range(1, years):
        @pl.when(me_y + j >= years)
        def _(j=j):
            pl.semaphore_signal(year_ready, inc=1, device_id=peer(0, j), device_id_type=MESH)
    for k in range(hours - 1, 0, -1):
        @pl.when(me_h >= k)
        def _(k=k):
            pl.semaphore_signal(hour_ready, inc=1, device_id=peer(hours - k, 0), device_id_type=MESH)

    loads[0].wait()
    loads[1].wait()
    local_upper = None
    for y in range(years_dev):
        total = None
        for h in range(hours_dev):
            r = y * hours_dev + h
            diff = upper_v[r] - lower_v[r]
            total = diff if total is None else total + diff
            local_upper = upper_v[r] if local_upper is None else local_upper + upper_v[r]
        dual_s[y] = total.astype(link)
    dual_s[years_dev] = local_upper.astype(link)
    total_v[...] = local_upper

    def remote(src, dst, sem, device):
        return pltpu.make_async_remote_copy(
            src_ref=src, dst_ref=dst, send_sem=send_sem, recv_sem=recv_sem.at[sem],
            device_id=device, device_id_type=MESH,
        )

    def arrive(ref, sem):
        pltpu.make_async_copy(ref, ref, sem).wait()

    def dual_copy(k):
        return remote(dual_s, dual_r.at[k - 1], 2, peer(hours - k, 0))

    def bar_copy(k):
        return remote(bar_s, bar_r.at[k - 1], 3, peer(k, 0))

    def mate_bar_copy(k):
        return remote(mate_sum, bar_r.at[k - 1], 3, {**peer(k, 0), **partner})

    def mate_dual_copy(k):
        return remote(dual_s.at[pl.ds(0, years_dev)], mate_r.at[k - 1], 6, {**peer(hours - k, 0), **partner})

    node_copy = remote(snode_v, mate_node, 4, partner)
    mate_copy = remote(mate_s, mate_v, 4, partner)
    bal_copy = remote(bal_s, bal_r, 7, partner)

    def up_copy(k):
        return remote(up_s, up_r.at[k - 1], 3, peer(k, 0))

    def cross_copy(k, j):
        slot = cross_r.at[k, j - 1]
        return remote(dual_s.at[years_dev], slot, 3 if k else 5, peer(hours - k, years - j))

    def above_copy(j):
        return remote(above_s, above_r.at[j - 1], 3, peer(0, j))

    net_copy = remote(net_s, net_r, 0, partner)
    inj_copy = remote(inj_s, inj_r, 1, partner)

    for j in range(1, years):
        for k in range(hours - 1, 0, -1):
            @pl.when(jnp.logical_and(me_h >= k, me_y >= j))
            def _(k=k, j=j):
                cross_copy(k, j).start()
    for k in range(hours - 1, 0, -1):
        @pl.when(jnp.logical_and(jnp.logical_and(me_h == k, me_l == 0), me_y > 0))
        def _(k=k):
            mate_dual_copy(k).start()

        @pl.when(me_h >= k)
        def _(k=k):
            dual_copy(k).start()

        @pl.when(jnp.logical_and(jnp.logical_and(me_h == k, me_l == 0), me_y == 0))
        def _(k=k):
            mate_dual_copy(k).start()

    for k in range(hours - 1, 0, -1):
        @pl.when(jnp.logical_and(me_h > k, me_l == 0))
        def _(k=k):
            mate_dual_copy(k).start()
    for j in range(1, years):
        @pl.when(me_y >= j)
        def _(j=j):
            cross_copy(0, j).start()

    for copy in loads[2:]:
        copy.wait()
    flow8[...] = jnp.zeros_like(flow8)
    for r in range(rows):
        flow8[r : r + 1, :] = flow_v[r]
    dual_half = flow8[...].astype(jnp.bfloat16)
    for first in range(0, node_tiles, 2 * THIN):
        def nodes_group(accs, first=first):
            group = range(first, min(first + 2 * THIN, node_tiles))
            jobs = [
                (n % 2, accs[n % 2][(n - first) // 2], dual_half[:, cols(k)], tile(n, k))
                for base in group[::2] for k in range(line_tiles) for n in (base, base + 1) if n in group
            ]
            multiply(jobs, False)
            for n in group:
                net_s[:, cols(n)] = pltpu.matmul_pop(accs[n % 2][(n - first) // 2])[:rows]

        scoped(padded, THIN, nodes_group)
    net_copy.start()

    @pl.when(me_y < years - 1)
    def _():
        pl.semaphore_wait(year_ready, years - 1 - me_y)

    for j in range(1, years):
        @pl.when(me_y + j < years)
        def _(j=j):
            cross_copy(0, years - j).start()

    @pl.when(me_l == 0)
    def _():
        node_copy.start()
    high_rows = lax.broadcasted_iota(jnp.int32, (hi_count, LANES), 0)
    lane_rows = lax.broadcasted_iota(jnp.int32, (LANES, LANES), 0)

    def encode(ref, first, count):
        for a in range(count):
            row = ref[a : a + 1, :]
            low = jnp.broadcast_to(row % LANES, (LANES, LANES))
            onehot[first + a] = jnp.where(low == lane_rows, 1.0, 0.0).astype(jnp.bfloat16)
            high = jnp.broadcast_to(row // LANES, (hi_count, LANES))
            highhot[first + a] = jnp.where(high == high_rows, 1.0, 0.0).astype(jnp.bfloat16)

    encode(snode_v, 0, store_rows)
    encode(gnode_v, store_rows, gen_rows)
    for r in range(rows):
        for j in range(hi_count):
            piece = slice(j * LANES, (j + 1) * LANES)
            demand_d[r, j : j + 1, :] = demand_v[r : r + 1, piece].astype(jnp.float32)
        for j in range(gen_rows):
            piece = slice(j * LANES, (j + 1) * LANES)
            avail_d[r, j : j + 1, :] = avail_v[r : r + 1, piece].astype(jnp.float32)

    diagonal = lax.broadcasted_iota(jnp.int32, (TILE, TILE), 0) == lax.broadcasted_iota(jnp.int32, (TILE, TILE), 1)

    def turn(accs):
        identity = jnp.where(diagonal, 1.0, 0.0).astype(jnp.bfloat16)
        work = [(k, n) for k in range(node_tiles) for n in range(line_tiles)]
        held = 2 * DEPTH
        for i in range(len(work) + held):
            if i >= held:
                k, n = work[i - held]
                turned = pltpu.matmul_pop(accs[i % 2][(i // 2) % DEPTH]).astype(ptdf_t.dtype)
                for c in range(2):
                    ptdf_t[k, n, c] = turned[:, c * LANES : (c + 1) * LANES]
            if i < len(work):
                k, n = work[i]
                pltpu.matmul_push_rhs(tile(k, n), (i // 2) % 2, i % 2, transpose=True)
                pltpu.matmul_acc_lhs(accs[i % 2][(i // 2) % DEPTH], identity, load_staged_rhs=(i // 2) % 2)

    @pl.when(me_l == 1)
    def _():
        scoped(TILE, DEPTH, turn)

    net_copy.wait_recv()
    prices = net_s[...] + net_r[...]

    def gather(r, node):
        price_row = prices[r : r + 1] + node_scale * balance_v[:, r : r + 1]
        high, low = node // LANES, node % LANES
        result = jnp.zeros(node.shape, jnp.float32)
        for j in range(hi_count):
            table = jnp.broadcast_to(price_row[:, j * LANES : (j + 1) * LANES], node.shape)
            picked = jnp.take_along_axis(table, low, axis=1, mode="promise_in_bounds")
            result = jnp.where(high == j, picked, result)
        return result

    for r in range(rows):
        for b in range(0, store_rows, 8):
            price_v[r, b : b + 8] = gather(r, snode_v[b : b + 8])

    @pl.when(me_l == 0)
    def _():
        mate_s[2 * rows] = power_v[...]
        for y in range(years_dev):
            own = None
            for h in reversed(range(hours_dev)):
                r = y * hours_dev + h
                diff = upper_v[r] - lower_v[r]
                own = diff if own is None else own + diff
                mate_s[r] = store_v[r] - TAU * (level_scale * own - price_v[r])
                mate_s[rows + r] = store_v[r]
        mate_copy.start()
        scoped(TILE, DEPTH, turn)

    for r in range(rows):
        for b in range(0, gen_rows, 8):
            part = slice(b, b + 8)
            price = gather(r, gnode_v[part])
            new = gen_v[r, part] - TAU * (cost_v[part] + price)
            new = jnp.minimum(jnp.maximum(new, 0.0), cap_v[part] * avail_d[r, part])
            gen_w[r, part] = new
            gbar_v[r, part] = 2.0 * new - gen_v[r, part]

    def place_tile(a):
        return jnp.concatenate([wide(onehot, a, 2), wide(onehot, a + 2, 2)], axis=0)

    def place(values, sign, first, count, start, target, staged=False):
        pieces = []
        for r in range(rows):
            rest = sign * values[r]
            for _ in range(SPLITS):
                piece = rest.astype(jnp.bfloat16).astype(jnp.float32)
                rest = rest - piece
                pieces.append(piece)

        def spread(a):
            return jnp.concatenate([
                jnp.broadcast_to(piece[a : a + 1], (hi_count, LANES)).astype(jnp.bfloat16) * highhot[first + a]
                for piece in pieces
            ], axis=0)

        def pair(make, a):
            return jnp.concatenate([make(a), make(a + 1)], axis=1)

        jobs = []
        for t in range(count // 4):
            left = jnp.concatenate([pair(spread, 4 * t), pair(spread, 4 * t + 2)], axis=0)
            jobs.append((t % 2, left, place_tile(first + 4 * t)))
        height = rows * SPLITS * hi_count

        def finish(accs):
            multiply([(i, accs[i][0], left, right) for i, left, right in jobs], True, staged)
            for i in range(2):
                both = pltpu.matmul_pop(accs[i][0])
                part = both[:height, :LANES] + both[height:, LANES:]
                target[...] = part + (start if i == 0 else target[...])

        scoped(2 * height, 1, finish)

    place(gbar_v, 1.0, store_rows, gen_rows, 0.0, placed_v)

    for r in range(rows):
        part = gbar_v[r, 0:8]
        for b in range(8, gen_rows, 8):
            part = part + gbar_v[r, b : b + 8]
        bal_s[r] = part

    def inject_part(r):
        total = None
        for p in range(SPLITS):
            base = (r * SPLITS + p) * hi_count
            piece = placed_v[base : base + hi_count]
            total = piece if total is None else total + piece
        return total

    @pl.when(me_l == 0)
    def _():
        for r in range(rows):
            inj_s[r] = inject_part(r)
        inj_copy.start()


    arrive(cross_r.at[0], recv_sem.at[5])
    hour_upper = total_v[...]
    for j in range(1, years):
        hour_upper = hour_upper + cross_r[0, j - 1].astype(jnp.float32)
    total_v[...] = hour_upper
    up_s[...] = hour_upper.astype(link)

    @pl.when(me_h < hours - 1)
    def _():
        pl.semaphore_wait(hour_ready, hours - 1 - me_h)
        for k in range(hours - 1, 0, -1):
            @pl.when(me_h + k < hours)
            def _(k=k):
                up_copy(k).start()

    store_tiles = range(store_rows // 4)
    stage_first([[place_tile(4 * t) for t in store_tiles if t % 2 == unit] for unit in range(2)], True)

    for count in range(1, hours):
        @pl.when(me_h + count == hours - 1)
        def _(count=count):
            arrive(dual_r.at[pl.ds(0, count)], recv_sem.at[2])
    above = dual_r[0, years_dev].astype(jnp.float32)
    for k in range(2, hours):
        above = above + dual_r[k - 1, years_dev].astype(jnp.float32)
    above_s[...] = above.astype(link)
    for j in range(1, years):
        @pl.when(jnp.logical_and(me_h < hours - 1, me_y + j < years))
        def _(j=j):
            above_copy(j).start()
    for y in range(years_dev):
        beyond = dual_r[0, y].astype(jnp.float32)
        for k in range(2, hours):
            beyond = beyond + dual_r[k - 1, y].astype(jnp.float32)
        bar_total = None
        for h in reversed(range(hours_dev)):
            r = y * hours_dev + h
            beyond = beyond + (upper_v[r] - lower_v[r])
            suffix = level_scale * beyond
            power = power_v[...]
            new = store_v[r] - TAU * (suffix - price_v[r])
            new = jnp.minimum(jnp.maximum(new, -power), power)
            store_w[r] = new
            sbar = 2.0 * new - store_v[r]
            sbar_v[r] = sbar
            bar_total = sbar if bar_total is None else bar_total + sbar
        bar_s[y] = bar_total.astype(link)
    for k in range(hours - 1, 0, -1):
        @pl.when(jnp.logical_and(me_h + k < hours, jnp.logical_or(me_h > 0, me_l == 1)))
        def _(k=k):
            bar_copy(k).start()
    for r in range(rows):
        part = bal_s[r]
        for b in range(0, store_rows, 8):
            part = part - sbar_v[r, b : b + 8]
        bal_s[r] = part
    bal_copy.start()
    total_v[...] = total_v[...] + above
    place(sbar_v, -1.0, 0, store_rows, placed_v[...], placed_v, True)

    @pl.when(me_l == 1)
    def _():
        for r in range(rows):
            inj_s[r] = inject_part(r)
        inj_copy.start()


    for c in range(line_local // LANES):
        limit1[:, c * LANES : (c + 1) * LANES] = limit_v[c : c + 1, :]
    inj8[...] = jnp.zeros_like(inj8)

    @pl.when(me_l == 1)
    def _():
        arrive(sent.at[pl.ds(0, (2 * rows + 2) * store_rows)], recv_sem.at[4])
        encode(mate_node, store_rows + gen_rows, store_rows)
        for count in range(1, hours):
            @pl.when(me_h + count == hours - 1)
            def _(count=count):
                arrive(mate_r.at[pl.ds(0, count)], recv_sem.at[6])
        power = mate_v[2 * rows]
        for y in range(years_dev):
            beyond = mate_r[0, y].astype(jnp.float32)
            for k in range(2, hours):
                beyond = beyond + mate_r[k - 1, y].astype(jnp.float32)
            bar_total = None
            for h in range(hours_dev):
                r = y * hours_dev + h
                new = mate_v[r] - TAU * level_scale * beyond
                new = jnp.minimum(jnp.maximum(new, -power), power)
                sbar = 2.0 * new - mate_v[rows + r]
                mate_bar[r] = sbar
                bar_total = sbar if bar_total is None else bar_total + sbar
            mate_sum[y] = bar_total.astype(link)
        for k in range(hours - 1, 0, -1):
            @pl.when(me_h == 0)
            def _(k=k):
                mate_bar_copy(k).start()
        place(mate_bar, -1.0, store_rows + gen_rows, store_rows, placed_v[...], placed_v)

    inj_copy.wait_recv()
    for r in range(rows):
        inject = inject_part(r) + inj_r[r] - demand_d[r]
        for j in range(hi_count):
            inj8[r : r + 1, j * LANES : (j + 1) * LANES] = inject[j : j + 1]
    inject_half = inj8[...].astype(jnp.bfloat16)
    for first in range(0, line_tiles, THIN):
        def lines_group(accs, first=first):
            group = range(first, min(first + THIN, line_tiles))
            multiply([
                (k % 2, accs[k % 2][n - first], inject_half[:, cols(k)], wide(ptdf_t.at[k, n], 0, 2))
                for n in group for k in range(node_tiles)
            ], False)
            for i, n in enumerate(group):
                line8[:, cols(n)] = pltpu.matmul_pop(accs[0][i]) + pltpu.matmul_pop(accs[1][i])

        scoped(padded, THIN, lines_group)
    line_flows = line8[...]
    shifted = flow8[...] + SIGMA * line_flows
    limit = limit1[...]
    line_next = shifted - SIGMA * jnp.minimum(jnp.maximum(shifted * (1.0 / SIGMA), -limit), limit)
    for r in range(rows):
        flow_w[r] = line_next[r : r + 1]

    for y in range(years):
        for h in range(hours):
            late = h * (years_dev + 1) + (hours - 1 - h) * (years - 1 - y) + (y if h < hours - 1 else 0)
            if late:
                @pl.when(jnp.logical_and(me_h == h, me_y == y))
                def _(size=late * block_rows):
                    arrive(sent.at[pl.ds(0, size)], recv_sem.at[3])
    bal_copy.wait_recv()
    for r in range(rows):
        part = bal_s[r] + bal_r[r]
        for b in range(0, hi_count, 8):
            part = part - demand_d[r, b : b + 8]
        balance_o[:, r : r + 1] = balance_v[:, r : r + 1] + SIGMA * node_scale * jnp.sum(part, keepdims=True)

    upper_total = total_v[...]
    for k in range(1, hours):
        upper_total = upper_total + up_r[k - 1].astype(jnp.float32)
        for j in range(1, years):
            upper_total = upper_total + cross_r[k, j - 1].astype(jnp.float32)
    for j in range(1, years):
        upper_total = upper_total + above_r[j - 1].astype(jnp.float32)
    capacity_next = jnp.maximum(capacity_v[...] - TAU_CAP * (capex_v[...] - upper_total / hour_count), 0.0)
    capacity_w[...] = capacity_next
    capacity_bar = 2.0 * capacity_next - capacity_v[...]

    for y in range(years_dev):
        before = bar_r[0, y].astype(jnp.float32)
        for k in range(2, hours):
            before = before + bar_r[k - 1, y].astype(jnp.float32)
        for h in range(hours_dev):
            r = y * hours_dev + h
            before = before + sbar_v[r]
            level = level_scale * before
            upper_w[r] = jnp.maximum(upper_v[r] + SIGMA * (level - capacity_bar), 0.0)
            lower_w[r] = jnp.maximum(lower_v[r] - SIGMA * level, 0.0)

    for y in range(years):
        for h in range(hours):
            blocks = h * years_dev + h * y + (years - 1 - y if h < hours - 1 else 0)
            near = years_dev * (h + (hours - 1 - h if h > 0 else 0))
            far = years_dev * (hours - 1 - h + (hours - 1 if h == 0 else 0))
            extra = (2 * rows + 2) * store_rows

            @pl.when(jnp.logical_and(jnp.logical_and(me_h == h, me_y == y), me_l == 0))
            def _(size=base_rows + (blocks + near) * block_rows + extra):
                arrive(sent.at[pl.ds(0, size)], send_sem)

            @pl.when(jnp.logical_and(jnp.logical_and(me_h == h, me_y == y), me_l == 1))
            def _(size=base_rows + (blocks + far) * block_rows):
                arrive(sent.at[pl.ds(0, size)], send_sem)


def finish_kernel(count, *refs):
    sources, targets, sem = refs[:count], refs[count : 2 * count], refs[2 * count]
    copies = [pltpu.make_async_copy(s, t, sem) for s, t in zip(sources, targets)]
    for copy in copies:
        copy.start()
    for copy in copies:
        copy.wait()


def local(
    mesh,
    demand, avail, ptdf, line_limit, gen_cost, gen_cap, gen_node, store_node, store_power,
    capex, gen_state, store_state, level_upper, level_lower, flow_dual, balance_dual, capacity,
):
    years_dev, hours_dev, nodes = demand.shape
    rows = years_dev * hours_dev
    hours, years = lax.axis_size("hours"), lax.axis_size("years")
    hours_total = hours_dev * hours
    hour_count = years_dev * years * hours_total
    level_scale = 1.0 / math.sqrt(hours_total)
    node_scale = 1.0 / math.sqrt(nodes)
    sizes = (years_dev, hours_dev, hours, years, level_scale, node_scale, hour_count)

    def fold(x):
        return x.reshape(-1, LANES)

    def fold_rows(x):
        return x.reshape(rows, -1, LANES)

    args = (
        demand.reshape(rows, nodes), avail.reshape(rows, -1), ptdf, fold(line_limit), fold(gen_cost),
        fold(gen_cap), fold(gen_node), fold(store_node), fold(store_power), fold(capex),
        fold_rows(gen_state), fold_rows(store_state), fold_rows(level_upper), fold_rows(level_lower),
        flow_dual.reshape(rows, 1, -1), fold(capacity), balance_dual.reshape(1, rows),
    )
    f32 = jnp.float32
    gen_rows, store_rows = args[6].shape[0], args[7].shape[0]
    line_local, hi_count = ptdf.shape[0], nodes // LANES
    padded = max(16, -(-rows // 16) * 16)
    out_shapes = [
        (rows, gen_rows, LANES), (rows, store_rows, LANES), (store_rows, LANES),
        (rows, 1, line_local), (rows, store_rows, LANES), (rows, store_rows, LANES),
    ]
    any_spec = pl.BlockSpec(memory_space=pl.ANY)
    block, blocks = (store_rows, LANES), (years_dev + 1, store_rows, LANES)
    h1, y1 = max(hours - 1, 1), max(years - 1, 1)
    dma = pltpu.SemaphoreType.DMA
    block_rows = store_rows * jnp.dtype(LINK).itemsize // 4
    sent_rows = 2 * rows * hi_count + 8 * rows + (2 * rows + 2) * store_rows + 2 * hours * years_dev * block_rows + (hours - 1) * (years_dev + 1) * block_rows + (hours + 1) * years * block_rows
    scratch = [pltpu.VMEM(a.shape, a.dtype) for a in args]
    scratch[2] = pltpu.VMEM((hi_count, line_local, LANES), ptdf.dtype)
    scratch += [
        pltpu.VMEM((padded, line_local), f32), pltpu.VMEM((1, line_local), f32),
        pltpu.VMEM((rows, nodes), f32), pltpu.VMEM((rows, nodes), f32),
        pltpu.VMEM((rows, hi_count, LANES), f32), pltpu.VMEM((rows, hi_count, LANES), f32),
        pltpu.VMEM((padded, nodes), f32), pltpu.VMEM((padded, line_local), f32),
        pltpu.VMEM((rows, gen_rows, LANES), f32),
        pltpu.VMEM((rows, hi_count, LANES), f32),
        pltpu.VMEM(blocks, LINK), pltpu.VMEM((h1,) + blocks, LINK),
        pltpu.VMEM(block, f32), pltpu.VMEM((hours, y1) + block, LINK),
        pltpu.VMEM(block, LINK), pltpu.VMEM((y1,) + block, LINK),
        pltpu.VMEM(block, LINK), pltpu.VMEM((h1,) + block, LINK),
        pltpu.VMEM((years_dev,) + block, LINK), pltpu.VMEM((h1, years_dev) + block, LINK),
        pltpu.VMEM((rows, gen_rows, LANES), f32), pltpu.VMEM((rows, store_rows, LANES), f32),
        pltpu.VMEM((rows, store_rows, LANES), f32),
        pltpu.VMEM((gen_rows + 2 * store_rows, LANES, LANES), jnp.bfloat16),
        pltpu.VMEM((gen_rows + 2 * store_rows, hi_count, LANES), jnp.bfloat16),
        pltpu.VMEM((rows * SPLITS * hi_count, LANES), f32),
        pltpu.VMEM((sent_rows, LANES), f32),
        pltpu.VMEM((2 * rows + 1,) + block, f32), pltpu.VMEM((2 * rows + 1,) + block, f32),
        pltpu.VMEM(block, jnp.int32), pltpu.VMEM((rows,) + block, f32), pltpu.VMEM((years_dev,) + block, LINK),
        pltpu.VMEM((h1, years_dev) + block, LINK),
        pltpu.VMEM((rows, 8, LANES), f32), pltpu.VMEM((rows, 8, LANES), f32),
        pltpu.VMEM((nodes // TILE, line_local // TILE, 2, TILE, LANES), ptdf.dtype),
        dma((2,)), dma, dma((8,)), pltpu.SemaphoreType.REGULAR, pltpu.SemaphoreType.REGULAR,
    ]
    results = pl.pallas_call(
        functools.partial(step_kernel, sizes),
        out_shape=[pltpu.VMEM(s, f32) for s in out_shapes] + [pltpu.VMEM((1, rows), f32)],
        in_specs=[any_spec] * 17,
        out_specs=[pl.BlockSpec(memory_space=pltpu.VMEM)] * 7,
        scratch_shapes=scratch,
        compiler_params=pltpu.CompilerParams(
            collective_id=0, has_side_effects=True, vmem_limit_bytes=56 * 1024 * 1024
        ),
    )(*args)
    gen, store, cap, flow, upper, lower, balance = pl.pallas_call(
        functools.partial(finish_kernel, len(results)),
        out_shape=[jax.ShapeDtypeStruct(x.shape, f32) for x in results],
        in_specs=[pl.BlockSpec(memory_space=pltpu.VMEM)] * len(results),
        out_specs=[any_spec] * len(results),
        scratch_shapes=[dma],
    )(*[pltpu.with_memory_space_constraint(x, pltpu.VMEM) for x in results])
    return (
        gen.reshape(gen_state.shape), store.reshape(store_state.shape), cap.reshape(capacity.shape),
        balance.reshape(balance_dual.shape), flow.reshape(flow_dual.shape),
        upper.reshape(level_upper.shape), lower.reshape(level_lower.shape),
    )


def solution(mesh):
    row = P(("groups", "years"), "hours", "lines")
    line = P("lines")
    in_specs = (
        P(("groups", "years"), "hours", None), row, P("lines", None), line, line, line, line, line,
        line, line, row, row, row, row, row, P(("groups", "years"), "hours"), P(("groups", "lines")),
    )
    out_specs = (row, row, P(("groups", "lines")), P(("groups", "years"), "hours"), row, row, row)
    step = jax.shard_map(functools.partial(local, mesh), mesh=mesh, in_specs=in_specs, out_specs=out_specs, check_vma=False)

    def run(*args):
        with jax.sharding.use_abstract_mesh(mesh.abstract_mesh):
            return step(*args)

    return run
```

```python
import functools
import math

import jax
import jax.numpy as jnp
from jax import lax
from jax.experimental import pallas as pl
from jax.experimental.pallas import tpu as pltpu
from jax.sharding import PartitionSpec as P

TAU = 0.1
SIGMA = 0.5
TAU_CAP = 1.0
LANES = 128
SPLITS = 2
TILE = 256
THIN = 4
DEPTH = 1
LINK = jnp.bfloat16
MESH = pl.DeviceIdType.MESH


def step_kernel(
    sizes,
    demand_h, avail_h, ptdf_h, limit_h, cost_h, cap_h, gnode_h, snode_h, power_h,
    capex_h, gen_h, store_h, upper_h, lower_h, flow_h, capacity_h, balance_h,
    gen_w, store_w, capacity_w, flow_w, upper_w, lower_w, balance_o,
    demand_v, avail_v, ptdf_v, limit_v, cost_v, cap_v, gnode_v, snode_v, power_v,
    capex_v, gen_v, store_v, upper_v, lower_v, flow_v, capacity_v, balance_v,
    flow8, limit1, net_s, net_r, inj_s, inj_r, inj8, line8, avail_d, demand_d,
    dual_s, dual_r, total_v, cross_r, above_s, above_r, up_s, up_r, bar_s, bar_r,
    gbar_v, sbar_v, price_v, onehot, highhot, placed_v, sent,
    mate_s, mate_v, mate_node, mate_bar, mate_sum, mate_r, bal_s, bal_r, ptdf_t,
    in_sem, send_sem, recv_sem, year_ready, hour_ready,
):
    years_dev, hours_dev, hours, years, level_scale, node_scale, hour_count = sizes
    rows = years_dev * hours_dev
    me_h, me_y, me_l = lax.axis_index("hours"), lax.axis_index("years"), lax.axis_index("lines")
    hi_count, line_local = ptdf_v.shape[0], ptdf_v.shape[1]
    padded = flow8.shape[0]
    gen_rows, store_rows = gnode_v.shape[0], snode_v.shape[0]
    link = dual_s.dtype
    block_rows = store_rows * link.itemsize // 4
    base_rows = 2 * rows * hi_count + 8 * rows + (hours - 1 + years - 1) * block_rows

    order = (
        (upper_h, upper_v, 0), (lower_h, lower_v, 0), (flow_h, flow_v, 1),
    ) + tuple((ptdf_h.at[:, pl.ds(j * LANES, LANES)], ptdf_v.at[j], 1) for j in range(hi_count)) + (
        (snode_h, snode_v, 1), (gnode_h, gnode_v, 1), (store_h, store_v, 1), (power_h, power_v, 1),
        (gen_h, gen_v, 1), (cost_h, cost_v, 1), (cap_h, cap_v, 1), (avail_h, avail_v, 1),
        (demand_h, demand_v, 1), (limit_h, limit_v, 1), (capex_h, capex_v, 1), (capacity_h, capacity_v, 1),
        (balance_h, balance_v, 1),
    )
    loads = [pltpu.make_async_copy(s, d, in_sem.at[i]) for s, d, i in order]
    for copy in loads:
        copy.start()

    def wide(ref, first, count):
        return jnp.concatenate([ref[first + i] for i in range(count)], axis=1)

    def multiply(jobs, transpose):
        stage = [0, 0]
        for unit, acc, left, right in jobs:
            pltpu.matmul_push_rhs(right, stage[unit], unit, transpose=transpose)
            pltpu.matmul_acc_lhs(acc, left, load_staged_rhs=stage[unit])
            stage[unit] = 1 - stage[unit]

    def tile(i, rows_from):
        rows_here = pl.ds(rows_from * TILE, TILE)
        return jnp.concatenate([ptdf_v[2 * i, rows_here], ptdf_v[2 * i + 1, rows_here]], axis=1)

    def scoped(height, count, body):
        specs = [pltpu.ACC(mxu_id=i)((height, TILE), jnp.float32) for i in range(2) for _ in range(count)]
        pl.run_scoped(lambda *accs: body((accs[:count], accs[count:])), *specs)

    def cols(i):
        return slice(i * TILE, (i + 1) * TILE)

    node_tiles, line_tiles = hi_count * LANES // TILE, line_local // TILE

    def peer(k, j):
        return {"hours": lax.rem(me_h + k, hours), "years": lax.rem(me_y + j, years)}

    partner = {"lines": 1 - me_l}
    barrier = pltpu.get_barrier_semaphore()

    def ready(device):
        pl.semaphore_signal(barrier, inc=1, device_id=device, device_id_type=MESH)

    dual_r[...] = jnp.zeros_like(dual_r)
    bar_r[...] = jnp.zeros_like(bar_r)
    up_r[...] = jnp.zeros_like(up_r)
    cross_r[...] = jnp.zeros_like(cross_r)
    mate_r[...] = jnp.zeros_like(mate_r)
    above_r[...] = jnp.zeros_like(above_r)
    ready(partner)
    for k in range(1, hours):
        @pl.when(me_h + k < hours)
        def _(k=k):
            ready(peer(k, 0))
        @pl.when(jnp.logical_and(me_h + k < hours, me_l == 1))
        def _(k=k):
            ready({**peer(k, 0), **partner})
    for j in range(1, years):
        @pl.when(me_y + j < years)
        def _(j=j):
            ready(peer(0, j))
            for k in range(1, hours):
                @pl.when(me_h + k < hours)
                def _(k=k):
                    ready(peer(k, j))

    pl.semaphore_wait(barrier, 1 + me_y + me_h * (2 + me_y - me_l))
    for j in range(1, years):
        @pl.when(me_y + j >= years)
        def _(j=j):
            pl.semaphore_signal(year_ready, inc=1, device_id=peer(0, j), device_id_type=MESH)
    for k in range(hours - 1, 0, -1):
        @pl.when(me_h >= k)
        def _(k=k):
            pl.semaphore_signal(hour_ready, inc=1, device_id=peer(hours - k, 0), device_id_type=MESH)

    loads[0].wait()
    loads[1].wait()
    local_upper = None
    for y in range(years_dev):
        total = None
        for h in range(hours_dev):
            r = y * hours_dev + h
            diff = upper_v[r] - lower_v[r]
            total = diff if total is None else total + diff
            local_upper = upper_v[r] if local_upper is None else local_upper + upper_v[r]
        dual_s[y] = total.astype(link)
    dual_s[years_dev] = local_upper.astype(link)
    total_v[...] = local_upper

    def remote(src, dst, sem, device):
        return pltpu.make_async_remote_copy(
            src_ref=src, dst_ref=dst, send_sem=send_sem, recv_sem=recv_sem.at[sem],
            device_id=device, device_id_type=MESH,
        )

    def arrive(ref, sem):
        pltpu.make_async_copy(ref, ref, sem).wait()

    def dual_copy(k):
        return remote(dual_s, dual_r.at[k - 1], 2, peer(hours - k, 0))

    def bar_copy(k):
        return remote(bar_s, bar_r.at[k - 1], 3, peer(k, 0))

    def mate_bar_copy(k):
        return remote(mate_sum, bar_r.at[k - 1], 3, {**peer(k, 0), **partner})

    def mate_dual_copy(k):
        return remote(dual_s.at[pl.ds(0, years_dev)], mate_r.at[k - 1], 6, {**peer(hours - k, 0), **partner})

    node_copy = remote(snode_v, mate_node, 4, partner)
    mate_copy = remote(mate_s, mate_v, 4, partner)
    bal_copy = remote(bal_s, bal_r, 7, partner)

    def up_copy(k):
        return remote(up_s, up_r.at[k - 1], 3, peer(k, 0))

    def cross_copy(k, j):
        slot = cross_r.at[k, j - 1]
        return remote(dual_s.at[years_dev], slot, 3 if k else 5, peer(hours - k, years - j))

    def above_copy(j):
        return remote(above_s, above_r.at[j - 1], 3, peer(0, j))

    net_copy = remote(net_s, net_r, 0, partner)
    inj_copy = remote(inj_s, inj_r, 1, partner)

    for j in range(1, years):
        for k in range(hours - 1, 0, -1):
            @pl.when(jnp.logical_and(me_h >= k, me_y >= j))
            def _(k=k, j=j):
                cross_copy(k, j).start()
    for k in range(hours - 1, 0, -1):
        @pl.when(jnp.logical_and(jnp.logical_and(me_h == k, me_l == 0), me_y > 0))
        def _(k=k):
            mate_dual_copy(k).start()

        @pl.when(me_h >= k)
        def _(k=k):
            dual_copy(k).start()

        @pl.when(jnp.logical_and(jnp.logical_and(me_h == k, me_l == 0), me_y == 0))
        def _(k=k):
            mate_dual_copy(k).start()

    for k in range(hours - 1, 0, -1):
        @pl.when(jnp.logical_and(me_h > k, me_l == 0))
        def _(k=k):
            mate_dual_copy(k).start()
    for j in range(1, years):
        @pl.when(me_y >= j)
        def _(j=j):
            cross_copy(0, j).start()

    for copy in loads[2:]:
        copy.wait()
    flow8[...] = jnp.zeros_like(flow8)
    for r in range(rows):
        flow8[r : r + 1, :] = flow_v[r]
    dual_half = flow8[...].astype(jnp.bfloat16)
    for first in range(0, node_tiles, 2 * THIN):
        def nodes_group(accs, first=first):
            group = range(first, min(first + 2 * THIN, node_tiles))
            jobs = [
                (n % 2, accs[n % 2][(n - first) // 2], dual_half[:, cols(k)], tile(n, k))
                for base in group[::2] for k in range(line_tiles) for n in (base, base + 1) if n in group
            ]
            multiply(jobs, False)
            for n in group:
                net_s[:, cols(n)] = pltpu.matmul_pop(accs[n % 2][(n - first) // 2])[:rows]

        scoped(padded, THIN, nodes_group)
    net_copy.start()

    @pl.when(me_y < years - 1)
    def _():
        pl.semaphore_wait(year_ready, years - 1 - me_y)

    for j in range(1, years):
        @pl.when(me_y + j < years)
        def _(j=j):
            cross_copy(0, years - j).start()

    @pl.when(me_l == 0)
    def _():
        node_copy.start()
    high_rows = lax.broadcasted_iota(jnp.int32, (hi_count, LANES), 0)
    lane_rows = lax.broadcasted_iota(jnp.int32, (LANES, LANES), 0)

    def encode(ref, first, count):
        for a in range(count):
            row = ref[a : a + 1, :]
            low = jnp.broadcast_to(row % LANES, (LANES, LANES))
            onehot[first + a] = jnp.where(low == lane_rows, 1.0, 0.0).astype(jnp.bfloat16)
            high = jnp.broadcast_to(row // LANES, (hi_count, LANES))
            highhot[first + a] = jnp.where(high == high_rows, 1.0, 0.0).astype(jnp.bfloat16)

    encode(snode_v, 0, store_rows)
    encode(gnode_v, store_rows, gen_rows)
    for r in range(rows):
        for j in range(hi_count):
            piece = slice(j * LANES, (j + 1) * LANES)
            demand_d[r, j : j + 1, :] = demand_v[r : r + 1, piece].astype(jnp.float32)
        for j in range(gen_rows):
            piece = slice(j * LANES, (j + 1) * LANES)
            avail_d[r, j : j + 1, :] = avail_v[r : r + 1, piece].astype(jnp.float32)

    diagonal = lax.broadcasted_iota(jnp.int32, (TILE, TILE), 0) == lax.broadcasted_iota(jnp.int32, (TILE, TILE), 1)

    def turn(accs):
        identity = jnp.where(diagonal, 1.0, 0.0).astype(jnp.bfloat16)
        work = [(k, n) for k in range(node_tiles) for n in range(line_tiles)]
        held = 2 * DEPTH
        for i in range(len(work) + held):
            if i >= held:
                k, n = work[i - held]
                turned = pltpu.matmul_pop(accs[i % 2][(i // 2) % DEPTH]).astype(ptdf_t.dtype)
                for c in range(2):
                    ptdf_t[k, n, c] = turned[:, c * LANES : (c + 1) * LANES]
            if i < len(work):
                k, n = work[i]
                pltpu.matmul_push_rhs(tile(k, n), (i // 2) % 2, i % 2, transpose=True)
                pltpu.matmul_acc_lhs(accs[i % 2][(i // 2) % DEPTH], identity, load_staged_rhs=(i // 2) % 2)

    @pl.when(me_l == 1)
    def _():
        scoped(TILE, DEPTH, turn)

    net_copy.wait_recv()
    prices = net_s[...] + net_r[...]

    def gather(r, node):
        price_row = prices[r : r + 1] + node_scale * balance_v[:, r : r + 1]
        high, low = node // LANES, node % LANES
        result = jnp.zeros(node.shape, jnp.float32)
        for j in range(hi_count):
            table = jnp.broadcast_to(price_row[:, j * LANES : (j + 1) * LANES], node.shape)
            picked = jnp.take_along_axis(table, low, axis=1, mode="promise_in_bounds")
            result = jnp.where(high == j, picked, result)
        return result

    for r in range(rows):
        for b in range(0, store_rows, 8):
            price_v[r, b : b + 8] = gather(r, snode_v[b : b + 8])

    @pl.when(me_l == 0)
    def _():
        mate_s[2 * rows] = power_v[...]
        for y in range(years_dev):
            own = None
            for h in reversed(range(hours_dev)):
                r = y * hours_dev + h
                diff = upper_v[r] - lower_v[r]
                own = diff if own is None else own + diff
                mate_s[r] = store_v[r] - TAU * (level_scale * own - price_v[r])
                mate_s[rows + r] = store_v[r]
        mate_copy.start()
        scoped(TILE, DEPTH, turn)

    for r in range(rows):
        for b in range(0, gen_rows, 8):
            part = slice(b, b + 8)
            price = gather(r, gnode_v[part])
            new = gen_v[r, part] - TAU * (cost_v[part] + price)
            new = jnp.minimum(jnp.maximum(new, 0.0), cap_v[part] * avail_d[r, part])
            gen_w[r, part] = new
            gbar_v[r, part] = 2.0 * new - gen_v[r, part]

    def place(values, sign, first, count, start, target):
        pieces = []
        for r in range(rows):
            rest = sign * values[r]
            for _ in range(SPLITS):
                piece = rest.astype(jnp.bfloat16).astype(jnp.float32)
                rest = rest - piece
                pieces.append(piece)

        def spread(a):
            return jnp.concatenate([
                jnp.broadcast_to(piece[a : a + 1], (hi_count, LANES)).astype(jnp.bfloat16) * highhot[first + a]
                for piece in pieces
            ], axis=0)

        def pair(make, a):
            return jnp.concatenate([make(a), make(a + 1)], axis=1)

        jobs = []
        for t in range(count // 4):
            left = jnp.concatenate([pair(spread, 4 * t), pair(spread, 4 * t + 2)], axis=0)
            right = jnp.concatenate([wide(onehot, first + 4 * t, 2), wide(onehot, first + 4 * t + 2, 2)], axis=0)
            jobs.append((t % 2, left, right))
        height = rows * SPLITS * hi_count

        def finish(accs):
            multiply([(i, accs[i][0], left, right) for i, left, right in jobs], True)
            for i in range(2):
                both = pltpu.matmul_pop(accs[i][0])
                part = both[:height, :LANES] + both[height:, LANES:]
                target[...] = part + (start if i == 0 else target[...])

        scoped(2 * height, 1, finish)

    place(gbar_v, 1.0, store_rows, gen_rows, 0.0, placed_v)

    for r in range(rows):
        part = gbar_v[r, 0:8]
        for b in range(8, gen_rows, 8):
            part = part + gbar_v[r, b : b + 8]
        bal_s[r] = part

    def inject_part(r):
        total = None
        for p in range(SPLITS):
            base = (r * SPLITS + p) * hi_count
            piece = placed_v[base : base + hi_count]
            total = piece if total is None else total + piece
        return total

    @pl.when(me_l == 0)
    def _():
        for r in range(rows):
            inj_s[r] = inject_part(r)
        inj_copy.start()


    arrive(cross_r.at[0], recv_sem.at[5])
    hour_upper = total_v[...]
    for j in range(1, years):
        hour_upper = hour_upper + cross_r[0, j - 1].astype(jnp.float32)
    total_v[...] = hour_upper
    up_s[...] = hour_upper.astype(link)

    @pl.when(me_h < hours - 1)
    def _():
        pl.semaphore_wait(hour_ready, hours - 1 - me_h)
        for k in range(hours - 1, 0, -1):
            @pl.when(me_h + k < hours)
            def _(k=k):
                up_copy(k).start()

    for count in range(1, hours):
        @pl.when(me_h + count == hours - 1)
        def _(count=count):
            arrive(dual_r.at[pl.ds(0, count)], recv_sem.at[2])
    above = dual_r[0, years_dev].astype(jnp.float32)
    for k in range(2, hours):
        above = above + dual_r[k - 1, years_dev].astype(jnp.float32)
    above_s[...] = above.astype(link)
    for j in range(1, years):
        @pl.when(jnp.logical_and(me_h < hours - 1, me_y + j < years))
        def _(j=j):
            above_copy(j).start()
    for y in range(years_dev):
        beyond = dual_r[0, y].astype(jnp.float32)
        for k in range(2, hours):
            beyond = beyond + dual_r[k - 1, y].astype(jnp.float32)
        bar_total = None
        for h in reversed(range(hours_dev)):
            r = y * hours_dev + h
            beyond = beyond + (upper_v[r] - lower_v[r])
            suffix = level_scale * beyond
            power = power_v[...]
            new = store_v[r] - TAU * (suffix - price_v[r])
            new = jnp.minimum(jnp.maximum(new, -power), power)
            store_w[r] = new
            sbar = 2.0 * new - store_v[r]
            sbar_v[r] = sbar
            bar_total = sbar if bar_total is None else bar_total + sbar
        bar_s[y] = bar_total.astype(link)
    for k in range(hours - 1, 0, -1):
        @pl.when(jnp.logical_and(me_h + k < hours, jnp.logical_or(me_h > 0, me_l == 1)))
        def _(k=k):
            bar_copy(k).start()
    for r in range(rows):
        part = bal_s[r]
        for b in range(0, store_rows, 8):
            part = part - sbar_v[r, b : b + 8]
        bal_s[r] = part
    bal_copy.start()
    total_v[...] = total_v[...] + above
    place(sbar_v, -1.0, 0, store_rows, placed_v[...], placed_v)

    @pl.when(me_l == 1)
    def _():
        for r in range(rows):
            inj_s[r] = inject_part(r)
        inj_copy.start()


    for c in range(line_local // LANES):
        limit1[:, c * LANES : (c + 1) * LANES] = limit_v[c : c + 1, :]
    inj8[...] = jnp.zeros_like(inj8)

    @pl.when(me_l == 1)
    def _():
        arrive(sent.at[pl.ds(0, (2 * rows + 2) * store_rows)], recv_sem.at[4])
        encode(mate_node, store_rows + gen_rows, store_rows)
        for count in range(1, hours):
            @pl.when(me_h + count == hours - 1)
            def _(count=count):
                arrive(mate_r.at[pl.ds(0, count)], recv_sem.at[6])
        power = mate_v[2 * rows]
        for y in range(years_dev):
            beyond = mate_r[0, y].astype(jnp.float32)
            for k in range(2, hours):
                beyond = beyond + mate_r[k - 1, y].astype(jnp.float32)
            bar_total = None
            for h in range(hours_dev):
                r = y * hours_dev + h
                new = mate_v[r] - TAU * level_scale * beyond
                new = jnp.minimum(jnp.maximum(new, -power), power)
                sbar = 2.0 * new - mate_v[rows + r]
                mate_bar[r] = sbar
                bar_total = sbar if bar_total is None else bar_total + sbar
            mate_sum[y] = bar_total.astype(link)
        for k in range(hours - 1, 0, -1):
            @pl.when(me_h == 0)
            def _(k=k):
                mate_bar_copy(k).start()
        place(mate_bar, -1.0, store_rows + gen_rows, store_rows, placed_v[...], placed_v)

    inj_copy.wait_recv()
    for r in range(rows):
        inject = inject_part(r) + inj_r[r] - demand_d[r]
        for j in range(hi_count):
            inj8[r : r + 1, j * LANES : (j + 1) * LANES] = inject[j : j + 1]
    inject_half = inj8[...].astype(jnp.bfloat16)
    for first in range(0, line_tiles, THIN):
        def lines_group(accs, first=first):
            group = range(first, min(first + THIN, line_tiles))
            multiply([
                (k % 2, accs[k % 2][n - first], inject_half[:, cols(k)], wide(ptdf_t.at[k, n], 0, 2))
                for n in group for k in range(node_tiles)
            ], False)
            for i, n in enumerate(group):
                line8[:, cols(n)] = pltpu.matmul_pop(accs[0][i]) + pltpu.matmul_pop(accs[1][i])

        scoped(padded, THIN, lines_group)
    line_flows = line8[...]
    shifted = flow8[...] + SIGMA * line_flows
    limit = limit1[...]
    line_next = shifted - SIGMA * jnp.minimum(jnp.maximum(shifted * (1.0 / SIGMA), -limit), limit)
    for r in range(rows):
        flow_w[r] = line_next[r : r + 1]

    for y in range(years):
        for h in range(hours):
            late = h * (years_dev + 1) + (hours - 1 - h) * (years - 1 - y) + (y if h < hours - 1 else 0)
            if late:
                @pl.when(jnp.logical_and(me_h == h, me_y == y))
                def _(size=late * block_rows):
                    arrive(sent.at[pl.ds(0, size)], recv_sem.at[3])
    bal_copy.wait_recv()
    for r in range(rows):
        part = bal_s[r] + bal_r[r]
        for b in range(0, hi_count, 8):
            part = part - demand_d[r, b : b + 8]
        balance_o[:, r : r + 1] = balance_v[:, r : r + 1] + SIGMA * node_scale * jnp.sum(part, keepdims=True)

    upper_total = total_v[...]
    for k in range(1, hours):
        upper_total = upper_total + up_r[k - 1].astype(jnp.float32)
        for j in range(1, years):
            upper_total = upper_total + cross_r[k, j - 1].astype(jnp.float32)
    for j in range(1, years):
        upper_total = upper_total + above_r[j - 1].astype(jnp.float32)
    capacity_next = jnp.maximum(capacity_v[...] - TAU_CAP * (capex_v[...] - upper_total / hour_count), 0.0)
    capacity_w[...] = capacity_next
    capacity_bar = 2.0 * capacity_next - capacity_v[...]

    for y in range(years_dev):
        before = bar_r[0, y].astype(jnp.float32)
        for k in range(2, hours):
            before = before + bar_r[k - 1, y].astype(jnp.float32)
        for h in range(hours_dev):
            r = y * hours_dev + h
            before = before + sbar_v[r]
            level = level_scale * before
            upper_w[r] = jnp.maximum(upper_v[r] + SIGMA * (level - capacity_bar), 0.0)
            lower_w[r] = jnp.maximum(lower_v[r] - SIGMA * level, 0.0)

    for y in range(years):
        for h in range(hours):
            blocks = h * years_dev + h * y + (years - 1 - y if h < hours - 1 else 0)
            near = years_dev * (h + (hours - 1 - h if h > 0 else 0))
            far = years_dev * (hours - 1 - h + (hours - 1 if h == 0 else 0))
            extra = (2 * rows + 2) * store_rows

            @pl.when(jnp.logical_and(jnp.logical_and(me_h == h, me_y == y), me_l == 0))
            def _(size=base_rows + (blocks + near) * block_rows + extra):
                arrive(sent.at[pl.ds(0, size)], send_sem)

            @pl.when(jnp.logical_and(jnp.logical_and(me_h == h, me_y == y), me_l == 1))
            def _(size=base_rows + (blocks + far) * block_rows):
                arrive(sent.at[pl.ds(0, size)], send_sem)


def finish_kernel(count, *refs):
    sources, targets, sem = refs[:count], refs[count : 2 * count], refs[2 * count]
    copies = [pltpu.make_async_copy(s, t, sem) for s, t in zip(sources, targets)]
    for copy in copies:
        copy.start()
    for copy in copies:
        copy.wait()


def local(
    mesh,
    demand, avail, ptdf, line_limit, gen_cost, gen_cap, gen_node, store_node, store_power,
    capex, gen_state, store_state, level_upper, level_lower, flow_dual, balance_dual, capacity,
):
    years_dev, hours_dev, nodes = demand.shape
    rows = years_dev * hours_dev
    hours, years = lax.axis_size("hours"), lax.axis_size("years")
    hours_total = hours_dev * hours
    hour_count = years_dev * years * hours_total
    level_scale = 1.0 / math.sqrt(hours_total)
    node_scale = 1.0 / math.sqrt(nodes)
    sizes = (years_dev, hours_dev, hours, years, level_scale, node_scale, hour_count)

    def fold(x):
        return x.reshape(-1, LANES)

    def fold_rows(x):
        return x.reshape(rows, -1, LANES)

    args = (
        demand.reshape(rows, nodes), avail.reshape(rows, -1), ptdf, fold(line_limit), fold(gen_cost),
        fold(gen_cap), fold(gen_node), fold(store_node), fold(store_power), fold(capex),
        fold_rows(gen_state), fold_rows(store_state), fold_rows(level_upper), fold_rows(level_lower),
        flow_dual.reshape(rows, 1, -1), fold(capacity), balance_dual.reshape(1, rows),
    )
    f32 = jnp.float32
    gen_rows, store_rows = args[6].shape[0], args[7].shape[0]
    line_local, hi_count = ptdf.shape[0], nodes // LANES
    padded = max(16, -(-rows // 16) * 16)
    out_shapes = [
        (rows, gen_rows, LANES), (rows, store_rows, LANES), (store_rows, LANES),
        (rows, 1, line_local), (rows, store_rows, LANES), (rows, store_rows, LANES),
    ]
    any_spec = pl.BlockSpec(memory_space=pl.ANY)
    block, blocks = (store_rows, LANES), (years_dev + 1, store_rows, LANES)
    h1, y1 = max(hours - 1, 1), max(years - 1, 1)
    dma = pltpu.SemaphoreType.DMA
    block_rows = store_rows * jnp.dtype(LINK).itemsize // 4
    sent_rows = 2 * rows * hi_count + 8 * rows + (2 * rows + 2) * store_rows + 2 * hours * years_dev * block_rows + (hours - 1) * (years_dev + 1) * block_rows + (hours + 1) * years * block_rows
    scratch = [pltpu.VMEM(a.shape, a.dtype) for a in args]
    scratch[2] = pltpu.VMEM((hi_count, line_local, LANES), ptdf.dtype)
    scratch += [
        pltpu.VMEM((padded, line_local), f32), pltpu.VMEM((1, line_local), f32),
        pltpu.VMEM((rows, nodes), f32), pltpu.VMEM((rows, nodes), f32),
        pltpu.VMEM((rows, hi_count, LANES), f32), pltpu.VMEM((rows, hi_count, LANES), f32),
        pltpu.VMEM((padded, nodes), f32), pltpu.VMEM((padded, line_local), f32),
        pltpu.VMEM((rows, gen_rows, LANES), f32),
        pltpu.VMEM((rows, hi_count, LANES), f32),
        pltpu.VMEM(blocks, LINK), pltpu.VMEM((h1,) + blocks, LINK),
        pltpu.VMEM(block, f32), pltpu.VMEM((hours, y1) + block, LINK),
        pltpu.VMEM(block, LINK), pltpu.VMEM((y1,) + block, LINK),
        pltpu.VMEM(block, LINK), pltpu.VMEM((h1,) + block, LINK),
        pltpu.VMEM((years_dev,) + block, LINK), pltpu.VMEM((h1, years_dev) + block, LINK),
        pltpu.VMEM((rows, gen_rows, LANES), f32), pltpu.VMEM((rows, store_rows, LANES), f32),
        pltpu.VMEM((rows, store_rows, LANES), f32),
        pltpu.VMEM((gen_rows + 2 * store_rows, LANES, LANES), jnp.bfloat16),
        pltpu.VMEM((gen_rows + 2 * store_rows, hi_count, LANES), jnp.bfloat16),
        pltpu.VMEM((rows * SPLITS * hi_count, LANES), f32),
        pltpu.VMEM((sent_rows, LANES), f32),
        pltpu.VMEM((2 * rows + 1,) + block, f32), pltpu.VMEM((2 * rows + 1,) + block, f32),
        pltpu.VMEM(block, jnp.int32), pltpu.VMEM((rows,) + block, f32), pltpu.VMEM((years_dev,) + block, LINK),
        pltpu.VMEM((h1, years_dev) + block, LINK),
        pltpu.VMEM((rows, 8, LANES), f32), pltpu.VMEM((rows, 8, LANES), f32),
        pltpu.VMEM((nodes // TILE, line_local // TILE, 2, TILE, LANES), ptdf.dtype),
        dma((2,)), dma, dma((8,)), pltpu.SemaphoreType.REGULAR, pltpu.SemaphoreType.REGULAR,
    ]
    results = pl.pallas_call(
        functools.partial(step_kernel, sizes),
        out_shape=[pltpu.VMEM(s, f32) for s in out_shapes] + [pltpu.VMEM((1, rows), f32)],
        in_specs=[any_spec] * 17,
        out_specs=[pl.BlockSpec(memory_space=pltpu.VMEM)] * 7,
        scratch_shapes=scratch,
        compiler_params=pltpu.CompilerParams(
            collective_id=0, has_side_effects=True, vmem_limit_bytes=56 * 1024 * 1024
        ),
    )(*args)
    gen, store, cap, flow, upper, lower, balance = pl.pallas_call(
        functools.partial(finish_kernel, len(results)),
        out_shape=[jax.ShapeDtypeStruct(x.shape, f32) for x in results],
        in_specs=[pl.BlockSpec(memory_space=pltpu.VMEM)] * len(results),
        out_specs=[any_spec] * len(results),
        scratch_shapes=[dma],
    )(*[pltpu.with_memory_space_constraint(x, pltpu.VMEM) for x in results])
    return (
        gen.reshape(gen_state.shape), store.reshape(store_state.shape), cap.reshape(capacity.shape),
        balance.reshape(balance_dual.shape), flow.reshape(flow_dual.shape),
        upper.reshape(level_upper.shape), lower.reshape(level_lower.shape),
    )


def solution(mesh):
    row = P(("groups", "years"), "hours", "lines")
    line = P("lines")
    in_specs = (
        P(("groups", "years"), "hours", None), row, P("lines", None), line, line, line, line, line,
        line, line, row, row, row, row, row, P(("groups", "years"), "hours"), P(("groups", "lines")),
    )
    out_specs = (row, row, P(("groups", "lines")), P(("groups", "years"), "hours"), row, row, row)
    step = jax.shard_map(functools.partial(local, mesh), mesh=mesh, in_specs=in_specs, out_specs=out_specs, check_vma=False)

    def run(*args):
        with jax.sharding.use_abstract_mesh(mesh.abstract_mesh):
            return step(*args)

    return run
```
